32 devices in a mesh: groups: 2 (over y), ctx: 4 (over z), head: 2 (over x), pair: 2 (over core).
Axes of the slice: x: 2, y: 2, z: 4, core: 2. Of those that a mesh axis runs over, the one named last changes fastest.
Arguments:
- q_raw: bfloat16 [4096, 2048], P(('groups', 'ctx', 'pair'), 'head'), parts along dimension 0, may hold values from -6 to 6
- k_raw: bfloat16 [4096, 2048], P(('groups', 'ctx', 'pair'), 'head'), parts along dimension 0, may hold values from -6 to 6
- v_raw: bfloat16 [4096, 4096], P(('groups', 'ctx', 'pair'), 'head'), parts along dimension 0, may hold values from -6 to 6
- beta_logit: bfloat16 [32, 4096], P('head', ('groups', 'ctx', 'pair')), parts along dimension 1, may hold values from -6 to 6
- gate_logit: bfloat16 [32, 4096], P('head', ('groups', 'ctx', 'pair')), parts along dimension 1, may hold values from -4 to 13
- out_grad: bfloat16 [4096, 4096], P(('groups', 'ctx', 'pair'), 'head'), parts along dimension 0, may hold values from -6 to 6
- conv_q: bfloat16 [4, 2048], P(None, 'head'), may hold values from -3 to 3
- conv_k: bfloat16 [4, 2048], P(None, 'head'), may hold values from -3 to 3
- conv_v: bfloat16 [4, 4096], P(None, 'head'), may hold values from -3 to 3
- a_log: float32 [32], P('head'), may hold values from 0 to 2.77
- dt_bias: float32 [32], P('head'), may hold values from -16 to -2.9
- doc_ids: int32 [4096], P(('groups', 'ctx', 'pair')), parts along dimension 0, may hold values from 0 to 7, never falling along the last dimension, each value on 1 to 512 neighbouring positions
- swap_blocks: int32 [8], P(('groups', 'ctx')), parts along dimension 0, may hold values from 0 to 1, as said below
Outputs:
- layer_out: bfloat16 [4096, 4096], P(('groups', 'ctx', 'pair'), 'head'), parts along dimension 0
- q_grad: bfloat16 [4096, 2048], P(('groups', 'ctx', 'pair'), 'head'), parts along dimension 0
- k_grad: bfloat16 [4096, 2048], P(('groups', 'ctx', 'pair'), 'head'), parts along dimension 0
- v_grad: bfloat16 [4096, 4096], P(('groups', 'ctx', 'pair'), 'head'), parts along dimension 0
- beta_grad: bfloat16 [32, 4096], P('head', ('groups', 'ctx', 'pair')), parts along dimension 1
- gate_grad: bfloat16 [32, 4096], P('head', ('groups', 'ctx', 'pair')), parts along dimension 1
The draws below stay inside these ranges and needn't reach their ends.
There are 2 independent parts, one for each index of `groups`. The reference program is written for one: setup_inputs(seed, part) draws one part's arguments, and reference() takes and returns one part's arrays. A program takes and returns all parts, laid end to end along the dimension named above; an argument that names none is the same for every part. Nothing has to cross between parts.
Inputs may be any that keep to these rules, and one draw needn't show every extreme that they name: `doc_ids`: document numbers start at 0 and never fall along the tokens; each document has 1 to 512 tokens, one exactly 512. `swap_blocks`: 1 occurs at some context index.
All inputs are finite; a program needn't handle non-finite values.
Results may differ from the reference program's by a relative error of at most 0.001.
Values may be sent and summed in bfloat16 or wider, within the bound.
A program may use at most 320 MiB of HBM per device.

```python
import math
import jax
import jax.numpy as jnp
import numpy as np
from jax import lax

HK = 16
OUTPUT_GROUPS = 32
DK = 128
DV = 128
TAPS = 4
CH = 128
SWAP = 128
DOCS = 8
SHARD_TOKENS = 256
MAXB = 1
CTXS = 4
SPAN_POSITIONS = 2048
DOCMAX = 512
N_CTX = 4
N_PAIR = 2


def draw_dt_bias(key, part):
    first_key = jax.random.fold_in(key, 0)
    result = jax.random.uniform(first_key, (OUTPUT_GROUPS,), jnp.float32, math.log(0.05 / SPAN_POSITIONS), math.log(0.05))
    return result.astype(jnp.float32)


def draw_gate_logit(key, part):
    first_key, next_address, third_key = jax.random.split(key, 3)
    initial_entries = 0.5 * jax.random.normal(first_key, (OUTPUT_GROUPS, SPAN_POSITIONS), jnp.float32)
    position_runs = jax.random.uniform(next_address, (OUTPUT_GROUPS, SPAN_POSITIONS), jnp.float32) < 4.0 / SPAN_POSITIONS
    tier_sizes = jax.random.uniform(third_key, (OUTPUT_GROUPS, SPAN_POSITIONS), jnp.float32, 10.0, 13.0)
    return jnp.where(position_runs, tier_sizes, jnp.clip(initial_entries, -3.9, 3.9)).astype(jnp.bfloat16)


def draw_swap_blocks(key, part):
    first_key, next_address = jax.random.split(key)
    counts = jax.random.randint(first_key, (CTXS,), 0, MAXB + 1)
    where_most = jax.random.randint(next_address, (), 0, CTXS)
    positions = jnp.arange(CTXS)
    return jnp.where(positions == where_most, MAXB, counts).astype(jnp.int32)


def level_of(own_key, dims, cuts, least, high):
    def one(dim, blocks):
        steps = jax.random.uniform(jax.random.fold_in(jax.random.fold_in(own_key, 6), dim), (blocks,), jnp.float32, least / len(cuts), high / len(cuts))
        return jnp.repeat(jnp.exp(steps), dims[dim] // blocks).reshape((-1,) + (1,) * (len(dims) - dim - 1))

    level = one(*cuts[0])
    for cut in cuts[1:]:
        level = level * one(*cut)
    return level


def profile(count, total, limit, lean):
    portions = [(1 << 20) // math.isqrt(rank ** lean) + 1 for rank in range(2, count + 1)]
    surplus, given = total - limit - (count - 1), [1] * (count - 1)
    while surplus > 0:
        movable = [i for i in range(count - 1) if given[i] < limit]
        whole, budget = sum([portions[i] for i in movable]), surplus
        for i in movable:
            more = min(limit - given[i], max(1, budget * portions[i] // whole), surplus)
            given[i] = given[i] + more
            surplus = surplus - more
    return np.array([limit] + given)


def ragged_sizes(rng, amount, total, bound, skew):
    if amount == 2:
        one = jax.random.randint(rng, (), max(1, total - bound), min(bound, total - 1) + 1)
        return jnp.stack([one, total - one])
    sizes = jnp.asarray(profile(amount, total, bound, skew), jnp.int32)
    twos = (amount - 1) // 2
    source_of, taker = sizes[1:1 + 2 * twos:2], sizes[2:2 + 2 * twos:2]
    slack = jnp.minimum(source_of - 1, bound - taker)
    shifted = jax.random.randint(jax.random.fold_in(rng, 1), (twos,), 0, 1 << 20) % (slack + 1)
    sizes = sizes.at[1:1 + 2 * twos:2].set(source_of - shifted).at[2:2 + 2 * twos:2].set(taker + shifted)
    return sizes[jax.random.permutation(jax.random.fold_in(rng, 2), amount)]


def scatter_about(stream_key, dims, deviation, limit, cuts=(), kind=jnp.bfloat16):
    values = deviation * jax.random.normal(stream_key, dims, jnp.float32)
    if cuts:
        values = values * level_of(stream_key, dims, cuts, -0.22, 0.18)
    return jnp.clip(values, -limit, limit).astype(kind)


def setup_inputs(seed: int = 0, part: int = 0) -> dict:
    streams_of = jax.random.split(jax.random.key(seed), 14)
    part_splits = jax.random.split(jax.random.fold_in(streams_of[13], part), 14)
    return {
        "q_raw": scatter_about(part_splits[0], (SPAN_POSITIONS, HK * DK), 1.0, 6.0, ((0, 8), (1, 2))),
        "k_raw": scatter_about(part_splits[1], (SPAN_POSITIONS, HK * DK), 1.0, 6.0, ((0, 8), (1, 2))),
        "v_raw": scatter_about(part_splits[2], (SPAN_POSITIONS, OUTPUT_GROUPS * DV), 1.0, 6.0, ((0, 8), (1, 2))),
        "beta_logit": scatter_about(part_splits[3], (OUTPUT_GROUPS, SPAN_POSITIONS), 1.5, 6.0, ((0, 2), (1, 8))),
        "gate_logit": draw_gate_logit(jax.random.fold_in(jax.random.fold_in(streams_of[13], part), 71), part),
        "out_grad": scatter_about(part_splits[5], (SPAN_POSITIONS, OUTPUT_GROUPS * DV), 1.0, 6.0, ((0, 8), (1, 2))),
        "conv_q": scatter_about(streams_of[6], (TAPS, HK * DK), TAPS ** -0.5, 3.0, ((1, 2),)),
        "conv_k": scatter_about(streams_of[7], (TAPS, HK * DK), TAPS ** -0.5, 3.0, ((1, 2),)),
        "conv_v": scatter_about(streams_of[8], (TAPS, OUTPUT_GROUPS * DV), TAPS ** -0.5, 3.0, ((1, 2),)),
        "a_log": jnp.clip(2.77 * jax.random.uniform(streams_of[9], (OUTPUT_GROUPS,), jnp.float32) ** level_of(streams_of[9], (OUTPUT_GROUPS,), ((0, 2),), -0.2, 0.2), 0.0, 2.77),
        "dt_bias": draw_dt_bias(jax.random.fold_in(streams_of[13], 71), part),
        "doc_ids": jnp.searchsorted(jnp.cumsum(ragged_sizes(part_splits[11], DOCS, SPAN_POSITIONS, DOCMAX, 0)), jnp.arange(SPAN_POSITIONS), side="right").astype(jnp.int32),
        "swap_blocks": draw_swap_blocks(jax.random.fold_in(jax.random.fold_in(streams_of[13], part), 71), part),
    }


highest = lax.Precision.HIGHEST
normalizer_guard = 1e-06

def product(left_matrix, right_matrix):
    return jnp.matmul(left_matrix, right_matrix, precision=highest)

def lower_solve(strict_lower, right_side):
    return jax.scipy.linalg.solve_triangular(strict_lower, right_side, lower=True, unit_diagonal=True)

def conv_silu(extended, weight, ext_ids):
    tap_count = weight.shape[0]
    out_rows = extended.shape[0] - tap_count + 1
    current = ext_ids[tap_count - 1:]
    summed = jnp.zeros((out_rows, extended.shape[1]), jnp.float32)
    for tap_index in range(tap_count):
        same_doc = (ext_ids[tap_index:tap_index + out_rows] == current).astype(jnp.float32)
        summed = summed + weight[tap_index].astype(jnp.float32) * extended[tap_index:tap_index + out_rows] * same_doc[:, None]
    return jax.nn.silu(summed)

def unit_rows(values, head_width):
    shaped = values.reshape(values.shape[0], -1, head_width)
    return shaped / jnp.sqrt(lax.optimization_barrier(jnp.sum(shaped * shaped, axis=-1, keepdims=True)) + normalizer_guard)

def span_pieces(queries, key_rows, values, beta_rate, decay_log, doc_index, before_doc):
    span_len = queries.shape[0]
    positions = jnp.arange(span_len)
    at_or_below = positions[:, None] >= positions[None, :]
    strictly_below = positions[:, None] > positions[None, :]
    cumulative = jnp.cumsum(decay_log)
    same_doc = (doc_index[:, None] == doc_index[None, :]) & at_or_below
    decay_table = jnp.where(same_doc, jnp.exp(jnp.where(same_doc, cumulative[:, None] - cumulative[None, :], 0.0)), 0.0)
    start_decay = jnp.where(doc_index == before_doc, jnp.exp(cumulative), 0.0)
    strict_part = jnp.where(strictly_below, beta_rate[:, None] * decay_table * product(key_rows, key_rows.T), 0.0)
    right_side = jnp.concatenate([beta_rate[:, None] * values, (beta_rate * start_decay)[:, None] * key_rows], axis=1)
    solved = lower_solve(strict_part, right_side)
    scores = decay_table * product(queries, key_rows.T)
    weighted = key_rows * decay_table[span_len - 1][:, None]
    value_width = values.shape[1]
    return (scores, solved[:, :value_width], solved[:, value_width:], start_decay, queries, weighted)

def span_step(carried, pieces):
    scores, base_update, correction, start_decay, queries, weighted = pieces
    updates = base_update - product(correction, carried)
    outputs = start_decay[:, None] * product(queries, carried) + product(scores, updates)
    new_state = start_decay[-1] * carried + product(weighted.T, updates)
    return (new_state, outputs)

def sequence_order(source, blocks, token_axis):
    moved_axis = jnp.moveaxis(source, token_axis, 0)
    shaped = moved_axis.reshape((N_CTX, N_PAIR, SHARD_TOKENS) + moved_axis.shape[1:])

    def fix_pair(couple_lines, block_count):
        first_shard = couple_lines[0]
        second_shard = couple_lines[1]
        moved_rows = (block_count * SWAP).astype(jnp.int32)
        positions = jnp.arange(SHARD_TOKENS, dtype=jnp.int32).reshape((SHARD_TOKENS,) + (1,) * (first_shard.ndim - 1))
        new_first = jnp.where(positions >= SHARD_TOKENS - moved_rows, jnp.roll(second_shard, SHARD_TOKENS - moved_rows, axis=0), first_shard)
        new_second = jnp.where(positions < moved_rows, jnp.roll(first_shard, moved_rows, axis=0), second_shard)
        return jnp.stack([new_first, new_second])
    repaired = jax.vmap(fix_pair)(shaped, blocks)
    return jnp.moveaxis(repaired.reshape(moved_axis.shape), 0, token_axis)

def reference(q_raw, k_raw, v_raw, beta_logit, gate_logit, out_grad, conv_q, conv_k, conv_v, a_log, dt_bias, doc_ids, swap_blocks):
    q_seq = sequence_order(q_raw, swap_blocks, 0)
    k_seq = sequence_order(k_raw, swap_blocks, 0)
    v_seq = sequence_order(v_raw, swap_blocks, 0)
    grad_seq = sequence_order(out_grad, swap_blocks, 0)
    beta_seq = sequence_order(beta_logit, swap_blocks, 1)
    gate_seq = sequence_order(gate_logit, swap_blocks, 1)
    ids_float = doc_ids.astype(jnp.float32)
    ext_ids = jnp.concatenate([jnp.full((TAPS - 1,), -1.0, jnp.float32), ids_float])
    length_all = ids_float.shape[0]
    spans = length_all // CH
    doc_now = ids_float.reshape(spans, CH)
    doc_before = ext_ids[TAPS - 2:TAPS - 2 + length_all:CH]

    def extend(rows_in):
        return jnp.concatenate([jnp.zeros((TAPS - 1, rows_in.shape[1]), jnp.float32), rows_in], axis=0)

    def forward(query_raw, key_raw, value_raw, beta_in, gate_in):
        queries = unit_rows(conv_silu(extend(query_raw), conv_q, ext_ids), DK) / math.sqrt(DK)
        key_rows = unit_rows(conv_silu(extend(key_raw), conv_k, ext_ids), DK)
        value_rows = conv_silu(extend(value_raw), conv_v, ext_ids).reshape(length_all, OUTPUT_GROUPS, DV)
        group_size = OUTPUT_GROUPS // HK
        queries = jnp.repeat(queries, group_size, axis=1).transpose(1, 0, 2)
        key_rows = jnp.repeat(key_rows, group_size, axis=1).transpose(1, 0, 2)
        value_rows = value_rows.transpose(1, 0, 2)
        beta_rate = jax.nn.sigmoid(beta_in)
        decay_log = -jnp.exp(a_log)[:, None] * jax.nn.softplus(gate_in + dt_bias[:, None])

        def one_head(head_inputs):
            head_query, head_key, head_value, head_beta, head_decay = head_inputs
            pieces = jax.vmap(span_pieces)(head_query.reshape(spans, CH, DK), head_key.reshape(spans, CH, DK), head_value.reshape(spans, CH, DV), head_beta.reshape(spans, CH), head_decay.reshape(spans, CH), doc_now, doc_before)
            final_state, outputs = lax.scan(span_step, jnp.zeros((DK, DV), jnp.float32), pieces)
            return outputs.reshape(length_all, DV)
        heads_out = lax.map(jax.checkpoint(one_head), (queries, key_rows, value_rows, beta_rate, decay_log))
        return heads_out.transpose(1, 0, 2).reshape(length_all, OUTPUT_GROUPS * DV)
    outputs, pullback = jax.vjp(forward, q_seq.astype(jnp.float32), k_seq.astype(jnp.float32), v_seq.astype(jnp.float32), beta_seq.astype(jnp.float32), gate_seq.astype(jnp.float32))
    grads = pullback(grad_seq.astype(jnp.float32))
    return (outputs.astype(jnp.bfloat16), grads[0].astype(jnp.bfloat16), grads[1].astype(jnp.bfloat16), grads[2].astype(jnp.bfloat16), grads[3].astype(jnp.bfloat16), grads[4].astype(jnp.bfloat16))
```

```python
import functools
import math

import jax
import jax.numpy as jnp
from jax import lax
from jax.experimental import pallas as pl
from jax.experimental.pallas import tpu as pltpu
from jax.sharding import PartitionSpec as P

DK = 128
TAPS = 4
CH = 128
SWAP = 128
HALO = 8
GUARD = 1e-06
SCALE = 1.0 / math.sqrt(DK)
DOC_PARTS = 4
GROUP = 2
BASE = 32

f32 = jnp.float32
bf16 = jnp.bfloat16
highest = lax.Precision.HIGHEST
SEQ = ("ctx", "pair")


def split(x):
    high = x.astype(bf16)
    return high, (x - high.astype(f32)).astype(bf16)


def mm(a, b):
    ah, al = split(a)
    bh, bl = split(b)
    lhs = jnp.concatenate([ah, al], axis=1)
    rhs = jnp.concatenate(
        [jnp.concatenate([bh, bl], axis=1), jnp.concatenate([bh, jnp.zeros_like(bh)], axis=1)], axis=0
    )
    r = lax.dot_general(lhs, rhs, (((1,), (0,)), ((), ())), preferred_element_type=f32)
    n = b.shape[1]
    return r[:, :n] + r[:, n:]


def mm_half(a, b):
    return lax.dot_general(
        jnp.concatenate(split(a), axis=1), jnp.concatenate([b, b], axis=0), (((1,), (0,)), ((), ())),
        preferred_element_type=f32,
    )


def odd_blocks(x, size):
    return jnp.concatenate([x[i : i + size] for i in range(size, CH, 2 * size)], axis=0)


def with_odd(even, odd, size):
    parts = []
    for i in range(0, CH // 2, size):
        parts.append(jnp.zeros((size, CH), odd.dtype) if even is None else even[2 * i : 2 * i + size])
        parts.append(odd[i : i + size])
    return jnp.concatenate(parts, axis=0)


def mm_nt(a, b):
    ah, al = split(a)
    bh, bl = split(b)
    lhs = jnp.concatenate([ah, al], axis=1)
    rhs = jnp.concatenate(
        [jnp.concatenate([bh, bh], axis=1), jnp.concatenate([bl, jnp.zeros_like(bl)], axis=1)], axis=0
    )
    r = lax.dot_general(lhs, rhs, (((1,), (1,)), ((), ())), preferred_element_type=f32)
    n = b.shape[0]
    return r[:, :n] + r[:, n:]


def iota(axis):
    return lax.broadcasted_iota(jnp.int32, (CH, CH), axis)


def rowsum(x):
    return jnp.sum(x, axis=1, keepdims=True)


def columns(rows):
    return jnp.concatenate([rows, jnp.zeros((CH - rows.shape[0], CH), f32)], axis=0).T


def sigmoid(a):
    return 1.0 / (1.0 + jnp.exp(-a))


def fetch(raw, recv, flags):
    first = raw[:SWAP, :]
    second = raw[SWAP:, :]
    got = recv[...]
    first = jnp.where(flags[0] > 0, got, first)
    second = jnp.where(flags[1] > 0, got, second)
    return jnp.concatenate([first, second], axis=0)


def conv(x, halo, taps, masks):
    ext = jnp.concatenate([halo, x], axis=0)
    width = x.shape[1] // CH
    total = taps[TAPS - 1 : TAPS, :] * x
    for d in range(1, TAPS):
        moved = pltpu.roll(ext, d, 0)[HALO:, :]
        mask = masks[d - 1]
        if width > 1:
            mask = jnp.concatenate([mask] * width, axis=1)
        total = total + taps[TAPS - 1 - d : TAPS - d, :] * (moved * mask)
    return total


def conv_back(da, taps, masks):
    width = da.shape[1] // CH
    zeros = jnp.zeros((HALO, da.shape[1]), f32)
    total = taps[TAPS - 1 : TAPS, :] * jnp.concatenate([da, zeros], axis=0)
    size = total.shape[0]
    for d in range(1, TAPS):
        mask = masks[d - 1]
        if width > 1:
            mask = jnp.concatenate([mask] * width, axis=1)
        ext = jnp.concatenate([da * mask, zeros], axis=0)
        total = total + taps[TAPS - 1 - d : TAPS - d, :] * pltpu.roll(ext, size - d, 0)
    return total


def local_maps(
    flags, q_raw, k_raw, v_raw, g_raw, q_got, k_got, v_got, g_got, q_halo, k_halo, v_halo,
    q_taps, k_taps, v_taps, masks, docs, rows,
    a_q, a_k, a_v, qn_out, kn_out, seq_grad, inv_out, kk_out, qk_out, pdo_out,
):
    blocks = q_raw.shape[0] // CH
    qa = conv(fetch(q_raw, q_got, flags).astype(f32), q_halo[...], q_taps, masks)
    ka = conv(fetch(k_raw, k_got, flags).astype(f32), k_halo[...], k_taps, masks)
    va = conv(fetch(v_raw, v_got, flags).astype(f32), v_halo[...], v_taps, masks)
    a_q[...] = qa
    a_k[...] = ka
    a_v[...] = va
    gs = fetch(g_raw, g_got, flags)
    seq_grad[...] = gs
    do_all = gs
    qu = qa * sigmoid(qa)
    ku = ka * sigmoid(ka)
    v_all = va * sigmoid(va)
    qn = qu * (SCALE / jnp.sqrt(rowsum(qu * qu) + GUARD))
    kn = ku * (1.0 / jnp.sqrt(rowsum(ku * ku) + GUARD))
    qn_out[...] = qn
    kn_out[...] = kn
    row, col = iota(0), iota(1)
    eye = (row == col).astype(f32)
    heads = v_raw.shape[1] // CH
    state = []
    for n in range(blocks):
        q = qn[n * CH : (n + 1) * CH]
        k = kn[n * CH : (n + 1) * CH]
        both = mm_nt(jnp.concatenate([k, q], axis=0), k)
        kk, qk = both[:CH], both[CH:]
        kk_out[0, n] = kk
        qk_out[0, n] = qk
        q_t, k_t = q.T, k.T
        flat = rows[0, n]
        cols = columns(flat)
        for e in range(heads):
            beta, c, s, w = [cols[:, 4 * e + i : 4 * e + i + 1] for i in range(4)]
            beta_r, c_r, s_r, w_r = [flat[4 * e + i : 4 * e + i + 1, :] for i in range(4)]
            s_last = s_r[:, CH - 1 :]
            decay = jnp.exp(jnp.minimum(c - c_r, 0.0)) * docs[n]
            low = jnp.where(row > col, beta * decay * kk, 0.0)
            do = do_all[n * CH : (n + 1) * CH, e * CH : (e + 1) * CH]
            v = v_all[n * CH : (n + 1) * CH, e * CH : (e + 1) * CH]
            state.append((n, e, low, decay * qk, do, v, k * w, (beta_r * s_r) * k_t, beta * s * k, s_r * q_t, beta * v, s_last))
    inv = []
    for item in state:
        inv.append(eye - jnp.where((row >> 1) == (col >> 1), item[2], 0.0))
    size = 1
    while (2 << size) <= CH:
        near = ((row >> (size + 1)) == (col >> (size + 1))) & ((row >> size) != (col >> size))
        width = 1 << size
        if width < 8:
            half = [mm(jnp.where(near, item[2], 0.0), t) for item, t in zip(state, inv)]
            inv = [t - mm(t, h) for t, h in zip(inv, half)]
        else:
            half = [mm(odd_blocks(jnp.where(near, item[2], 0.0), width), t) for item, t in zip(state, inv)]
            odds = [odd_blocks(t, width) for t in inv]
            odds = [t - mm(t, with_odd(None, h, width)) for t, h in zip(odds, half)]
            inv = [with_odd(t, o, width) for t, o in zip(inv, odds)]
        size += 1
    maps = {}
    for item, t in zip(state, inv):
        n, e, low, p, do, v, kw, bsk_t, bsk, sq_t, bv, s_last = item
        inv_out[0, e, n] = t
        pdo = mm_half(p.T, do)
        pdo_out[0, e, n] = pdo
        t_t = t.T
        b = mm(t_t, kw)
        cc = mm(t_t, pdo)
        b_t = b.T
        m = s_last * eye - mm(b_t, bsk)
        a = mm(b_t, bv)
        g = mm_half(sq_t, do) - mm(bsk_t, cc)
        maps[n, e] = (m, a, g)
    results = []
    for e in range(heads):
        m, a, g = maps[0, e]
        for n in range(1, blocks):
            m2, a2, g2 = maps[n, e]
            g = g + mm(m.T, g2)
            a = mm(m2, a) + a2
            m = mm(m2, m)
        results.append((m, a, g))
    return results


def prepare_kernel(*refs):
    m_out, a_out, g_out = refs[-3:]
    for e, (m, a, g) in enumerate(local_maps(*refs[:-3])):
        m_out[e] = m
        a_out[e] = a
        g_out[e] = g


def inverse_blocks(low, size):
    regs = size // 8
    lane = lax.broadcasted_iota(jnp.int32, (8, CH), 1)
    sub = lax.broadcasted_iota(jnp.int32, (8, CH), 0)
    base = lane - lax.rem(lane, size)
    packed, inv = [], []
    for r in range(regs):
        acc = low[8 * r : 8 * r + 8]
        for at in range(size, CH, size):
            acc = jnp.where(lane >= at, low[at + 8 * r : at + 8 * r + 8], acc)
        packed.append(acc)
        inv.append((lane - base == sub + 8 * r).astype(f32))
    for j in range(size - 1):
        here = j // 8
        line = jnp.broadcast_to(inv[here][j % 8 : j % 8 + 1], (8, CH))
        for r in range(here if j % 8 < 7 else here + 1, regs):
            factor = jnp.take_along_axis(packed[r], base + j, axis=1, mode="promise_in_bounds")
            inv[r] = inv[r] - factor * line
    parts = []
    for at in range(0, CH, size):
        parts += [jnp.where(base == at, t, 0.0) for t in inv]
    return jnp.concatenate(parts, axis=0)


def head_scalars(cols, flat, e):
    return (
        [cols[:, 4 * e + i : 4 * e + i + 1] for i in range(4)],
        [flat[4 * e + i : 4 * e + i + 1, :] for i in range(4)],
    )


def part(x, n, h):
    return x[n * CH : (n + 1) * CH, h * CH : (h + 1) * CH]


def forward_phase(
    j, first, flags, q_raw, k_raw, v_raw, g_raw, q_got, k_got, v_got, g_got, q_halo, k_halo, v_halo,
    q_taps, k_taps, v_taps, masks, docs, rows,
    a_q, a_k, a_v, qn_out, kn_out, grad_out, inv_out, decay_out, ub_out, ws_out, pdo_out, kk_out, qk_out,
    maps, affs, w_buf,
):
    keys = q_raw.shape[1] // CH
    heads = v_raw.shape[1] // CH
    rep = heads // keys
    blocks = q_raw.shape[0] // CH
    qa = conv(fetch(q_raw, q_got, flags).astype(f32), q_halo[...], q_taps, masks)
    ka = conv(fetch(k_raw, k_got, flags).astype(f32), k_halo[...], k_taps, masks)
    va = conv(fetch(v_raw, v_got, flags).astype(f32), v_halo[...], v_taps, masks)
    a_q[j] = qa
    a_k[j] = ka
    a_v[j] = va
    do_all = fetch(g_raw, g_got, flags)
    grad_out[j] = do_all
    qu = qa * sigmoid(qa)
    ku = ka * sigmoid(ka)
    v_all = va * sigmoid(va)
    qn, kn = [], []
    for h in range(keys):
        x = qu[:, h * CH : (h + 1) * CH]
        qn.append(x * (SCALE / jnp.sqrt(rowsum(x * x) + GUARD)))
        x = ku[:, h * CH : (h + 1) * CH]
        kn.append(x * (1.0 / jnp.sqrt(rowsum(x * x) + GUARD)))
    qn = jnp.concatenate(qn, axis=1)
    kn = jnp.concatenate(kn, axis=1)
    qn_out[j] = qn
    kn_out[j] = kn
    row, col = iota(0), iota(1)
    eye = (row == col).astype(f32)
    units = []
    for n in range(blocks):
        flat = rows[0, n]
        cols = columns(flat)
        for h in range(keys):
            q, k = part(qn, n, h), part(kn, n, h)
            both = mm_nt(jnp.concatenate([k, q], axis=0), k)
            kk, qk = both[:CH], both[CH:]
            kk_out[j, n * keys + h] = kk
            qk_out[j, n * keys + h] = qk
            q_t, k_t = q.T, k.T
            for e in range(h * rep, (h + 1) * rep):
                (beta, c, s, w), (beta_r, c_r, s_r, w_r) = head_scalars(cols, flat, e)
                decay = jnp.exp(jnp.minimum(c - c_r, 0.0)) * docs[n]
                decay_out[j, n * heads + e] = decay
                low = jnp.where(row > col, beta * decay * kk, 0.0)
                units.append((
                    n, e, low, decay * qk, part(do_all, n, e), beta * part(v_all, n, e), (beta * s) * k,
                    k_t * w_r, s_r * q_t, s_r[:, CH - 1 :],
                ))
    inv = [inverse_blocks(u[2], BASE) for u in units]
    size = BASE.bit_length() - 1
    while (1 << size) < CH:
        near = ((row >> (size + 1)) == (col >> (size + 1))) & ((row >> size) != (col >> size))
        width = 1 << size
        half = [mm(odd_blocks(jnp.where(near, u[2], 0.0), width), t) for u, t in zip(units, inv)]
        odds = [odd_blocks(t, width) for t in inv]
        odds = [t - mm(t, with_odd(None, h, width)) for t, h in zip(odds, half)]
        inv = [with_odd(t, o, width) for t, o in zip(inv, odds)]
        size += 1
    got = {}
    solved = []
    for (n, e, low, p, do, bv, bsk, kw_t, sq_t, s_last), t in zip(units, inv):
        inv_out[j, n * heads + e] = t
        ub = mm(t, bv)
        ws = mm(t, bsk)
        by_do = mm_half(jnp.concatenate([p.T, sq_t], axis=0), do)
        ub_out[j, n * heads + e] = ub
        ws_out[j, n * heads + e] = ws
        pdo_out[j, n * heads + e] = by_do[:CH]
        solved.append((ub, ws, by_do))
    for (n, e, low, p, do, bv, bsk, kw_t, sq_t, s_last), (ub, ws, by_do) in zip(units, solved):
        a = mm(kw_t, ub)
        m = s_last * eye - mm(kw_t, ws)
        g = by_do[CH:] - mm(ws.T, by_do[:CH])
        got[n, e] = (m, m.T, a, g)
    for e in range(heads):
        m0, m0_t, a0, g0 = got[0, e]
        m1, m1_t, a1, g1 = got[1, e]
        for i, x in enumerate((m0, m1, m1_t, m0_t)):
            maps[j, e, i] = x
        for i, x in enumerate((a0, a1, g1, g0)):
            affs[j, e, i] = x
        w_buf[j, e] = jnp.where(first, a1, g0) + mm(jnp.where(first, m1, m0_t), jnp.where(first, a0, g1))


def backward_phase(
    j, first, other, q_taps, k_taps, v_taps, masks, rows,
    a_q, a_k, a_v, qn, kn, seq_grad, inv, decays, ub_in, ws_in, pdo_in, kk_in, qk_in,
    maps, affs, y_buf, s_buf, z_got,
    out, q_grad, k_grad, v_grad, q_end, k_end, v_end, q_spill, k_spill, v_spill, row_grads,
):
    tokens = a_q.shape[1]
    blocks = tokens // CH
    keys = a_q.shape[2] // CH
    heads = a_v.shape[2] // CH
    rep = heads // keys
    row, col = iota(0), iota(1)
    va = a_v[j]
    v_sig = sigmoid(va)
    v_all = va * v_sig
    states, leaving = [], []
    for e in range(heads):
        y, s1, z = y_buf[j, e], s_buf[j, e], z_got[j, e]
        t1 = affs[j, e, other] + mm(maps[j, e, other], z)
        states.append((jnp.where(first, y, z), jnp.where(first, s1, t1)))
        leaving.append((jnp.where(first, t1, s1), jnp.where(first, z, y)))
    info = [(rows[0, n], columns(rows[0, n])) for n in range(blocks)]
    q_all, k_all, do_all = qn[j], kn[j], seq_grad[j]
    order = [(n, e) for n in range(blocks) for e in range(heads)]
    work = {}
    for n, e in order:
        flat, cols = info[n]
        (beta, c, s, w), rs = head_scalars(cols, flat, e)
        i = n * heads + e
        q, k = part(q_all, n, e // rep), part(k_all, n, e // rep)
        st, ds_out = states[e][n], leaving[e][n]
        by_st = mm(jnp.concatenate([ws_in[j, i], q], axis=0), st)
        u = ub_in[j, i] - by_st[:CH]
        du = pdo_in[j, i] + mm(k * w, ds_out)
        work[n, e] = (by_st[CH:], u, du)
    for n, e in order:
        flat, cols = info[n]
        (beta, c, s, w), rs = head_scalars(cols, flat, e)
        i = n * heads + e
        qs, u, du = work[n, e]
        p = decays[j, i] * qk_in[j, n * keys + e // rep]
        o = s * qs + mm(p, u)
        out[n * CH : (n + 1) * CH, e * CH : (e + 1) * CH] = o.astype(bf16)
        y = mm(inv[j, i].T, du)
        work[n, e] = (qs, u, y)
    dqs, dks, dvs = [], [], {}
    for n in range(blocks):
        flat, cols = info[n]
        packed = jnp.zeros((CH, CH), f32)
        minus = []
        dq_row, dk_row = [], []
        for h in range(keys):
            q, k = part(q_all, n, h), part(k_all, n, h)
            dqk_sum = dkk_sum = dq = dk = 0.0
            for e in range(h * rep, (h + 1) * rep):
                (beta, c, s, w), (beta_r, c_r, s_r, w_r) = head_scalars(cols, flat, e)
                s_last = s_r[:, CH - 1 :]
                i = n * heads + e
                qs, u, y = work[n, e]
                st, ds_out = states[e][n], leaving[e][n]
                do = part(do_all, n, e).astype(f32)
                decay = decays[j, i]
                p = decay * qk_in[j, n * keys + h]
                do_y = jnp.concatenate([do, y], axis=0)
                by_u = mm_nt(do_y, u)
                by_s = mm_nt(do_y, st)
                dp, dl = by_u[:CH], -by_u[CH:]
                dos, z = by_s[:CH], -by_s[CH:]
                dkw = mm_nt(u, ds_out)
                strict = jnp.where(row > col, decay, 0.0)
                dlb = dl * (strict * kk_in[j, n * keys + h])
                f = dp * p + beta * dlb
                zk = z * k
                wk = w * (dkw * k)
                bs = beta * s
                dbeta = rowsum(y * part(v_all, n, e) + s * zk + dlb)
                extra = jnp.sum(rowsum(wk + s_last * (ds_out * st)), axis=0, keepdims=True)
                dc = rowsum(f + s * (do * qs) + bs * zk - wk)
                dc = dc + jnp.where(row[:, :1] == CH - 1, extra, 0.0)
                packed = jnp.where(col == 2 * e, dbeta, packed)
                packed = jnp.where(col == 2 * e + 1, dc, packed)
                minus += [jnp.zeros((1, CH), f32), jnp.sum(f, axis=0, keepdims=True)]
                dqk_sum = dqk_sum + dp * decay
                dkk_sum = dkk_sum + dl * (beta * strict)
                dq = dq + s * dos
                dk = dk + w * dkw + bs * z
                dvs[n, e] = beta * y
            dq_row.append(dq + mm(dqk_sum, k))
            dk_row.append(dk + mm(dqk_sum.T, q) + mm(dkk_sum + dkk_sum.T, k))
        dqs.append(dq_row)
        dks.append(dk_row)
        row_grads[0, n] = packed.T[: row_grads.shape[2]] - jnp.concatenate(minus, axis=0)
    qa, ka = a_q[j], a_k[j]
    daq = jnp.concatenate(
        [norm_back(jnp.concatenate([d[h] for d in dqs], axis=0), qa[:, h * CH : (h + 1) * CH], SCALE) for h in range(keys)],
        axis=1,
    )
    dak = jnp.concatenate(
        [norm_back(jnp.concatenate([d[h] for d in dks], axis=0), ka[:, h * CH : (h + 1) * CH], 1.0) for h in range(keys)],
        axis=1,
    )
    dv = jnp.concatenate(
        [jnp.concatenate([dvs[n, e] for e in range(heads)], axis=1) for n in range(blocks)], axis=0
    )
    dav = dv * (v_sig + v_all * (1.0 - v_sig))
    for da, taps, grad, end, spill in (
        (daq, q_taps, q_grad, q_end, q_spill),
        (dak, k_taps, k_grad, k_end, k_spill),
        (dav, v_taps, v_grad, v_end, v_spill),
    ):
        full = conv_back(da, taps, masks)
        grad[...] = full[:tokens].astype(bf16)
        end[...] = full[tokens - HALO : tokens]
        spill[...] = full[tokens:]


def fused_kernel(ctxs, steps, *refs):
    ins, refs = refs[:18], refs[18:]
    outs, refs = refs[:11], refs[11:]
    saved, refs = refs[:13], refs[13:]
    maps, affs, w_buf, w_got, x_buf, y_buf, s_buf, z_buf, z_got = refs[:9]
    swap_s, swap_r, hop_s, hop_r, pair_s, pair_r = refs[9:]
    step = pl.program_id(0)
    heads = w_buf.shape[1]
    core = lax.axis_index("pair")
    ctx = lax.axis_index("ctx")
    first = core == 0
    mine, other = 2 * core, 2 - 2 * core
    partner = {"pair": 1 - core}
    peer_ctx = jnp.where(first, ctx - 1, ctx + 1)
    has_peer = (peer_ctx >= 0) & (peer_ctx < ctxs)
    peer = {"ctx": jnp.clip(peer_ctx, 0, ctxs - 1), "pair": 1 - core}
    mesh_id = pl.DeviceIdType.MESH

    def swap(j):
        return pltpu.make_async_remote_copy(
            w_buf.at[j], w_got.at[j], swap_s.at[j], swap_r.at[j], device_id=partner, device_id_type=mesh_id
        )

    def hop(j):
        return pltpu.make_async_remote_copy(
            x_buf.at[j], y_buf.at[j], hop_s.at[j], hop_r.at[j], device_id=peer, device_id_type=mesh_id
        )

    def pair(j):
        return pltpu.make_async_remote_copy(
            z_buf.at[j], z_got.at[j], pair_s.at[j], pair_r.at[j], device_id=partner, device_id_type=mesh_id
        )

    @pl.when(step == 0)
    def _():
        barrier = pltpu.get_barrier_semaphore()
        pl.semaphore_signal(barrier, inc=1, device_id=partner, device_id_type=mesh_id)

        @pl.when(has_peer)
        def _():
            pl.semaphore_signal(barrier, inc=1, device_id=peer, device_id_type=mesh_id)

        pl.semaphore_wait(barrier, jnp.where(has_peer, 2, 1))

    @pl.when((step >= 1) & (step < steps + 1))
    def _():
        j = step - 1
        swap(j).wait_recv()
        mid = [affs[j, e, other] + mm(maps[j, e, other], w_got[j, e]) for e in range(heads)]
        for e in range(heads):
            x_buf[j, e] = affs[j, e, other + 1] + mm(maps[j, e, other + 1], mid[e])

        @pl.when(has_peer)
        def _():
            hop(j).start()

    @pl.when((step >= 2) & (step < steps + 2))
    def _():
        j = step - 2

        @pl.when(has_peer)
        def _():
            hop(j).wait_recv()

        @pl.when(jnp.logical_not(has_peer))
        def _():
            y_buf[j] = jnp.zeros(y_buf.shape[1:], f32)

        mid = [affs[j, e, mine] + mm(maps[j, e, mine], y_buf[j, e]) for e in range(heads)]
        for e in range(heads):
            s_buf[j, e] = mid[e]
            z_buf[j, e] = affs[j, e, mine + 1] + mm(maps[j, e, mine + 1], mid[e])
        pair(j).start()

    @pl.when(step < steps)
    def _():
        forward_phase(step, first, *ins, *saved, maps, affs, w_buf)
        swap(step).start()

    @pl.when(step >= steps)
    def _():
        j = step - steps
        pair(j).wait_recv()
        backward_phase(j, first, other, *ins[12:16], ins[17], *saved, maps, affs, y_buf, s_buf, z_got, *outs)
        swap(j).wait_send()
        pair(j).wait_send()

        @pl.when(has_peer)
        def _():
            hop(j).wait_send()


def join_kernel(m, a, g, a_in, g_in, a_out, g_out):
    for e in range(m.shape[0]):
        here = m[e]
        a_out[e] = a[e] + mm(here, a_in[e])
        g_out[e] = g[e] + mm(here.T, g_in[e])


def norm_back(dy, a, scale):
    sig = sigmoid(a)
    u = a * sig
    inverse = 1.0 / jnp.sqrt(rowsum(u * u) + GUARD)
    y = u * inverse
    dy = dy * scale
    du = (dy - y * rowsum(y * dy)) * inverse
    return du * (sig + u * (1.0 - sig))


def main_kernel(
    a_q, a_k, a_v, qn, kn, seq_grad, inv, kk_in, qk_in, pdo_in, q_taps, k_taps, v_taps, masks, docs, rows,
    s_in, d_in, out, q_grad, k_grad, v_grad, q_end, k_end, v_end, q_spill, k_spill, v_spill, row_grads,
):
    tokens = a_q.shape[0]
    blocks = tokens // CH
    heads = a_v.shape[1] // CH
    row, col = iota(0), iota(1)
    va = a_v[...]
    v_sig = sigmoid(va)
    v_all = va * v_sig
    info = []
    for n in range(blocks):
        q = qn[n * CH : (n + 1) * CH, :]
        k = kn[n * CH : (n + 1) * CH, :]
        info.append((q, k, q.T, k.T, rows[0, n], columns(rows[0, n])))
    fwd = {}
    carried = [s_in[e] for e in range(heads)]
    for n in range(blocks):
        q, k, q_t, k_t, flat, cols = info[n]
        kq = jnp.concatenate([k, q], axis=0)
        for e in range(heads):
            beta, c, s, w = [cols[:, 4 * e + i : 4 * e + i + 1] for i in range(4)]
            beta_r, c_r, s_r, w_r = [flat[4 * e + i : 4 * e + i + 1, :] for i in range(4)]
            s_last = s_r[:, CH - 1 :]
            v = v_all[n * CH : (n + 1) * CH, e * CH : (e + 1) * CH]
            decay = jnp.exp(jnp.minimum(c - c_r, 0.0)) * docs[n]
            p = decay * qk_in[0, n]
            st = carried[e]
            kqs = mm(kq, st)
            ks, qs = kqs[:CH], kqs[CH:]
            t = inv[0, e, n]
            u = mm(t, beta * (v - s * ks))
            o = s * qs + mm(p, u)
            out[n * CH : (n + 1) * CH, e * CH : (e + 1) * CH] = o.astype(bf16)
            if n + 1 < blocks:
                carried[e] = s_last * st + mm(k_t * w_r, u)
            fwd[n, e] = (st, u, qs, decay, p, v)
    grads = [d_in[e] for e in range(heads)]
    dqs, dks, dvs = [None] * blocks, [None] * blocks, {}
    for n in reversed(range(blocks)):
        q, k, q_t, k_t, flat, cols = info[n]
        packed = jnp.zeros((CH, CH), f32)
        dqk_sum = dkk_sum = dq = dk = 0.0
        for e in range(heads):
            beta, c, s, w = [cols[:, 4 * e + i : 4 * e + i + 1] for i in range(4)]
            beta_r, c_r, s_r, w_r = [flat[4 * e + i : 4 * e + i + 1, :] for i in range(4)]
            s_last = s_r[:, CH - 1 :]
            st, u, qs, decay, p, v = fwd[n, e]
            ds_out = grads[e]
            do_half = seq_grad[n * CH : (n + 1) * CH, e * CH : (e + 1) * CH]
            do = do_half.astype(f32)
            du = pdo_in[0, e, n] + mm(k * w, ds_out)
            y = mm(inv[0, e, n].T, du)
            do_y = jnp.concatenate([do, y], axis=0)
            by_u = mm_nt(do_y, u)
            by_s = mm_nt(do_y, st)
            dp, dl = by_u[:CH], -by_u[CH:]
            dos, z = by_s[:CH], -by_s[CH:]
            dkw = mm_nt(u, ds_out)
            strict = jnp.where(row > col, decay, 0.0)
            bk = strict * kk_in[0, n]
            dlb = dl * bk
            f = dp * p + beta * dlb
            zk = z * k
            wk = w * (dkw * k)
            bs = beta * s
            dbeta = rowsum(y * v + s * zk + dlb)
            extra = jnp.sum(rowsum(wk + s_last * (ds_out * st)), axis=0, keepdims=True)
            dc = rowsum((f - f.T) + s * (do * qs) + bs * zk - wk)
            dc = dc + jnp.where(row[:, :1] == CH - 1, extra, 0.0)
            packed = jnp.where(col == 2 * e, dbeta, packed)
            packed = jnp.where(col == 2 * e + 1, dc, packed)
            dqk_sum = dqk_sum + dp * decay
            dkk_sum = dkk_sum + dl * (beta * strict)
            dq = dq + s * dos
            dk = dk + w * dkw + bs * z
            dvs[n, e] = beta * y
            if n > 0:
                grads[e] = mm_half(q_t * s_r, do_half) + s_last * ds_out - mm(k_t * (beta_r * s_r), y)
        dqs[n] = dq + mm(dqk_sum, k)
        dks[n] = dk + mm(dqk_sum.T, q) + mm(dkk_sum + dkk_sum.T, k)
        row_grads[0, n] = packed.T[: row_grads.shape[2]]
    dq = jnp.concatenate(dqs, axis=0)
    dk = jnp.concatenate(dks, axis=0)
    dv = jnp.concatenate(
        [jnp.concatenate([dvs[n, e] for e in range(heads)], axis=1) for n in range(blocks)], axis=0
    )
    daq = norm_back(dq, a_q[...], SCALE)
    dak = norm_back(dk, a_k[...], 1.0)
    dav = dv * (v_sig + v_all * (1.0 - v_sig))
    for da, taps, grad, end, spill in (
        (daq, q_taps, q_grad, q_end, q_spill),
        (dak, k_taps, k_grad, k_end, k_spill),
        (dav, v_taps, v_grad, v_end, v_spill),
    ):
        full = conv_back(da, taps, masks)
        grad[...] = full[:tokens].astype(bf16)
        end[...] = full[tokens - HALO : tokens]
        spill[...] = full[tokens:]


def shifted(array, by):
    peers = lax.axis_size(SEQ)
    return lax.ppermute(array, SEQ, [(i, i + by) for i in range(peers) if 0 <= i + by < peers])


def tri(upper):
    i = jnp.arange(CH)
    return ((i[:, None] <= i[None, :]) if upper else (i[:, None] >= i[None, :])).astype(f32)


def sds(shape, dtype=f32):
    return jax.ShapeDtypeStruct(shape, dtype)


def staged_call(inputs, hk, hv, tokens, hops):
    blocks = tokens // CH
    rep = hv // hk
    qw = hk * DK
    vw = rep * DK
    col = lambda rows_, width, off=0: pl.BlockSpec((rows_, width), lambda i, off=off, width=width: (0, off // width + i))
    fixed = lambda shape: pl.BlockSpec(shape, lambda i: (0,) * len(shape))
    per = lambda shape: pl.BlockSpec(shape, lambda i: (i,) + (0,) * (len(shape) - 1))
    taps_specs = [col(TAPS, DK), col(TAPS, DK), col(TAPS, vw)]
    common_specs = taps_specs + [
        fixed((TAPS - 1, tokens, CH)),
        fixed((blocks, CH, CH)),
        per((1, blocks, rep * 4, CH)),
    ]
    params = pltpu.CompilerParams(dimension_semantics=("arbitrary",), vmem_limit_bytes=48 * 2**20)
    saved_specs = [
        col(tokens, DK), col(tokens, DK), col(tokens, vw), col(tokens, DK), col(tokens, DK), col(tokens, vw),
        per((1, rep, blocks, CH, CH)), per((1, blocks, CH, CH)), per((1, blocks, CH, CH)),
        per((1, rep, blocks, CH, CH)),
    ]
    saved_shapes = [
        sds((tokens, qw)), sds((tokens, qw)), sds((tokens, hv * DK)), sds((tokens, qw)), sds((tokens, qw)),
        sds((tokens, hv * DK), bf16), sds((hk, rep, blocks, CH, CH)), sds((hk, blocks, CH, CH)),
        sds((hk, blocks, CH, CH)), sds((hk, rep, blocks, CH, CH)),
    ]
    state_spec = per((rep, DK, DK))
    state_shape = sds((hv, DK, DK))
    units = hv * blocks * 2 * 4 * CH**3
    *taps, masks, docs, rows = inputs[12:]
    in_specs = [
        pl.BlockSpec(memory_space=pltpu.SMEM),
        col(tokens, DK), col(tokens, DK), col(tokens, vw), col(tokens, vw),
        col(SWAP, DK), col(SWAP, DK, qw), col(SWAP, vw, 2 * qw), col(SWAP, vw, 2 * qw + hv * DK),
        col(HALO, DK), col(HALO, DK, qw), col(HALO, vw, 2 * qw),
    ] + common_specs
    prepare_cost = pl.CostEstimate(flops=22 * units, bytes_accessed=24 * 2**20, transcendentals=2**20)
    prepared = pl.pallas_call(
        prepare_kernel,
        grid=(hk,),
        in_specs=in_specs,
        out_specs=saved_specs + [state_spec] * 3,
        out_shape=saved_shapes + [state_shape] * 3,
        compiler_params=params,
        cost_estimate=prepare_cost,
        name="prepare",
    )(*inputs)
    saved, (m, a, g) = prepared[:10], prepared[10:]
    join = pl.pallas_call(
        join_kernel,
        grid=(hk,),
        in_specs=[state_spec] * 5,
        out_specs=[state_spec] * 2,
        out_shape=[state_shape] * 2,
        compiler_params=params,
        cost_estimate=pl.CostEstimate(flops=hv * 16 * CH**3, bytes_accessed=7 * 2**20, transcendentals=0),
        name="join",
    )
    s_in, d_in = a, g
    for step in range(hops):
        s_in, d_in = shifted(s_in, 1), shifted(d_in, -1)
        if step < hops - 1:
            s_in, d_in = join(m, a, g, s_in, d_in)

    ends = [col(HALO, DK), col(HALO, DK), col(HALO, vw)]
    end_shapes = [sds((HALO, qw)), sds((HALO, qw)), sds((HALO, hv * DK))]
    return pl.pallas_call(
        main_kernel,
        grid=(hk,),
        in_specs=saved_specs + common_specs + [state_spec] * 2,
        out_specs=[col(tokens, vw), col(tokens, DK), col(tokens, DK), col(tokens, vw)] + ends + ends + [per((1, blocks, 8, CH))],
        out_shape=[
            sds((tokens, hv * DK), bf16), sds((tokens, qw), bf16), sds((tokens, qw), bf16), sds((tokens, hv * DK), bf16)
        ] + end_shapes + end_shapes + [sds((hk, blocks, 8, CH))],
        compiler_params=params,
        cost_estimate=pl.CostEstimate(flops=17 * units, bytes_accessed=24 * 2**20, transcendentals=2**20),
        name="main",
    )(*saved, *taps, masks, docs, rows, s_in, d_in)


def fused_call(inputs, rows, hk, hv, tokens):
    blocks = tokens // CH
    rep = hv // hk
    qw = hk * DK
    steps = hk // GROUP
    heads = GROUP * rep
    gw, vw = GROUP * DK, heads * DK
    rows = rows.reshape(steps, GROUP, blocks, rep * 4, CH).transpose(0, 2, 1, 3, 4).reshape(steps, blocks, heads * 4, CH)
    early = lambda i: jnp.minimum(i, steps - 1)
    late = lambda i: jnp.maximum(i - steps, 0)
    both = lambda i: jnp.where(i < steps, i, i - steps)
    col = lambda when, count, width, off=0: pl.BlockSpec((count, width), lambda i: (0, off // width + when(i)))
    fixed = lambda shape: pl.BlockSpec(shape, lambda i: (0,) * len(shape))
    per = lambda when, shape: pl.BlockSpec(shape, lambda i: (when(i),) + (0,) * (len(shape) - 1))
    in_specs = [
        pl.BlockSpec(memory_space=pltpu.SMEM),
        col(early, tokens, gw), col(early, tokens, gw), col(early, tokens, vw), col(early, tokens, vw),
        col(early, SWAP, gw), col(early, SWAP, gw, qw), col(early, SWAP, vw, 2 * qw), col(early, SWAP, vw, 2 * qw + hv * DK),
        col(early, HALO, gw), col(early, HALO, gw, qw), col(early, HALO, vw, 2 * qw),
        col(both, TAPS, gw), col(both, TAPS, gw), col(both, TAPS, vw),
        fixed((TAPS - 1, tokens, CH)), fixed((blocks, CH, CH)), per(both, (1, blocks, heads * 4, CH)),
    ]
    ends = [col(late, HALO, gw), col(late, HALO, gw), col(late, HALO, vw)]
    end_shapes = [sds((HALO, qw)), sds((HALO, qw)), sds((HALO, hv * DK))]
    square = lambda *lead: pltpu.VMEM((steps, *lead, CH, CH), f32)
    wide = lambda width, dtype=f32: pltpu.VMEM((steps, tokens, width), dtype)
    units = blocks * heads
    sems = pltpu.SemaphoreType.DMA((steps,))
    return pl.pallas_call(
        functools.partial(fused_kernel, lax.axis_size("ctx"), steps),
        grid=(2 * steps,),
        in_specs=in_specs,
        out_specs=[col(late, tokens, vw), col(late, tokens, gw), col(late, tokens, gw), col(late, tokens, vw)]
        + ends + ends + [per(late, (1, blocks, 2 * heads, CH))],
        out_shape=[
            sds((tokens, hv * DK), bf16), sds((tokens, qw), bf16), sds((tokens, qw), bf16), sds((tokens, hv * DK), bf16)
        ] + end_shapes + end_shapes + [sds((steps, blocks, 2 * heads, CH))],
        scratch_shapes=[wide(gw), wide(gw), wide(vw), wide(gw), wide(gw), wide(vw, bf16)]
        + [square(units)] * 5 + [square(blocks * GROUP)] * 2 + [square(heads, 4)] * 2 + [square(heads)] * 7 + [sems] * 6,
        compiler_params=pltpu.CompilerParams(
            dimension_semantics=("arbitrary",), vmem_limit_bytes=56 * 2**20, collective_id=0, has_side_effects=True
        ),
        cost_estimate=pl.CostEstimate(
            flops=30 * hv * blocks * 8 * CH**3, bytes_accessed=8 * 2**20, transcendentals=2**21
        ),
        name="fused",
    )(*inputs, rows)


def body(
    q_raw, k_raw, v_raw, beta_logit, gate_logit, out_grad, conv_q, conv_k, conv_v, a_log, dt_bias, doc_ids, swap_blocks
):
    tokens = q_raw.shape[0]
    blocks = tokens // CH
    hk = q_raw.shape[1] // DK
    hv = v_raw.shape[1] // DK
    rep = hv // hk
    shards = lax.axis_size(SEQ)
    hops = max(1, shards // DOC_PARTS)
    core = lax.axis_index("pair")
    swap = swap_blocks[0]
    flags = jnp.stack([jnp.where(core == 1, swap, 0), jnp.where(core == 0, swap, 0)]).astype(jnp.int32)

    start = jnp.where(core == 0, SWAP, 0)
    logits = jnp.concatenate([beta_logit, gate_logit], axis=0)
    bg_send = lax.dynamic_slice_in_dim(logits, start, SWAP, 1)
    send = jnp.concatenate(
        [lax.dynamic_slice_in_dim(x, start, SWAP, 0) for x in (q_raw, k_raw, v_raw, out_grad)], axis=1
    )
    got = lax.ppermute(send, "pair", [(0, 1), (1, 0)])
    send, bg_send, tail_ids, tails = lax.optimization_barrier(
        (send, bg_send, doc_ids[tokens - HALO :], [x[tokens - HALO :] for x in (q_raw, k_raw, v_raw)])
    )
    bg_got = lax.ppermute(bg_send, "pair", [(0, 1), (1, 0)])
    ids_col = jnp.broadcast_to((tail_ids + 1).astype(bf16)[:, None], (HALO, CH))
    tail = jnp.concatenate(tails + [ids_col], axis=1)
    before = shifted(tail, 1)
    own = jnp.concatenate([x[SWAP - HALO : SWAP] for x in (q_raw, k_raw, v_raw)], axis=1)
    chans = own.shape[1]
    halo = jnp.where(flags[0] > 0, own, before[:, :chans]).astype(f32)
    qw = hk * DK

    first = jnp.where(flags[0] > 0, bg_got, logits[:, :SWAP])
    second = jnp.where(flags[1] > 0, bg_got, logits[:, SWAP:])
    logits = jnp.concatenate([first, second], axis=1).astype(f32)
    beta = jax.nn.sigmoid(logits[:hv])
    gate = logits[hv:] + dt_bias[:, None]
    rate = -jnp.exp(a_log)[:, None]
    decay_log = rate * jax.nn.softplus(gate)
    c = jnp.dot(decay_log.reshape(hv * blocks, CH), tri(True), precision=highest).reshape(hv, blocks, CH)
    ids = doc_ids.astype(f32) + 1.0
    ext_ids = jnp.concatenate([before[:, chans].astype(f32), ids])
    doc = ids.reshape(blocks, CH)
    doc_before = ext_ids[HALO - 1 : HALO - 1 + tokens : CH]
    s = jnp.where(doc == doc_before[:, None], jnp.exp(c), 0.0)
    w = jnp.where(doc == doc[:, CH - 1 :], jnp.exp(jnp.minimum(c[:, :, CH - 1 :] - c, 0.0)), 0.0)
    rows = jnp.stack([beta.reshape(hv, blocks, CH), c, s, w], axis=2)
    rows = rows.reshape(hk, rep, blocks, 4, CH).transpose(0, 2, 1, 3, 4).reshape(hk, blocks, rep * 4, CH)
    docs = ((doc[:, :, None] == doc[:, None, :]) & (tri(False) > 0)[None]).astype(f32)
    masks = jnp.stack(
        [
            jnp.broadcast_to((ext_ids[HALO - d : HALO - d + tokens] == ids).astype(f32)[:, None], (tokens, CH))
            for d in range(1, TAPS)
        ]
    )
    taps = [x.astype(f32) for x in (conv_q, conv_k, conv_v)]

    if shards // DOC_PARTS == lax.axis_size("pair") and blocks == 2:
        results = fused_call(
            (flags, q_raw, k_raw, v_raw, out_grad, got, got, got, got, halo, halo, halo, *taps, masks, docs), rows, hk, hv,
            tokens,
        )
        rows_out = results[10].reshape(hk // GROUP, blocks, GROUP, 2 * rep, CH).transpose(0, 2, 1, 3, 4)
        rows_out = rows_out.reshape(hk, blocks, 2 * rep, CH)
    else:
        results = staged_call(
            (flags, q_raw, k_raw, v_raw, out_grad, got, got, got, got, halo, halo, halo, *taps, masks, docs, rows), hk, hv,
            tokens, hops,
        )
        rows_out = results[10][:, :, : 2 * rep]
    layer_out, q_grad, k_grad, v_grad = results[:4]
    spilled = shifted(jnp.concatenate(results[7:10], axis=1), -1)
    ends_out = []
    at = 0
    for grad, end in zip((q_grad, k_grad, v_grad), results[4:7]):
        width = end.shape[1]
        last = (end + spilled[:, at : at + width]).astype(bf16)
        ends_out.append(lax.dynamic_update_slice(grad, last, (tokens - HALO, 0)))
        at += width
    rg = rows_out.reshape(hk, blocks, rep, 2, CH).transpose(3, 0, 2, 1, 4)
    dbeta = rg[0].reshape(hv, tokens)
    dg = jnp.dot(rg[1].reshape(hv * blocks, CH), tri(False), precision=highest).reshape(hv, tokens)
    beta_grad = dbeta * beta * (1.0 - beta)
    gate_grad = dg * rate * jax.nn.sigmoid(gate)
    return (layer_out, ends_out[0], ends_out[1], ends_out[2], beta_grad.astype(bf16), gate_grad.astype(bf16))


def solution(mesh):
    rows = P(("groups", "ctx", "pair"), "head")
    rates = P("head", ("groups", "ctx", "pair"))
    taps = P(None, "head")
    return jax.shard_map(
        body,
        mesh=mesh,
        in_specs=(
            rows, rows, rows, rates, rates, rows, taps, taps, taps, P("head"), P("head"),
            P(("groups", "ctx", "pair")), P(("groups", "ctx")),
        ),
        out_specs=(rows, rows, rows, rows, rates, rates),
        check_vma=False,
    )
```

```python
import functools
import math

import jax
import jax.numpy as jnp
from jax import lax
from jax.experimental import pallas as pl
from jax.experimental.pallas import tpu as pltpu
from jax.sharding import PartitionSpec as P

DK = 128
TAPS = 4
CH = 128
SWAP = 128
HALO = 8
GUARD = 1e-06
SCALE = 1.0 / math.sqrt(DK)
DOC_PARTS = 4
GROUP = 2
BASE = 32
KINDS = 5

f32 = jnp.float32
bf16 = jnp.bfloat16
highest = lax.Precision.HIGHEST
SEQ = ("ctx", "pair")


def split(x):
    high = x.astype(bf16)
    return high, (x - high.astype(f32)).astype(bf16)


def mm(a, b):
    ah, al = split(a)
    bh, bl = split(b)
    lhs = jnp.concatenate([ah, al], axis=1)
    rhs = jnp.concatenate(
        [jnp.concatenate([bh, bl], axis=1), jnp.concatenate([bh, jnp.zeros_like(bh)], axis=1)], axis=0
    )
    r = lax.dot_general(lhs, rhs, (((1,), (0,)), ((), ())), preferred_element_type=f32)
    n = b.shape[1]
    return r[:, :n] + r[:, n:]


def mm_half(a, b):
    return lax.dot_general(
        jnp.concatenate(split(a), axis=1), jnp.concatenate([b, b], axis=0), (((1,), (0,)), ((), ())),
        preferred_element_type=f32,
    )


def odd_blocks(x, size):
    return jnp.concatenate([x[i : i + size] for i in range(size, CH, 2 * size)], axis=0)


def with_odd(even, odd, size):
    parts = []
    for i in range(0, CH // 2, size):
        parts.append(jnp.zeros((size, CH), odd.dtype) if even is None else even[2 * i : 2 * i + size])
        parts.append(odd[i : i + size])
    return jnp.concatenate(parts, axis=0)


def mm_nt(a, b):
    ah, al = split(a)
    bh, bl = split(b)
    lhs = jnp.concatenate([ah, al], axis=1)
    rhs = jnp.concatenate(
        [jnp.concatenate([bh, bh], axis=1), jnp.concatenate([bl, jnp.zeros_like(bl)], axis=1)], axis=0
    )
    r = lax.dot_general(lhs, rhs, (((1,), (1,)), ((), ())), preferred_element_type=f32)
    n = b.shape[0]
    return r[:, :n] + r[:, n:]


def mm_nt_split(lhs, b):
    bh, bl = split(b)
    rhs = jnp.concatenate(
        [jnp.concatenate([bh, bh], axis=1), jnp.concatenate([bl, jnp.zeros_like(bl)], axis=1)], axis=0
    )
    r = lax.dot_general(lhs, rhs, (((1,), (1,)), ((), ())), preferred_element_type=f32)
    n = b.shape[0]
    return r[:, :n] + r[:, n:]


def iota(axis):
    return lax.broadcasted_iota(jnp.int32, (CH, CH), axis)


def rowsum(x):
    return jnp.sum(x, axis=1, keepdims=True)


def columns(rows):
    return jnp.concatenate([rows, jnp.zeros((CH - rows.shape[0], CH), f32)], axis=0).T


def sigmoid(a):
    return 1.0 / (1.0 + jnp.exp(-a))


def fetch(raw, recv, flags):
    first = raw[:SWAP, :]
    second = raw[SWAP:, :]
    got = recv[...]
    first = jnp.where(flags[0] > 0, got, first)
    second = jnp.where(flags[1] > 0, got, second)
    return jnp.concatenate([first, second], axis=0)


def conv(x, halo, taps, masks):
    ext = jnp.concatenate([halo, x], axis=0)
    width = x.shape[1] // CH
    total = taps[TAPS - 1 : TAPS, :] * x
    for d in range(1, TAPS):
        moved = pltpu.roll(ext, d, 0)[HALO:, :]
        mask = masks[d - 1]
        if width > 1:
            mask = jnp.concatenate([mask] * width, axis=1)
        total = total + taps[TAPS - 1 - d : TAPS - d, :] * (moved * mask)
    return total


def conv_back(da, taps, masks):
    width = da.shape[1] // CH
    zeros = jnp.zeros((HALO, da.shape[1]), f32)
    total = taps[TAPS - 1 : TAPS, :] * jnp.concatenate([da, zeros], axis=0)
    size = total.shape[0]
    for d in range(1, TAPS):
        mask = masks[d - 1]
        if width > 1:
            mask = jnp.concatenate([mask] * width, axis=1)
        ext = jnp.concatenate([da * mask, zeros], axis=0)
        total = total + taps[TAPS - 1 - d : TAPS - d, :] * pltpu.roll(ext, size - d, 0)
    return total


def local_maps(
    flags, q_raw, k_raw, v_raw, g_raw, q_got, k_got, v_got, g_got, q_halo, k_halo, v_halo,
    q_taps, k_taps, v_taps, masks, docs, rows,
    a_q, a_k, a_v, qn_out, kn_out, seq_grad, inv_out, kk_out, qk_out, pdo_out,
):
    blocks = q_raw.shape[0] // CH
    qa = conv(fetch(q_raw, q_got, flags).astype(f32), q_halo[...], q_taps, masks)
    ka = conv(fetch(k_raw, k_got, flags).astype(f32), k_halo[...], k_taps, masks)
    va = conv(fetch(v_raw, v_got, flags).astype(f32), v_halo[...], v_taps, masks)
    a_q[...] = qa
    a_k[...] = ka
    a_v[...] = va
    gs = fetch(g_raw, g_got, flags)
    seq_grad[...] = gs
    do_all = gs
    qu = qa * sigmoid(qa)
    ku = ka * sigmoid(ka)
    v_all = va * sigmoid(va)
    qn = qu * (SCALE / jnp.sqrt(rowsum(qu * qu) + GUARD))
    kn = ku * (1.0 / jnp.sqrt(rowsum(ku * ku) + GUARD))
    qn_out[...] = qn
    kn_out[...] = kn
    row, col = iota(0), iota(1)
    eye = (row == col).astype(f32)
    heads = v_raw.shape[1] // CH
    state = []
    for n in range(blocks):
        q = qn[n * CH : (n + 1) * CH]
        k = kn[n * CH : (n + 1) * CH]
        both = mm_nt(jnp.concatenate([k, q], axis=0), k)
        kk, qk = both[:CH], both[CH:]
        kk_out[0, n] = kk
        qk_out[0, n] = qk
        q_t, k_t = q.T, k.T
        flat = rows[0, n]
        cols = columns(flat)
        for e in range(heads):
            beta, c, s, w = [cols[:, 4 * e + i : 4 * e + i + 1] for i in range(4)]
            beta_r, c_r, s_r, w_r = [flat[4 * e + i : 4 * e + i + 1, :] for i in range(4)]
            s_last = s_r[:, CH - 1 :]
            decay = jnp.exp(jnp.minimum(c - c_r, 0.0)) * docs[n]
            low = jnp.where(row > col, beta * decay * kk, 0.0)
            do = do_all[n * CH : (n + 1) * CH, e * CH : (e + 1) * CH]
            v = v_all[n * CH : (n + 1) * CH, e * CH : (e + 1) * CH]
            state.append((n, e, low, decay * qk, do, v, k * w, (beta_r * s_r) * k_t, beta * s * k, s_r * q_t, beta * v, s_last))
    inv = []
    for item in state:
        inv.append(eye - jnp.where((row >> 1) == (col >> 1), item[2], 0.0))
    size = 1
    while (2 << size) <= CH:
        near = ((row >> (size + 1)) == (col >> (size + 1))) & ((row >> size) != (col >> size))
        width = 1 << size
        if width < 8:
            half = [mm(jnp.where(near, item[2], 0.0), t) for item, t in zip(state, inv)]
            inv = [t - mm(t, h) for t, h in zip(inv, half)]
        else:
            half = [mm(odd_blocks(jnp.where(near, item[2], 0.0), width), t) for item, t in zip(state, inv)]
            odds = [odd_blocks(t, width) for t in inv]
            odds = [t - mm(t, with_odd(None, h, width)) for t, h in zip(odds, half)]
            inv = [with_odd(t, o, width) for t, o in zip(inv, odds)]
        size += 1
    maps = {}
    for item, t in zip(state, inv):
        n, e, low, p, do, v, kw, bsk_t, bsk, sq_t, bv, s_last = item
        inv_out[0, e, n] = t
        pdo = mm_half(p.T, do)
        pdo_out[0, e, n] = pdo
        t_t = t.T
        b = mm(t_t, kw)
        cc = mm(t_t, pdo)
        b_t = b.T
        m = s_last * eye - mm(b_t, bsk)
        a = mm(b_t, bv)
        g = mm_half(sq_t, do) - mm(bsk_t, cc)
        maps[n, e] = (m, a, g)
    results = []
    for e in range(heads):
        m, a, g = maps[0, e]
        for n in range(1, blocks):
            m2, a2, g2 = maps[n, e]
            g = g + mm(m.T, g2)
            a = mm(m2, a) + a2
            m = mm(m2, m)
        results.append((m, a, g))
    return results


def prepare_kernel(*refs):
    m_out, a_out, g_out = refs[-3:]
    for e, (m, a, g) in enumerate(local_maps(*refs[:-3])):
        m_out[e] = m
        a_out[e] = a
        g_out[e] = g


def inverse_blocks(lows, size, fillers):
    regs = size // 8
    lane = lax.broadcasted_iota(jnp.int32, (8, CH), 1)
    sub = lax.broadcasted_iota(jnp.int32, (8, CH), 0)
    base = lane - lax.rem(lane, size)
    packed, inv = [], []
    for low in lows:
        rows_, eyes = [], []
        for r in range(regs):
            acc = low[8 * r : 8 * r + 8]
            for at in range(size, CH, size):
                acc = jnp.where(lane >= at, low[at + 8 * r : at + 8 * r + 8], acc)
            rows_.append(acc)
            eyes.append((lane - base == sub + 8 * r).astype(f32))
        packed.append(rows_)
        inv.append(eyes)
    fillers = list(fillers)
    every = max(1, (size - 1) // max(1, len(fillers)))
    for j in range(size - 1):
        here = j // 8
        index = base + j
        for low, t in zip(packed, inv):
            line = jnp.broadcast_to(t[here][j % 8 : j % 8 + 1], (8, CH))
            for r in range(here if j % 8 < 7 else here + 1, regs):
                t[r] = t[r] - jnp.take_along_axis(low[r], index, axis=1, mode="promise_in_bounds") * line
        if fillers and j % every == 0:
            fillers.pop(0)()
    for filler in fillers:
        filler()
    return [
        jnp.concatenate([jnp.where(base == at, x, 0.0) for at in range(0, CH, size) for x in t], axis=0) for t in inv
    ]


def head_scalars(cols, flat, e, heads):
    return (
        [cols[:, i * heads + e : i * heads + e + 1] for i in range(KINDS)],
        [flat[i * heads + e : i * heads + e + 1, :] for i in range(KINDS)],
    )


def part(x, n, h):
    return x[n * CH : (n + 1) * CH, h * CH : (h + 1) * CH]


def tile(h):
    return slice(h * CH, (h + 1) * CH)


def summed(x, weights):
    high = x.astype(bf16)
    rest = x - high.astype(f32)
    middle = rest.astype(bf16)
    low = (rest - middle.astype(f32)).astype(bf16)
    n = x.shape[0]
    r = lax.dot_general(
        jnp.concatenate([high, middle, low], axis=0), weights, (((1,), (0,)), ((), ())), preferred_element_type=f32
    )
    return r[:n] + r[n : 2 * n] + r[2 * n :]


def per_head(ref, count):
    row = lax.broadcasted_iota(jnp.int32, (count, CH), 0)
    total = jnp.zeros((count, CH), f32)
    for h in range(count):
        total = jnp.where(row == h, ref[h], total)
    return total


def setup_phase(
    has_prev, swaps, a_log, dt_bias, beta_logit, gate_logit, doc_ids, beta_got, gate_got, ids_got,
    masks, docs, rows, betas, factors,
):
    blocks = doc_ids.shape[0]
    steps = rows.shape[0]
    hv = beta_logit.shape[0]
    heads = hv // steps
    row, col = iota(0), iota(1)
    before = jnp.where(has_prev, ids_got[blocks - 1 :].astype(f32) + 1.0, 0.0)
    ids = jnp.concatenate(
        [before, doc_ids[...].astype(f32) + 1.0, jnp.zeros((8 - 1 - blocks, CH), f32)], axis=0
    )
    lane = lax.broadcasted_iota(jnp.int32, (8, CH), 1)
    same = []
    for d in range(1, TAPS):
        moved = pltpu.roll(ids, d, 1)
        moved = jnp.where(lane < d, pltpu.roll(moved, 1, 0), moved)
        same.append((moved == ids).astype(f32))
    rate = -jnp.exp(per_head(a_log, hv))
    bias = per_head(dt_bias, hv)
    logs = []
    for n in range(blocks):
        cols = columns(jnp.concatenate([x[n + 1 : n + 2] for x in same] + [ids[n + 1 : n + 2]], axis=0))
        for d in range(TAPS - 1):
            masks[d, n * CH : (n + 1) * CH] = jnp.broadcast_to(cols[:, d : d + 1], (CH, CH))
        here = (cols[:, TAPS - 1 : TAPS] == ids[n + 1 : n + 2]) & (row >= col)
        docs[n] = jnp.where(here, 1.0, 0.0)
        beta = jnp.where(swaps[n] > 0, beta_got[...], beta_logit[:, tile(n)]).astype(f32)
        gate = jnp.where(swaps[n] > 0, gate_got[...], gate_logit[:, tile(n)]).astype(f32) + bias
        betas[n] = sigmoid(beta)
        factors[n] = rate * sigmoid(gate)
        logs.append(rate * (jnp.maximum(gate, 0.0) + jnp.log1p(jnp.exp(-jnp.abs(gate)))))
    sums = summed(jnp.concatenate(logs, axis=0), (row <= col).astype(bf16))
    for n in range(blocks):
        doc = ids[n + 1 : n + 2]
        c = sums[n * hv : (n + 1) * hv]
        s = jnp.where(doc == ids[n : n + 1, CH - 1 :], jnp.exp(c), 0.0)
        w = jnp.where(doc == doc[:, CH - 1 :], jnp.exp(jnp.minimum(c[:, CH - 1 :] - c, 0.0)), 0.0)
        beta = betas[n]
        for i, x in enumerate((beta, c, s, w, beta * s)):
            for j in range(steps):
                rows[j, n, i * heads : (i + 1) * heads] = x[j * heads : (j + 1) * heads]


def forward_phase(
    j, first, swaps, q_raw, k_raw, v_raw, g_raw, q_taps, k_taps, v_taps,
    q_got, k_got, v_got, g_got, q_halo, k_halo, v_halo, masks, docs, rows,
    q_scale, k_scale, v_scale, v_out, qn_out, kn_out, grad_out,
    inv_out, decay_out, ub_out, ws_out, pdo_out, kk_out, qk_out, maps, affs, w_buf,
):
    keys = q_raw.shape[1] // CH
    heads = v_raw.shape[1] // CH
    rep = heads // keys
    blocks = q_raw.shape[0] // CH
    mask = [masks[d] for d in range(TAPS - 1)]
    tail = 2 * HALO

    def fetched(raw, got, h):
        parts = [jnp.where(swaps[n] > 0, got[j, :, tile(h)], raw[n * CH : (n + 1) * CH, tile(h)]) for n in range(blocks)]
        return jnp.concatenate(parts, axis=0)

    def activate(raw, got, halo, taps, h):
        own = raw[SWAP - tail : SWAP, tile(h)]
        before = jnp.where(swaps[0] > 0, own, halo[j, :, tile(h)]).astype(f32)[HALO:]
        x = conv(fetched(raw, got, h).astype(f32), before, taps[:, tile(h)].astype(f32), mask)
        sig = sigmoid(x)
        u = x * sig
        return u, sig + u * (1.0 - sig)

    def unit(raw, got, halo, taps, h, scale, out, scale_out):
        u, slope = activate(raw, got, halo, taps, h)
        factor = scale / jnp.sqrt(rowsum(u * u) + GUARD)
        y = u * factor
        out[j, :, tile(h)] = y
        scale_out[j, :, tile(h)] = slope * factor
        return y

    kn = [unit(k_raw, k_got, k_halo, k_taps, h, 1.0, kn_out, k_scale) for h in range(keys)]
    qn = [unit(q_raw, q_got, q_halo, q_taps, h, SCALE, qn_out, q_scale) for h in range(keys)]
    row, col = iota(0), iota(1)
    eye = (row == col).astype(f32)
    units = []
    for n in range(blocks):
        flat = rows[j, n]
        cols = columns(flat)
        for h in range(keys):
            q, k = qn[h][n * CH : (n + 1) * CH], kn[h][n * CH : (n + 1) * CH]
            both = mm_nt(jnp.concatenate([k, q], axis=0), k)
            kk, qk = both[:CH], both[CH:]
            kk_out[j, n * keys + h] = kk
            qk_out[j, n * keys + h] = qk
            q_t, k_t = q.T, k.T
            for e in range(h * rep, (h + 1) * rep):
                (beta, c, s, w, bs), (beta_r, c_r, s_r, w_r, bs_r) = head_scalars(cols, flat, e, heads)
                decay = jnp.exp(jnp.minimum(c - c_r, 0.0)) * docs[n]
                decay_out[j, n * heads + e] = decay
                low = jnp.where(row > col, beta * decay * kk, 0.0)
                units.append((n, e, low, decay * qk, beta, bs * k, k_t * w_r, s_r * q_t, s_r[:, CH - 1 :]))
    values, by_do = {}, {}

    def value(e):
        u, slope = activate(v_raw, v_got, v_halo, v_taps, e)
        v_out[j, :, tile(e)] = u
        v_scale[j, :, tile(e)] = slope
        values[e] = u

    def output(u):
        n, e, p, sq_t = u[0], u[1], u[3], u[7]
        do = jnp.where(swaps[n] > 0, g_got[j, :, tile(e)], g_raw[n * CH : (n + 1) * CH, tile(e)])
        grad_out[j, n * CH : (n + 1) * CH, tile(e)] = do
        by_do[n, e] = mm_half(jnp.concatenate([p.T, sq_t], axis=0), do)
        pdo_out[j, n * heads + e] = by_do[n, e][:CH]

    fillers = [functools.partial(output, u) for u in units] + [functools.partial(value, e) for e in range(heads)]
    inv = inverse_blocks([u[2] for u in units], BASE, fillers)
    size = BASE.bit_length() - 1
    while (1 << size) < CH:
        near = ((row >> (size + 1)) == (col >> (size + 1))) & ((row >> size) != (col >> size))
        width = 1 << size
        half = [mm(odd_blocks(jnp.where(near, u[2], 0.0), width), t) for u, t in zip(units, inv)]
        odds = [odd_blocks(t, width) for t in inv]
        odds = [t - mm(t, with_odd(None, h, width)) for t, h in zip(odds, half)]
        inv = [with_odd(t, o, width) for t, o in zip(inv, odds)]
        size += 1
    solved = []
    for (n, e, low, p, beta, bsk, kw_t, sq_t, s_last), t in zip(units, inv):
        inv_out[j, n * heads + e] = t
        ub = mm(t, beta * values[e][n * CH : (n + 1) * CH])
        ws = mm(t, bsk)
        ub_out[j, n * heads + e] = ub
        ws_out[j, n * heads + e] = ws
        solved.append((ub, ws))
    result = {}
    for (n, e, low, p, beta, bsk, kw_t, sq_t, s_last), (ub, ws) in zip(units, solved):
        a = mm(kw_t, ub)
        m = s_last * eye - mm(kw_t, ws)
        g = by_do[n, e][CH:] - mm(ws.T, by_do[n, e][:CH])
        result[n, e] = (m, m.T, a, g)
    for e in range(heads):
        m0, m0_t, a0, g0 = result[0, e]
        m1, m1_t, a1, g1 = result[1, e]
        for i, x in enumerate((m0, m1, m1_t, m0_t)):
            maps[j, e, i] = x
        for i, x in enumerate((a0, a1, g1, g0)):
            affs[j, e, i] = x
        w_buf[j, e] = jnp.where(first, a1, g0) + mm(jnp.where(first, m1, m0_t), jnp.where(first, a0, g1))


def backward_phase(
    j, first, other, q_taps, k_taps, v_taps, masks, rows,
    q_scale, k_scale, v_scale, v_all, qn, kn, seq_grad, inv, decays, ub_in, ws_in, pdo_in, kk_in, qk_in,
    maps, affs, y_buf, s_buf, z_got, out, q_body, k_body, v_body, q_tail, k_tail, v_tail, spill, row_grads,
):
    tokens = qn.shape[1]
    blocks = tokens // CH
    keys = qn.shape[2] // CH
    heads = v_all.shape[2] // CH
    rep = heads // keys
    row, col = iota(0), iota(1)
    states, leaving = [], []
    for e in range(heads):
        y, s1, z = y_buf[j, e], s_buf[j, e], z_got[j, e]
        t1 = affs[j, e, other] + mm(maps[j, e, other], z)
        states.append((jnp.where(first, y, z), jnp.where(first, s1, t1)))
        leaving.append((jnp.where(first, t1, s1), jnp.where(first, z, y)))
    info = []
    for n in range(blocks):
        flat = rows[j, n]
        info.append((flat, columns(flat)))
    order = [(n, e) for n in range(blocks) for e in range(heads)]
    work = {}

    def at(ref, n, h):
        return ref[j, n * CH : (n + 1) * CH, tile(h)]

    for n, e in order:
        flat, cols = info[n]
        (beta, c, s, w, bs), rs = head_scalars(cols, flat, e, heads)
        i = n * heads + e
        q, k = at(qn, n, e // rep), at(kn, n, e // rep)
        st, ds_out = states[e][n], leaving[e][n]
        by_st = mm(jnp.concatenate([ws_in[j, i], q], axis=0), st)
        u = ub_in[j, i] - by_st[:CH]
        du = pdo_in[j, i] + mm(k * w, ds_out)
        work[n, e] = (by_st[CH:], u, du)
    for n, e in order:
        flat, cols = info[n]
        (beta, c, s, w, bs), rs = head_scalars(cols, flat, e, heads)
        i = n * heads + e
        qs, u, du = work[n, e]
        o = s * qs + mm(decays[j, i] * qk_in[j, n * keys + e // rep], u)
        out[n * CH : (n + 1) * CH, tile(e)] = o.astype(bf16)
        work[n, e] = (qs, u, mm(inv[j, i].T, du))
    dqs, dks, dvs = {}, {}, {}
    none = jnp.zeros((CH, CH), bf16)
    for n in range(blocks):
        flat, cols = info[n]
        packed = jnp.zeros((CH, CH), f32)
        minus = []
        for h in range(keys):
            q, k = at(qn, n, h), at(kn, n, h)
            kk, qk = kk_in[j, n * keys + h], qk_in[j, n * keys + h]
            dqk_sum = dkk_sum = dq = dk = 0.0
            for e in range(h * rep, (h + 1) * rep):
                (beta, c, s, w, bs), rs = head_scalars(cols, flat, e, heads)
                s_last = rs[2][:, CH - 1 :]
                i = n * heads + e
                qs, u, y = work[n, e]
                st, ds_out = states[e][n], leaving[e][n]
                do_half = at(seq_grad, n, e)
                do = do_half.astype(f32)
                y_high, y_low = split(y)
                do_y = jnp.concatenate(
                    [jnp.concatenate([do_half, y_high], axis=0), jnp.concatenate([none, y_low], axis=0)], axis=1
                )
                by_u = mm_nt_split(do_y, u)
                by_s = mm_nt_split(do_y, st)
                dos, zneg = by_s[:CH], by_s[CH:]
                dkw = mm_nt(u, ds_out)
                decay = decays[j, i]
                dpd = by_u[:CH] * decay
                dls = by_u[CH:] * jnp.where(row > col, decay, 0.0)
                dlb = dls * kk
                f = dpd * qk - beta * dlb
                zk = zneg * k
                wk = w * (dkw * k)
                dbeta = rowsum(y * at(v_all, n, e) - s * zk - dlb)
                extra = jnp.sum(rowsum(wk + s_last * (ds_out * st)), axis=0, keepdims=True)
                dc = rowsum(f + s * (do * qs) - bs * zk - wk)
                dc = dc + jnp.where(row[:, :1] == CH - 1, extra, 0.0)
                packed = jnp.where(col == e, dbeta, packed)
                packed = jnp.where(col == heads + e, dc, packed)
                minus.append(jnp.sum(f, axis=0, keepdims=True))
                dqk_sum = dqk_sum + dpd
                dkk_sum = dkk_sum + beta * dls
                dq = dq + s * dos
                dk = dk + w * dkw - bs * zneg
                dvs[n, e] = beta * y
            by_k = mm(jnp.concatenate([dqk_sum, dkk_sum + dkk_sum.T], axis=0), k)
            dqs[n, h] = dq + by_k[:CH]
            dks[n, h] = dk + mm(dqk_sum.T, q) - by_k[CH:]
        row_grads[j, n] = packed.T[: 2 * heads] - jnp.concatenate([jnp.zeros((heads, CH), f32)] + minus, axis=0)
    mask = [masks[d] for d in range(TAPS - 1)]
    at_col = 0
    for grads, count, taps, body_out, tail_out, y_ref, scale_ref, gain in (
        (dqs, keys, q_taps, q_body, q_tail, qn, q_scale, DK),
        (dks, keys, k_taps, k_body, k_tail, kn, k_scale, 1),
        (dvs, heads, v_taps, v_body, v_tail, None, v_scale, 1),
    ):
        for h in range(count):
            da = jnp.concatenate([grads[n, h] for n in range(blocks)], axis=0)
            if y_ref is not None:
                y = y_ref[j, :, tile(h)]
                da = da - y * (rowsum(y * da) * float(gain))
            full = conv_back(da * scale_ref[j, :, tile(h)], taps[:, tile(h)].astype(f32), mask)
            body_out[j, :, tile(h)] = full[:tokens].astype(bf16)
            tail_out[j, :, tile(h)] = full[tokens - 2 * HALO : tokens]
            spill[j, :, at_col : at_col + CH] = full[tokens:]
            at_col += CH


def fused_kernel(ctxs, steps, *refs):
    swap_ref, a_log, dt_bias, beta_logit, gate_logit, doc_ids = refs[:6]
    raws, taps, sources, refs = refs[6:10], refs[10:13], refs[13:20], refs[20:]
    (out, *grads, beta_grad, gate_grad), refs = refs[:6], refs[6:]
    gots, halos, (beta_got, gate_got, ids_got), refs = refs[:4], refs[4:7], refs[7:10], refs[10:]
    (masks, docs, rows, betas, factors), refs = refs[:5], refs[5:]
    saved, refs = refs[:14], refs[14:]
    (maps, affs, w_buf, w_got, x_buf, y_buf, s_buf, z_buf, z_got), refs = refs[:9], refs[9:]
    bodies, tails, (spill, spill_got, row_grads), refs = refs[:3], refs[3:6], refs[6:9], refs[9:]
    swap_s, swap_r, hop_s, hop_r, pair_s, pair_r, spill_s, spill_r, got_s, got_r, halo_s, halo_r, few_s, few_r = refs
    step = pl.program_id(0)
    heads = w_buf.shape[1]
    tokens = raws[0].shape[0]
    core = lax.axis_index("pair")
    ctx = lax.axis_index("ctx")
    first = core == 0
    mine, other = 2 * core, 2 - 2 * core
    peer_ctx = jnp.where(first, ctx - 1, ctx + 1)
    has_peer = (peer_ctx >= 0) & (peer_ctx < ctxs)
    has_prev = jnp.logical_not(first) | has_peer
    has_next = first | has_peer
    partner = {"pair": 1 - core}
    peer = {"ctx": jnp.clip(peer_ctx, 0, ctxs - 1), "pair": 1 - core}
    following = {"ctx": jnp.clip(ctx + core, 0, ctxs - 1), "pair": 1 - core}
    previous = {"ctx": jnp.clip(ctx - 1 + core, 0, ctxs - 1), "pair": 1 - core}
    swap_flag = swap_ref[0]
    swaps = [jnp.where(first, 0, swap_flag), jnp.where(first, swap_flag, 0)]

    def remote(src, dst, send, recv, device):
        return pltpu.make_async_remote_copy(src, dst, send, recv, device_id=device, device_id_type=pl.DeviceIdType.MESH)

    def swap(j):
        return remote(w_buf.at[j], w_got.at[j], swap_s.at[j], swap_r.at[j], partner)

    def hop(j):
        return remote(x_buf.at[j], y_buf.at[j], hop_s.at[j], hop_r.at[j], peer)

    def pair(j):
        return remote(z_buf.at[j], z_got.at[j], pair_s.at[j], pair_r.at[j], partner)

    def spilled(j):
        return remote(spill.at[j], spill_got.at[j], spill_s.at[j], spill_r.at[j], previous)

    start = pl.multiple_of(jnp.where(first, SWAP, 0), SWAP)

    def exchanged(i, j):
        width = gots[i].shape[2]
        at = pl.multiple_of(j * width, CH)
        return remote(
            sources[i].at[pl.ds(start, SWAP), pl.ds(at, width)], gots[i].at[j], got_s.at[i, j], got_r.at[i, j], partner
        )

    def neighbour(i, j):
        width = halos[i].shape[2]
        at = pl.multiple_of(j * width, CH)
        return remote(
            sources[i].at[pl.ds(tokens - 2 * HALO, 2 * HALO), pl.ds(at, width)], halos[i].at[j], halo_s.at[i, j],
            halo_r.at[i, j], following,
        )

    def logits(i):
        return remote(sources[4 + i].at[:, pl.ds(start, SWAP)], (beta_got, gate_got)[i], few_s.at[i], few_r.at[i], partner)

    ids_copy = remote(sources[6], ids_got, few_s.at[2], few_r.at[2], following)

    @pl.when(step == 0)
    def _():
        barrier = pltpu.get_barrier_semaphore()
        pl.semaphore_signal(barrier, inc=1, device_id=partner, device_id_type=pl.DeviceIdType.MESH)

        @pl.when(has_peer)
        def _():
            pl.semaphore_signal(barrier, inc=1, device_id=peer, device_id_type=pl.DeviceIdType.MESH)

        pl.semaphore_wait(barrier, jnp.where(has_peer, 2, 1))

        @pl.when(has_next)
        def _():
            ids_copy.start()

        for i in range(2):
            logits(i).start()
        for j in range(steps):
            for i in range(4):
                exchanged(i, j).start()

            @pl.when(has_next)
            def _():
                for i in range(3):
                    neighbour(i, j).start()

        @pl.when(has_prev)
        def _():
            ids_copy.wait_recv()

        @pl.when(jnp.logical_not(has_prev))
        def _():
            ids_got[...] = jnp.zeros(ids_got.shape, jnp.int32)
            for halo in halos:
                halo[...] = jnp.zeros(halo.shape, bf16)

        for i in range(2):
            logits(i).wait_recv()
        setup_phase(
            has_prev, swaps, a_log, dt_bias, beta_logit, gate_logit, doc_ids, beta_got, gate_got, ids_got,
            masks, docs, rows, betas, factors,
        )

    def advance(j, at, got):
        mid = [affs[j, e, at] + mm(maps[j, e, at], got[j, e]) for e in range(heads)]
        return mid, [affs[j, e, at + 1] + mm(maps[j, e, at + 1], mid[e]) for e in range(heads)]

    def chains(over, back):
        if over:
            swap(step - 1).wait_recv()
        if back:
            @pl.when(has_peer)
            def _():
                hop(step - 2).wait_recv()

            @pl.when(jnp.logical_not(has_peer))
            def _():
                y_buf[step - 2] = jnp.zeros(y_buf.shape[1:], f32)

        if over:
            mid, end = advance(step - 1, other, w_got)
            for e in range(heads):
                x_buf[step - 1, e] = end[e]
        if back:
            mid, end = advance(step - 2, mine, y_buf)
            for e in range(heads):
                s_buf[step - 2, e] = mid[e]
                z_buf[step - 2, e] = end[e]
        if over:
            @pl.when(has_peer)
            def _():
                hop(step - 1).start()

        if back:
            pair(step - 2).start()

    @pl.when(step == 1)
    def _():
        chains(True, False)

    @pl.when((step >= 2) & (step <= steps))
    def _():
        chains(True, True)

    @pl.when(step == steps + 1)
    def _():
        chains(False, True)

    @pl.when(step < steps)
    def _():
        for i in range(4):
            exchanged(i, step).wait_recv()

        @pl.when(has_prev)
        def _():
            for i in range(3):
                neighbour(i, step).wait_recv()

        forward_phase(step, first, swaps, *raws, *taps, *gots, *halos, masks, docs, rows, *saved, maps, affs, w_buf)
        swap(step).start()

    @pl.when((step >= steps) & (step < 2 * steps))
    def _():
        j = step - steps
        pair(j).wait_recv()
        backward_phase(
            j, first, other, *taps, masks, rows, *saved, maps, affs, y_buf, s_buf, z_got, out, *bodies, *tails, spill,
            row_grads,
        )

        @pl.when(has_prev)
        def _():
            spilled(j).start()

    @pl.when(step > steps)
    def _():
        j = step - steps - 1

        @pl.when(has_next)
        def _():
            spilled(j).wait_recv()

        @pl.when(jnp.logical_not(has_next))
        def _():
            spill_got[j] = jnp.zeros(spill_got.shape[1:], f32)

        at = 0
        for grad, body_, tail in zip(grads, bodies, tails):
            width = grad.shape[1]
            last = tail[j]
            last = jnp.concatenate([last[:HALO], last[HALO:] + spill_got[j, :, at : at + width]], axis=0)
            grad[: tokens - 2 * HALO] = body_[j, : tokens - 2 * HALO]
            grad[tokens - 2 * HALO :] = last.astype(bf16)
            at += width

    @pl.when(step == 2 * steps)
    def _():
        blocks = tokens // CH
        weights = (iota(0) >= iota(1)).astype(bf16)
        for n in range(blocks):
            dbeta = jnp.concatenate([row_grads[j, n, :heads] for j in range(steps)], axis=0)
            dc = jnp.concatenate([row_grads[j, n, heads:] for j in range(steps)], axis=0)
            beta = betas[n]
            beta_grad[:, tile(n)] = (dbeta * beta * (1.0 - beta)).astype(bf16)
            gate_grad[:, tile(n)] = (summed(dc, weights) * factors[n]).astype(bf16)
        for i in range(2):
            logits(i).wait_send()

        @pl.when(has_next)
        def _():
            ids_copy.wait_send()

        for j in range(steps):
            swap(j).wait_send()
            pair(j).wait_send()
            for i in range(4):
                exchanged(i, j).wait_send()

            @pl.when(has_peer)
            def _():
                hop(j).wait_send()

            @pl.when(has_next)
            def _():
                for i in range(3):
                    neighbour(i, j).wait_send()

            @pl.when(has_prev)
            def _():
                spilled(j).wait_send()


def join_kernel(m, a, g, a_in, g_in, a_out, g_out):
    for e in range(m.shape[0]):
        here = m[e]
        a_out[e] = a[e] + mm(here, a_in[e])
        g_out[e] = g[e] + mm(here.T, g_in[e])


def norm_back(dy, a, scale):
    sig = sigmoid(a)
    u = a * sig
    inverse = 1.0 / jnp.sqrt(rowsum(u * u) + GUARD)
    y = u * inverse
    dy = dy * scale
    du = (dy - y * rowsum(y * dy)) * inverse
    return du * (sig + u * (1.0 - sig))


def main_kernel(
    a_q, a_k, a_v, qn, kn, seq_grad, inv, kk_in, qk_in, pdo_in, q_taps, k_taps, v_taps, masks, docs, rows,
    s_in, d_in, out, q_grad, k_grad, v_grad, q_end, k_end, v_end, q_spill, k_spill, v_spill, row_grads,
):
    tokens = a_q.shape[0]
    blocks = tokens // CH
    heads = a_v.shape[1] // CH
    row, col = iota(0), iota(1)
    va = a_v[...]
    v_sig = sigmoid(va)
    v_all = va * v_sig
    info = []
    for n in range(blocks):
        q = qn[n * CH : (n + 1) * CH, :]
        k = kn[n * CH : (n + 1) * CH, :]
        info.append((q, k, q.T, k.T, rows[0, n], columns(rows[0, n])))
    fwd = {}
    carried = [s_in[e] for e in range(heads)]
    for n in range(blocks):
        q, k, q_t, k_t, flat, cols = info[n]
        kq = jnp.concatenate([k, q], axis=0)
        for e in range(heads):
            beta, c, s, w = [cols[:, 4 * e + i : 4 * e + i + 1] for i in range(4)]
            beta_r, c_r, s_r, w_r = [flat[4 * e + i : 4 * e + i + 1, :] for i in range(4)]
            s_last = s_r[:, CH - 1 :]
            v = v_all[n * CH : (n + 1) * CH, e * CH : (e + 1) * CH]
            decay = jnp.exp(jnp.minimum(c - c_r, 0.0)) * docs[n]
            p = decay * qk_in[0, n]
            st = carried[e]
            kqs = mm(kq, st)
            ks, qs = kqs[:CH], kqs[CH:]
            t = inv[0, e, n]
            u = mm(t, beta * (v - s * ks))
            o = s * qs + mm(p, u)
            out[n * CH : (n + 1) * CH, e * CH : (e + 1) * CH] = o.astype(bf16)
            if n + 1 < blocks:
                carried[e] = s_last * st + mm(k_t * w_r, u)
            fwd[n, e] = (st, u, qs, decay, p, v)
    grads = [d_in[e] for e in range(heads)]
    dqs, dks, dvs = [None] * blocks, [None] * blocks, {}
    for n in reversed(range(blocks)):
        q, k, q_t, k_t, flat, cols = info[n]
        packed = jnp.zeros((CH, CH), f32)
        dqk_sum = dkk_sum = dq = dk = 0.0
        for e in range(heads):
            beta, c, s, w = [cols[:, 4 * e + i : 4 * e + i + 1] for i in range(4)]
            beta_r, c_r, s_r, w_r = [flat[4 * e + i : 4 * e + i + 1, :] for i in range(4)]
            s_last = s_r[:, CH - 1 :]
            st, u, qs, decay, p, v = fwd[n, e]
            ds_out = grads[e]
            do_half = seq_grad[n * CH : (n + 1) * CH, e * CH : (e + 1) * CH]
            do = do_half.astype(f32)
            du = pdo_in[0, e, n] + mm(k * w, ds_out)
            y = mm(inv[0, e, n].T, du)
            do_y = jnp.concatenate([do, y], axis=0)
            by_u = mm_nt(do_y, u)
            by_s = mm_nt(do_y, st)
            dp, dl = by_u[:CH], -by_u[CH:]
            dos, z = by_s[:CH], -by_s[CH:]
            dkw = mm_nt(u, ds_out)
            strict = jnp.where(row > col, decay, 0.0)
            bk = strict * kk_in[0, n]
            dlb = dl * bk
            f = dp * p + beta * dlb
            zk = z * k
            wk = w * (dkw * k)
            bs = beta * s
            dbeta = rowsum(y * v + s * zk + dlb)
            extra = jnp.sum(rowsum(wk + s_last * (ds_out * st)), axis=0, keepdims=True)
            dc = rowsum((f - f.T) + s * (do * qs) + bs * zk - wk)
            dc = dc + jnp.where(row[:, :1] == CH - 1, extra, 0.0)
            packed = jnp.where(col == 2 * e, dbeta, packed)
            packed = jnp.where(col == 2 * e + 1, dc, packed)
            dqk_sum = dqk_sum + dp * decay
            dkk_sum = dkk_sum + dl * (beta * strict)
            dq = dq + s * dos
            dk = dk + w * dkw + bs * z
            dvs[n, e] = beta * y
            if n > 0:
                grads[e] = mm_half(q_t * s_r, do_half) + s_last * ds_out - mm(k_t * (beta_r * s_r), y)
        dqs[n] = dq + mm(dqk_sum, k)
        dks[n] = dk + mm(dqk_sum.T, q) + mm(dkk_sum + dkk_sum.T, k)
        row_grads[0, n] = packed.T[: row_grads.shape[2]]
    dq = jnp.concatenate(dqs, axis=0)
    dk = jnp.concatenate(dks, axis=0)
    dv = jnp.concatenate(
        [jnp.concatenate([dvs[n, e] for e in range(heads)], axis=1) for n in range(blocks)], axis=0
    )
    daq = norm_back(dq, a_q[...], SCALE)
    dak = norm_back(dk, a_k[...], 1.0)
    dav = dv * (v_sig + v_all * (1.0 - v_sig))
    for da, taps, grad, end, spill in (
        (daq, q_taps, q_grad, q_end, q_spill),
        (dak, k_taps, k_grad, k_end, k_spill),
        (dav, v_taps, v_grad, v_end, v_spill),
    ):
        full = conv_back(da, taps, masks)
        grad[...] = full[:tokens].astype(bf16)
        end[...] = full[tokens - HALO : tokens]
        spill[...] = full[tokens:]


def shifted(array, by):
    peers = lax.axis_size(SEQ)
    return lax.ppermute(array, SEQ, [(i, i + by) for i in range(peers) if 0 <= i + by < peers])


def tri(upper):
    i = jnp.arange(CH)
    return ((i[:, None] <= i[None, :]) if upper else (i[:, None] >= i[None, :])).astype(f32)


def sds(shape, dtype=f32):
    return jax.ShapeDtypeStruct(shape, dtype)


def staged_call(inputs, hk, hv, tokens, hops):
    blocks = tokens // CH
    rep = hv // hk
    qw = hk * DK
    vw = rep * DK
    col = lambda rows_, width, off=0: pl.BlockSpec((rows_, width), lambda i, off=off, width=width: (0, off // width + i))
    fixed = lambda shape: pl.BlockSpec(shape, lambda i: (0,) * len(shape))
    per = lambda shape: pl.BlockSpec(shape, lambda i: (i,) + (0,) * (len(shape) - 1))
    taps_specs = [col(TAPS, DK), col(TAPS, DK), col(TAPS, vw)]
    common_specs = taps_specs + [
        fixed((TAPS - 1, tokens, CH)),
        fixed((blocks, CH, CH)),
        per((1, blocks, rep * 4, CH)),
    ]
    params = pltpu.CompilerParams(dimension_semantics=("arbitrary",), vmem_limit_bytes=48 * 2**20)
    saved_specs = [
        col(tokens, DK), col(tokens, DK), col(tokens, vw), col(tokens, DK), col(tokens, DK), col(tokens, vw),
        per((1, rep, blocks, CH, CH)), per((1, blocks, CH, CH)), per((1, blocks, CH, CH)),
        per((1, rep, blocks, CH, CH)),
    ]
    saved_shapes = [
        sds((tokens, qw)), sds((tokens, qw)), sds((tokens, hv * DK)), sds((tokens, qw)), sds((tokens, qw)),
        sds((tokens, hv * DK), bf16), sds((hk, rep, blocks, CH, CH)), sds((hk, blocks, CH, CH)),
        sds((hk, blocks, CH, CH)), sds((hk, rep, blocks, CH, CH)),
    ]
    state_spec = per((rep, DK, DK))
    state_shape = sds((hv, DK, DK))
    units = hv * blocks * 2 * 4 * CH**3
    *taps, masks, docs, rows = inputs[12:]
    in_specs = [
        pl.BlockSpec(memory_space=pltpu.SMEM),
        col(tokens, DK), col(tokens, DK), col(tokens, vw), col(tokens, vw),
        col(SWAP, DK), col(SWAP, DK, qw), col(SWAP, vw, 2 * qw), col(SWAP, vw, 2 * qw + hv * DK),
        col(HALO, DK), col(HALO, DK, qw), col(HALO, vw, 2 * qw),
    ] + common_specs
    prepare_cost = pl.CostEstimate(flops=22 * units, bytes_accessed=24 * 2**20, transcendentals=2**20)
    prepared = pl.pallas_call(
        prepare_kernel,
        grid=(hk,),
        in_specs=in_specs,
        out_specs=saved_specs + [state_spec] * 3,
        out_shape=saved_shapes + [state_shape] * 3,
        compiler_params=params,
        cost_estimate=prepare_cost,
        name="prepare",
    )(*inputs)
    saved, (m, a, g) = prepared[:10], prepared[10:]
    join = pl.pallas_call(
        join_kernel,
        grid=(hk,),
        in_specs=[state_spec] * 5,
        out_specs=[state_spec] * 2,
        out_shape=[state_shape] * 2,
        compiler_params=params,
        cost_estimate=pl.CostEstimate(flops=hv * 16 * CH**3, bytes_accessed=7 * 2**20, transcendentals=0),
        name="join",
    )
    s_in, d_in = a, g
    for step in range(hops):
        s_in, d_in = shifted(s_in, 1), shifted(d_in, -1)
        if step < hops - 1:
            s_in, d_in = join(m, a, g, s_in, d_in)

    ends = [col(HALO, DK), col(HALO, DK), col(HALO, vw)]
    end_shapes = [sds((HALO, qw)), sds((HALO, qw)), sds((HALO, hv * DK))]
    return pl.pallas_call(
        main_kernel,
        grid=(hk,),
        in_specs=saved_specs + common_specs + [state_spec] * 2,
        out_specs=[col(tokens, vw), col(tokens, DK), col(tokens, DK), col(tokens, vw)] + ends + ends + [per((1, blocks, 8, CH))],
        out_shape=[
            sds((tokens, hv * DK), bf16), sds((tokens, qw), bf16), sds((tokens, qw), bf16), sds((tokens, hv * DK), bf16)
        ] + end_shapes + end_shapes + [sds((hk, blocks, 8, CH))],
        compiler_params=params,
        cost_estimate=pl.CostEstimate(flops=17 * units, bytes_accessed=24 * 2**20, transcendentals=2**20),
        name="main",
    )(*saved, *taps, masks, docs, rows, s_in, d_in)


def fused_call(
    q_raw, k_raw, v_raw, beta_logit, gate_logit, out_grad, conv_q, conv_k, conv_v, a_log, dt_bias, doc_ids, swap_blocks
):
    tokens, qw = q_raw.shape
    blocks = tokens // CH
    hk = qw // DK
    hv = v_raw.shape[1] // DK
    steps = hk // GROUP
    heads = hv // steps
    gw, vw = GROUP * DK, heads * DK
    doc_ids = doc_ids.reshape(blocks, CH)
    early = lambda i: jnp.minimum(i, steps - 1)
    late = lambda i: jnp.clip(i - steps, 0, steps - 1)
    last = lambda i: jnp.clip(i - steps - 1, 0, steps - 1)
    both = lambda i: jnp.where(i < steps, i, late(i))
    col = lambda when, count, width: pl.BlockSpec((count, width), lambda i: (0, when(i)))
    fixed = lambda shape: pl.BlockSpec(shape, lambda i: (0,) * len(shape))
    smem = pl.BlockSpec(memory_space=pltpu.SMEM)
    hbm = pl.BlockSpec(memory_space=pl.ANY)
    in_specs = [smem] * 3 + [fixed((hv, tokens)), fixed((hv, tokens)), fixed((blocks, CH))]
    in_specs += [col(early, tokens, gw), col(early, tokens, gw), col(early, tokens, vw), col(early, tokens, vw)]
    in_specs += [col(both, TAPS, gw), col(both, TAPS, gw), col(both, TAPS, vw)] + [hbm] * 7
    vm = lambda *shape: pltpu.VMEM(shape, f32)
    half = lambda *shape: pltpu.VMEM(shape, bf16)
    square = lambda *lead: vm(steps, *lead, CH, CH)
    wide = lambda width: vm(steps, tokens, width)
    units = blocks * heads
    sems = lambda *shape: pltpu.SemaphoreType.DMA(shape)
    scratch = [half(steps, SWAP, gw), half(steps, SWAP, gw), half(steps, SWAP, vw), half(steps, SWAP, vw)]
    scratch += [half(steps, 2 * HALO, gw), half(steps, 2 * HALO, gw), half(steps, 2 * HALO, vw)]
    scratch += [half(hv, SWAP), half(hv, SWAP), pltpu.VMEM((blocks, CH), jnp.int32)]
    scratch += [vm(TAPS - 1, tokens, CH), vm(blocks, CH, CH), vm(steps, blocks, KINDS * heads, CH)]
    scratch += [vm(blocks, hv, CH), vm(blocks, hv, CH)]
    scratch += [wide(gw), wide(gw), wide(vw), wide(vw), wide(gw), wide(gw), half(steps, tokens, vw)]
    scratch += [square(units)] * 5 + [square(blocks * GROUP)] * 2 + [square(heads, 4)] * 2 + [square(heads)] * 7
    scratch += [half(steps, tokens, gw), half(steps, tokens, gw), half(steps, tokens, vw)]
    scratch += [vm(steps, 2 * HALO, gw), vm(steps, 2 * HALO, gw), vm(steps, 2 * HALO, vw)]
    scratch += [vm(steps, HALO, 2 * gw + vw)] * 2 + [vm(steps, blocks, 2 * heads, CH)]
    scratch += [sems(steps)] * 8 + [sems(4, steps)] * 2 + [sems(3, steps)] * 2 + [sems(3)] * 2
    return pl.pallas_call(
        functools.partial(fused_kernel, lax.axis_size("ctx"), steps),
        grid=(2 * steps + 1,),
        in_specs=in_specs,
        out_specs=[col(late, tokens, vw), col(last, tokens, gw), col(last, tokens, gw), col(last, tokens, vw)]
        + [fixed((hv, tokens))] * 2,
        out_shape=[
            sds((tokens, hv * DK), bf16), sds((tokens, qw), bf16), sds((tokens, qw), bf16), sds((tokens, hv * DK), bf16),
            sds((hv, tokens), bf16), sds((hv, tokens), bf16),
        ],
        scratch_shapes=scratch,
        compiler_params=pltpu.CompilerParams(
            dimension_semantics=("arbitrary",), vmem_limit_bytes=56 * 2**20, collective_id=0, has_side_effects=True
        ),
        cost_estimate=pl.CostEstimate(
            flops=30 * hv * blocks * 8 * CH**3, bytes_accessed=8 * 2**20, transcendentals=2**21
        ),
        name="fused",
    )(
        swap_blocks, a_log, dt_bias, beta_logit, gate_logit, doc_ids, q_raw, k_raw, v_raw, out_grad, conv_q, conv_k, conv_v,
        q_raw, k_raw, v_raw, out_grad, beta_logit, gate_logit, doc_ids,
    )


def body(
    q_raw, k_raw, v_raw, beta_logit, gate_logit, out_grad, conv_q, conv_k, conv_v, a_log, dt_bias, doc_ids, swap_blocks
):
    tokens = q_raw.shape[0]
    blocks = tokens // CH
    hk = q_raw.shape[1] // DK
    hv = v_raw.shape[1] // DK
    rep = hv // hk
    shards = lax.axis_size(SEQ)
    hops = max(1, shards // DOC_PARTS)
    if hops == lax.axis_size("pair") and blocks == 2 and hk % GROUP == 0:
        return tuple(
            fused_call(
                q_raw, k_raw, v_raw, beta_logit, gate_logit, out_grad, conv_q, conv_k, conv_v, a_log, dt_bias, doc_ids,
                swap_blocks,
            )
        )
    core = lax.axis_index("pair")
    swap = swap_blocks[0]
    flags = jnp.stack([jnp.where(core == 1, swap, 0), jnp.where(core == 0, swap, 0)]).astype(jnp.int32)

    start = jnp.where(core == 0, SWAP, 0)
    logits = jnp.concatenate([beta_logit, gate_logit], axis=0)
    bg_send = lax.dynamic_slice_in_dim(logits, start, SWAP, 1)
    send = jnp.concatenate(
        [lax.dynamic_slice_in_dim(x, start, SWAP, 0) for x in (q_raw, k_raw, v_raw, out_grad)], axis=1
    )
    got = lax.ppermute(send, "pair", [(0, 1), (1, 0)])
    send, bg_send, tail_ids, tails = lax.optimization_barrier(
        (send, bg_send, doc_ids[tokens - HALO :], [x[tokens - HALO :] for x in (q_raw, k_raw, v_raw)])
    )
    bg_got = lax.ppermute(bg_send, "pair", [(0, 1), (1, 0)])
    ids_col = jnp.broadcast_to((tail_ids + 1).astype(bf16)[:, None], (HALO, CH))
    tail = jnp.concatenate(tails + [ids_col], axis=1)
    before = shifted(tail, 1)
    own = jnp.concatenate([x[SWAP - HALO : SWAP] for x in (q_raw, k_raw, v_raw)], axis=1)
    chans = own.shape[1]
    halo = jnp.where(flags[0] > 0, own, before[:, :chans]).astype(f32)
    qw = hk * DK

    first = jnp.where(flags[0] > 0, bg_got, logits[:, :SWAP])
    second = jnp.where(flags[1] > 0, bg_got, logits[:, SWAP:])
    logits = jnp.concatenate([first, second], axis=1).astype(f32)
    beta = jax.nn.sigmoid(logits[:hv])
    gate = logits[hv:] + dt_bias[:, None]
    rate = -jnp.exp(a_log)[:, None]
    decay_log = rate * jax.nn.softplus(gate)
    c = jnp.dot(decay_log.reshape(hv * blocks, CH), tri(True), precision=highest).reshape(hv, blocks, CH)
    ids = doc_ids.astype(f32) + 1.0
    ext_ids = jnp.concatenate([before[:, chans].astype(f32), ids])
    doc = ids.reshape(blocks, CH)
    doc_before = ext_ids[HALO - 1 : HALO - 1 + tokens : CH]
    s = jnp.where(doc == doc_before[:, None], jnp.exp(c), 0.0)
    w = jnp.where(doc == doc[:, CH - 1 :], jnp.exp(jnp.minimum(c[:, :, CH - 1 :] - c, 0.0)), 0.0)
    rows = jnp.stack([beta.reshape(hv, blocks, CH), c, s, w], axis=2)
    rows = rows.reshape(hk, rep, blocks, 4, CH).transpose(0, 2, 1, 3, 4).reshape(hk, blocks, rep * 4, CH)
    docs = ((doc[:, :, None] == doc[:, None, :]) & (tri(False) > 0)[None]).astype(f32)
    masks = jnp.stack(
        [
            jnp.broadcast_to((ext_ids[HALO - d : HALO - d + tokens] == ids).astype(f32)[:, None], (tokens, CH))
            for d in range(1, TAPS)
        ]
    )
    taps = [x.astype(f32) for x in (conv_q, conv_k, conv_v)]

    results = staged_call(
        (flags, q_raw, k_raw, v_raw, out_grad, got, got, got, got, halo, halo, halo, *taps, masks, docs, rows), hk, hv,
        tokens, hops,
    )
    layer_out, q_grad, k_grad, v_grad = results[:4]
    spilled = shifted(jnp.concatenate(results[7:10], axis=1), -1)
    ends_out = []
    at = 0
    for grad, end in zip((q_grad, k_grad, v_grad), results[4:7]):
        width = end.shape[1]
        last = (end + spilled[:, at : at + width]).astype(bf16)
        ends_out.append(lax.dynamic_update_slice(grad, last, (tokens - HALO, 0)))
        at += width
    rg = results[10][:, :, : 2 * rep].reshape(hk, blocks, rep, 2, CH).transpose(3, 0, 2, 1, 4)
    dbeta = rg[0].reshape(hv, tokens)
    dg = jnp.dot(rg[1].reshape(hv * blocks, CH), tri(False), precision=highest).reshape(hv, tokens)
    beta_grad = dbeta * beta * (1.0 - beta)
    gate_grad = dg * rate * jax.nn.sigmoid(gate)
    return (layer_out, ends_out[0], ends_out[1], ends_out[2], beta_grad.astype(bf16), gate_grad.astype(bf16))


def solution(mesh):
    rows = P(("groups", "ctx", "pair"), "head")
    rates = P("head", ("groups", "ctx", "pair"))
    taps = P(None, "head")
    return jax.shard_map(
        body,
        mesh=mesh,
        in_specs=(
            rows, rows, rows, rates, rates, rows, taps, taps, taps, P("head"), P("head"),
            P(("groups", "ctx", "pair")), P(("groups", "ctx")),
        ),
        out_specs=(rows, rows, rows, rows, rates, rates),
        check_vma=False,
    )
```

```python
import functools
import math

import jax
import jax.numpy as jnp
from jax import lax
from jax.experimental import pallas as pl
from jax.experimental.pallas import tpu as pltpu
from jax.sharding import PartitionSpec as P

DK = 128
TAPS = 4
CH = 128
SWAP = 128
HALO = 8
GUARD = 1e-06
SCALE = 1.0 / math.sqrt(DK)
DOC_PARTS = 4
GROUP = 2
BASE = 16
KINDS = 5
COPY_BYTES = 2**18

f32 = jnp.float32
bf16 = jnp.bfloat16
highest = lax.Precision.HIGHEST
SEQ = ("ctx", "pair")


def split(x):
    high = x.astype(bf16)
    return high, (x - high.astype(f32)).astype(bf16)


def mm(a, b):
    ah, al = split(a)
    bh, bl = split(b)
    lhs = jnp.concatenate([ah, al], axis=1)
    rhs = jnp.concatenate(
        [jnp.concatenate([bh, bl], axis=1), jnp.concatenate([bh, jnp.zeros_like(bh)], axis=1)], axis=0
    )
    r = lax.dot_general(lhs, rhs, (((1,), (0,)), ((), ())), preferred_element_type=f32)
    n = b.shape[1]
    return r[:, :n] + r[:, n:]


def mm_half(a, b):
    return lax.dot_general(
        jnp.concatenate(split(a), axis=1), jnp.concatenate([b, b], axis=0), (((1,), (0,)), ((), ())),
        preferred_element_type=f32,
    )


def odd_blocks(x, size):
    return jnp.concatenate([x[i : i + size] for i in range(size, CH, 2 * size)], axis=0)


def with_odd(even, odd, size):
    parts = []
    for i in range(0, CH // 2, size):
        parts.append(jnp.zeros((size, CH), odd.dtype) if even is None else even[2 * i : 2 * i + size])
        parts.append(odd[i : i + size])
    return jnp.concatenate(parts, axis=0)


def mm_nt(a, b):
    ah, al = split(a)
    bh, bl = split(b)
    lhs = jnp.concatenate([ah, al], axis=1)
    rhs = jnp.concatenate(
        [jnp.concatenate([bh, bh], axis=1), jnp.concatenate([bl, jnp.zeros_like(bl)], axis=1)], axis=0
    )
    r = lax.dot_general(lhs, rhs, (((1,), (1,)), ((), ())), preferred_element_type=f32)
    n = b.shape[0]
    return r[:, :n] + r[:, n:]


def mm_nt_split(lhs, b):
    bh, bl = split(b)
    rhs = jnp.concatenate(
        [jnp.concatenate([bh, bh], axis=1), jnp.concatenate([bl, jnp.zeros_like(bl)], axis=1)], axis=0
    )
    r = lax.dot_general(lhs, rhs, (((1,), (1,)), ((), ())), preferred_element_type=f32)
    n = b.shape[0]
    return r[:, :n] + r[:, n:]


def iota(axis):
    return lax.broadcasted_iota(jnp.int32, (CH, CH), axis)


def rowsum(x):
    return jnp.sum(x, axis=1, keepdims=True)


def columns(rows):
    return jnp.concatenate([rows, jnp.zeros((CH - rows.shape[0], CH), f32)], axis=0).T


def sigmoid(a):
    return 1.0 / (1.0 + jnp.exp(-a))


def fetch(raw, recv, flags):
    first = raw[:SWAP, :]
    second = raw[SWAP:, :]
    got = recv[...]
    first = jnp.where(flags[0] > 0, got, first)
    second = jnp.where(flags[1] > 0, got, second)
    return jnp.concatenate([first, second], axis=0)


def conv(x, halo, taps, masks):
    ext = jnp.concatenate([halo, x], axis=0)
    width = x.shape[1] // CH
    total = taps[TAPS - 1 : TAPS, :] * x
    for d in range(1, TAPS):
        moved = pltpu.roll(ext, d, 0)[HALO:, :]
        mask = masks[d - 1]
        if width > 1:
            mask = jnp.concatenate([mask] * width, axis=1)
        total = total + taps[TAPS - 1 - d : TAPS - d, :] * (moved * mask)
    return total


def conv_back(da, taps, masks):
    width = da.shape[1] // CH
    zeros = jnp.zeros((HALO, da.shape[1]), f32)
    total = taps[TAPS - 1 : TAPS, :] * jnp.concatenate([da, zeros], axis=0)
    size = total.shape[0]
    for d in range(1, TAPS):
        mask = masks[d - 1]
        if width > 1:
            mask = jnp.concatenate([mask] * width, axis=1)
        ext = jnp.concatenate([da * mask, zeros], axis=0)
        total = total + taps[TAPS - 1 - d : TAPS - d, :] * pltpu.roll(ext, size - d, 0)
    return total


def local_maps(
    flags, q_raw, k_raw, v_raw, g_raw, q_got, k_got, v_got, g_got, q_halo, k_halo, v_halo,
    q_taps, k_taps, v_taps, masks, docs, rows,
    a_q, a_k, a_v, qn_out, kn_out, seq_grad, inv_out, kk_out, qk_out, pdo_out,
):
    blocks = q_raw.shape[0] // CH
    qa = conv(fetch(q_raw, q_got, flags).astype(f32), q_halo[...], q_taps, masks)
    ka = conv(fetch(k_raw, k_got, flags).astype(f32), k_halo[...], k_taps, masks)
    va = conv(fetch(v_raw, v_got, flags).astype(f32), v_halo[...], v_taps, masks)
    a_q[...] = qa
    a_k[...] = ka
    a_v[...] = va
    gs = fetch(g_raw, g_got, flags)
    seq_grad[...] = gs
    do_all = gs
    qu = qa * sigmoid(qa)
    ku = ka * sigmoid(ka)
    v_all = va * sigmoid(va)
    qn = qu * (SCALE / jnp.sqrt(rowsum(qu * qu) + GUARD))
    kn = ku * (1.0 / jnp.sqrt(rowsum(ku * ku) + GUARD))
    qn_out[...] = qn
    kn_out[...] = kn
    row, col = iota(0), iota(1)
    eye = (row == col).astype(f32)
    heads = v_raw.shape[1] // CH
    state = []
    for n in range(blocks):
        q = qn[n * CH : (n + 1) * CH]
        k = kn[n * CH : (n + 1) * CH]
        both = mm_nt(jnp.concatenate([k, q], axis=0), k)
        kk, qk = both[:CH], both[CH:]
        kk_out[0, n] = kk
        qk_out[0, n] = qk
        q_t, k_t = q.T, k.T
        flat = rows[0, n]
        cols = columns(flat)
        for e in range(heads):
            beta, c, s, w = [cols[:, 4 * e + i : 4 * e + i + 1] for i in range(4)]
            beta_r, c_r, s_r, w_r = [flat[4 * e + i : 4 * e + i + 1, :] for i in range(4)]
            s_last = s_r[:, CH - 1 :]
            decay = jnp.exp(jnp.minimum(c - c_r, 0.0)) * docs[n]
            low = jnp.where(row > col, beta * decay * kk, 0.0)
            do = do_all[n * CH : (n + 1) * CH, e * CH : (e + 1) * CH]
            v = v_all[n * CH : (n + 1) * CH, e * CH : (e + 1) * CH]
            state.append((n, e, low, decay * qk, do, v, k * w, (beta_r * s_r) * k_t, beta * s * k, s_r * q_t, beta * v, s_last))
    inv = []
    for item in state:
        inv.append(eye - jnp.where((row >> 1) == (col >> 1), item[2], 0.0))
    size = 1
    while (2 << size) <= CH:
        near = ((row >> (size + 1)) == (col >> (size + 1))) & ((row >> size) != (col >> size))
        width = 1 << size
        if width < 8:
            half = [mm(jnp.where(near, item[2], 0.0), t) for item, t in zip(state, inv)]
            inv = [t - mm(t, h) for t, h in zip(inv, half)]
        else:
            half = [mm(odd_blocks(jnp.where(near, item[2], 0.0), width), t) for item, t in zip(state, inv)]
            odds = [odd_blocks(t, width) for t in inv]
            odds = [t - mm(t, with_odd(None, h, width)) for t, h in zip(odds, half)]
            inv = [with_odd(t, o, width) for t, o in zip(inv, odds)]
        size += 1
    maps = {}
    for item, t in zip(state, inv):
        n, e, low, p, do, v, kw, bsk_t, bsk, sq_t, bv, s_last = item
        inv_out[0, e, n] = t
        pdo = mm_half(p.T, do)
        pdo_out[0, e, n] = pdo
        t_t = t.T
        b = mm(t_t, kw)
        cc = mm(t_t, pdo)
        b_t = b.T
        m = s_last * eye - mm(b_t, bsk)
        a = mm(b_t, bv)
        g = mm_half(sq_t, do) - mm(bsk_t, cc)
        maps[n, e] = (m, a, g)
    results = []
    for e in range(heads):
        m, a, g = maps[0, e]
        for n in range(1, blocks):
            m2, a2, g2 = maps[n, e]
            g = g + mm(m.T, g2)
            a = mm(m2, a) + a2
            m = mm(m2, m)
        results.append((m, a, g))
    return results


def prepare_kernel(*refs):
    m_out, a_out, g_out = refs[-3:]
    for e, (m, a, g) in enumerate(local_maps(*refs[:-3])):
        m_out[e] = m
        a_out[e] = a
        g_out[e] = g


def inverse_blocks(lows, size, fillers):
    regs = size // 8
    lane = lax.broadcasted_iota(jnp.int32, (8, CH), 1)
    sub = lax.broadcasted_iota(jnp.int32, (8, CH), 0)
    base = lane - lax.rem(lane, size)
    packed, inv = [], []
    for low in lows:
        rows_, eyes = [], []
        for r in range(regs):
            acc = low[8 * r : 8 * r + 8]
            for at in range(size, CH, size):
                acc = jnp.where(lane >= at, low[at + 8 * r : at + 8 * r + 8], acc)
            rows_.append(acc)
            eyes.append((lane - base == sub + 8 * r).astype(f32))
        packed.append(rows_)
        inv.append(eyes)
    fillers = list(fillers)
    every = max(1, (size - 1) // max(1, len(fillers)))
    for j in range(size - 1):
        here = j // 8
        index = base + j
        for low, t in zip(packed, inv):
            line = jnp.broadcast_to(t[here][j % 8 : j % 8 + 1], (8, CH))
            for r in range(here if j % 8 < 7 else here + 1, regs):
                t[r] = t[r] - jnp.take_along_axis(low[r], index, axis=1, mode="promise_in_bounds") * line
        if fillers and j % every == 0:
            fillers.pop(0)()
    for filler in fillers:
        filler()
    return [
        jnp.concatenate([jnp.where(base == at, x, 0.0) for at in range(0, CH, size) for x in t], axis=0) for t in inv
    ]


def head_scalars(cols, flat, e, heads):
    return (
        [cols[:, i * heads + e : i * heads + e + 1] for i in range(KINDS)],
        [flat[i * heads + e : i * heads + e + 1, :] for i in range(KINDS)],
    )


def part(x, n, h):
    return x[n * CH : (n + 1) * CH, h * CH : (h + 1) * CH]


def tile(h):
    return slice(h * CH, (h + 1) * CH)


def summed(x, weights):
    high = x.astype(bf16)
    rest = x - high.astype(f32)
    middle = rest.astype(bf16)
    low = (rest - middle.astype(f32)).astype(bf16)
    n = x.shape[0]
    r = lax.dot_general(
        jnp.concatenate([high, middle, low], axis=0), weights, (((1,), (0,)), ((), ())), preferred_element_type=f32
    )
    return r[:n] + r[n : 2 * n] + r[2 * n :]


def per_head(ref, count):
    row = lax.broadcasted_iota(jnp.int32, (count, CH), 0)
    total = jnp.zeros((count, CH), f32)
    for h in range(count):
        total = jnp.where(row == h, ref[h], total)
    return total


def setup_phase(
    has_prev, swaps, a_log, dt_bias, beta_logit, gate_logit, doc_ids, beta_got, gate_got, ids_got,
    masks, docs, rows, betas, factors,
):
    blocks = doc_ids.shape[0]
    steps = rows.shape[0]
    hv = beta_logit.shape[0]
    heads = hv // steps
    row, col = iota(0), iota(1)
    before = jnp.where(has_prev, ids_got[blocks - 1 :].astype(f32) + 1.0, 0.0)
    ids = jnp.concatenate(
        [before, doc_ids[...].astype(f32) + 1.0, jnp.zeros((8 - 1 - blocks, CH), f32)], axis=0
    )
    lane = lax.broadcasted_iota(jnp.int32, (8, CH), 1)
    same = []
    for d in range(1, TAPS):
        moved = pltpu.roll(ids, d, 1)
        moved = jnp.where(lane < d, pltpu.roll(moved, 1, 0), moved)
        same.append((moved == ids).astype(f32))
    rate = -jnp.exp(per_head(a_log, hv))
    bias = per_head(dt_bias, hv)
    logs = []
    for n in range(blocks):
        cols = columns(jnp.concatenate([x[n + 1 : n + 2] for x in same] + [ids[n + 1 : n + 2]], axis=0))
        for d in range(TAPS - 1):
            masks[d, n * CH : (n + 1) * CH] = jnp.broadcast_to(cols[:, d : d + 1], (CH, CH))
        here = (cols[:, TAPS - 1 : TAPS] == ids[n + 1 : n + 2]) & (row >= col)
        docs[n] = jnp.where(here, 1.0, 0.0)
        beta = jnp.where(swaps[n] > 0, beta_got[...], beta_logit[:, tile(n)]).astype(f32)
        gate = jnp.where(swaps[n] > 0, gate_got[...], gate_logit[:, tile(n)]).astype(f32) + bias
        betas[n] = sigmoid(beta)
        factors[n] = rate * sigmoid(gate)
        logs.append(rate * (jnp.maximum(gate, 0.0) + jnp.log1p(jnp.exp(-jnp.abs(gate)))))
    sums = summed(jnp.concatenate(logs, axis=0), (row <= col).astype(bf16))
    for n in range(blocks):
        doc = ids[n + 1 : n + 2]
        c = sums[n * hv : (n + 1) * hv]
        s = jnp.where(doc == ids[n : n + 1, CH - 1 :], jnp.exp(c), 0.0)
        w = jnp.where(doc == doc[:, CH - 1 :], jnp.exp(jnp.minimum(c[:, CH - 1 :] - c, 0.0)), 0.0)
        beta = betas[n]
        for i, x in enumerate((beta, c, s, w, beta * s)):
            for j in range(steps):
                rows[j, n, i * heads : (i + 1) * heads] = x[j * heads : (j + 1) * heads]


def forward_phase(
    j, first, swaps, q_raw, k_raw, v_raw, g_raw, q_taps, k_taps, v_taps,
    q_got, k_got, v_got, g_got, q_halo, k_halo, v_halo, masks, docs, rows,
    q_scale, k_scale, v_scale, v_out, qn_out, kn_out, grad_out,
    inv_out, decay_out, ub_out, ws_out, pdo_out, kk_out, qk_out, maps, affs, w_buf,
):
    keys = q_raw.shape[1] // CH
    heads = v_raw.shape[1] // CH
    rep = heads // keys
    blocks = q_raw.shape[0] // CH
    mask = [masks[d] for d in range(TAPS - 1)]
    tail = 2 * HALO

    def fetched(raw, got, h):
        parts = [jnp.where(swaps[n] > 0, got[j, :, tile(h)], raw[n * CH : (n + 1) * CH, tile(h)]) for n in range(blocks)]
        return jnp.concatenate(parts, axis=0)

    def activate(raw, got, halo, taps, h):
        own = raw[SWAP - tail : SWAP, tile(h)]
        before = jnp.where(swaps[0] > 0, own, halo[j, :, tile(h)]).astype(f32)[HALO:]
        x = conv(fetched(raw, got, h).astype(f32), before, taps[:, tile(h)].astype(f32), mask)
        sig = sigmoid(x)
        u = x * sig
        return u, sig + u * (1.0 - sig)

    def unit(raw, got, halo, taps, h, scale, out, scale_out):
        u, slope = activate(raw, got, halo, taps, h)
        factor = scale / jnp.sqrt(rowsum(u * u) + GUARD)
        y = u * factor
        out[j, :, tile(h)] = y
        scale_out[j, :, tile(h)] = slope * factor
        return y

    kn = [unit(k_raw, k_got, k_halo, k_taps, h, 1.0, kn_out, k_scale) for h in range(keys)]
    qn = [unit(q_raw, q_got, q_halo, q_taps, h, SCALE, qn_out, q_scale) for h in range(keys)]
    row, col = iota(0), iota(1)
    eye = (row == col).astype(f32)
    units = []
    for n in range(blocks):
        flat = rows[j, n]
        cols = columns(flat)
        for h in range(keys):
            q, k = qn[h][n * CH : (n + 1) * CH], kn[h][n * CH : (n + 1) * CH]
            both = mm_nt(jnp.concatenate([k, q], axis=0), k)
            kk, qk = both[:CH], both[CH:]
            kk_out[j, n * keys + h] = kk
            qk_out[j, n * keys + h] = qk
            q_t, k_t = q.T, k.T
            for e in range(h * rep, (h + 1) * rep):
                (beta, c, s, w, bs), (beta_r, c_r, s_r, w_r, bs_r) = head_scalars(cols, flat, e, heads)
                decay = jnp.exp(jnp.minimum(c - c_r, 0.0)) * docs[n]
                decay_out[j, n * heads + e] = decay
                low = jnp.where(row > col, beta * decay * kk, 0.0)
                units.append((n, e, low, decay * qk, beta, bs * k, k_t * w_r, s_r * q_t, s_r[:, CH - 1 :]))
    values, by_do = {}, {}

    def value(e):
        u, slope = activate(v_raw, v_got, v_halo, v_taps, e)
        v_out[j, :, tile(e)] = u
        v_scale[j, :, tile(e)] = slope
        values[e] = u

    def output(u):
        n, e, p, sq_t = u[0], u[1], u[3], u[7]
        do = jnp.where(swaps[n] > 0, g_got[j, :, tile(e)], g_raw[n * CH : (n + 1) * CH, tile(e)])
        grad_out[j, n * CH : (n + 1) * CH, tile(e)] = do
        by_do[n, e] = mm_half(jnp.concatenate([p.T, sq_t], axis=0), do)
        pdo_out[j, n * heads + e] = by_do[n, e][:CH]

    fillers = [functools.partial(output, u) for u in units] + [functools.partial(value, e) for e in range(heads)]
    inv = inverse_blocks([u[2] for u in units], BASE, fillers)
    size = BASE.bit_length() - 1
    while (1 << size) < CH:
        near = ((row >> (size + 1)) == (col >> (size + 1))) & ((row >> size) != (col >> size))
        width = 1 << size
        half = [mm(odd_blocks(jnp.where(near, u[2], 0.0), width), t) for u, t in zip(units, inv)]
        odds = [odd_blocks(t, width) for t in inv]
        odds = [t - mm(t, with_odd(None, h, width)) for t, h in zip(odds, half)]
        inv = [with_odd(t, o, width) for t, o in zip(inv, odds)]
        size += 1
    solved = []
    for (n, e, low, p, beta, bsk, kw_t, sq_t, s_last), t in zip(units, inv):
        inv_out[j, n * heads + e] = t
        ub = mm(t, beta * values[e][n * CH : (n + 1) * CH])
        ws = mm(t, bsk)
        ub_out[j, n * heads + e] = ub
        ws_out[j, n * heads + e] = ws
        solved.append((ub, ws))
    result = {}
    for (n, e, low, p, beta, bsk, kw_t, sq_t, s_last), (ub, ws) in zip(units, solved):
        a = mm(kw_t, ub)
        m = s_last * eye - mm(kw_t, ws)
        g = by_do[n, e][CH:] - mm(ws.T, by_do[n, e][:CH])
        result[n, e] = (m, m.T, a, g)
    for e in range(heads):
        m0, m0_t, a0, g0 = result[0, e]
        m1, m1_t, a1, g1 = result[1, e]
        for i, x in enumerate((m0, m1, m1_t, m0_t)):
            maps[j, e, i] = x
        for i, x in enumerate((a0, a1, g1, g0)):
            affs[j, e, i] = x
        w_buf[j, e] = jnp.where(first, a1, g0) + mm(jnp.where(first, m1, m0_t), jnp.where(first, a0, g1))


def backward_phase(
    j, first, other, q_taps, k_taps, v_taps, masks, rows,
    q_scale, k_scale, v_scale, v_all, qn, kn, seq_grad, inv, decays, ub_in, ws_in, pdo_in, kk_in, qk_in,
    maps, affs, y_buf, s_buf, z_got, out, q_body, k_body, v_body, q_tail, k_tail, v_tail, spill, row_grads,
):
    tokens = qn.shape[1]
    blocks = tokens // CH
    keys = qn.shape[2] // CH
    heads = v_all.shape[2] // CH
    rep = heads // keys
    row, col = iota(0), iota(1)
    states, leaving = [], []
    for e in range(heads):
        y, s1, z = y_buf[j, e], s_buf[j, e], z_got[j, e]
        t1 = affs[j, e, other] + mm(maps[j, e, other], z)
        states.append((jnp.where(first, y, z), jnp.where(first, s1, t1)))
        leaving.append((jnp.where(first, t1, s1), jnp.where(first, z, y)))
    info = []
    for n in range(blocks):
        flat = rows[j, n]
        info.append((flat, columns(flat)))
    order = [(n, e) for n in range(blocks) for e in range(heads)]
    work = {}

    def at(ref, n, h):
        return ref[j, n * CH : (n + 1) * CH, tile(h)]

    for n, e in order:
        flat, cols = info[n]
        (beta, c, s, w, bs), rs = head_scalars(cols, flat, e, heads)
        i = n * heads + e
        q, k = at(qn, n, e // rep), at(kn, n, e // rep)
        st, ds_out = states[e][n], leaving[e][n]
        by_st = mm(jnp.concatenate([ws_in[j, i], q], axis=0), st)
        u = ub_in[j, i] - by_st[:CH]
        du = pdo_in[j, i] + mm(k * w, ds_out)
        work[n, e] = (by_st[CH:], u, du)
    for n, e in order:
        flat, cols = info[n]
        (beta, c, s, w, bs), rs = head_scalars(cols, flat, e, heads)
        i = n * heads + e
        qs, u, du = work[n, e]
        o = s * qs + mm(decays[j, i] * qk_in[j, n * keys + e // rep], u)
        out[n * CH : (n + 1) * CH, tile(e)] = o.astype(bf16)
        work[n, e] = (qs, u, mm(inv[j, i].T, du))
    dqs, dks, dvs = {}, {}, {}
    none = jnp.zeros((CH, CH), bf16)
    for n in range(blocks):
        flat, cols = info[n]
        packed = jnp.zeros((CH, CH), f32)
        minus = []
        for h in range(keys):
            q, k = at(qn, n, h), at(kn, n, h)
            kk, qk = kk_in[j, n * keys + h], qk_in[j, n * keys + h]
            dqk_sum = dkk_sum = dq = dk = 0.0
            for e in range(h * rep, (h + 1) * rep):
                (beta, c, s, w, bs), rs = head_scalars(cols, flat, e, heads)
                s_last = rs[2][:, CH - 1 :]
                i = n * heads + e
                qs, u, y = work[n, e]
                st, ds_out = states[e][n], leaving[e][n]
                do_half = at(seq_grad, n, e)
                do = do_half.astype(f32)
                y_high, y_low = split(y)
                do_y = jnp.concatenate(
                    [jnp.concatenate([do_half, y_high], axis=0), jnp.concatenate([none, y_low], axis=0)], axis=1
                )
                by_u = mm_nt_split(do_y, u)
                by_s = mm_nt_split(do_y, st)
                dos, zneg = by_s[:CH], by_s[CH:]
                dkw = mm_nt(u, ds_out)
                decay = decays[j, i]
                dpd = by_u[:CH] * decay
                dls = by_u[CH:] * jnp.where(row > col, decay, 0.0)
                dlb = dls * kk
                f = dpd * qk - beta * dlb
                zk = zneg * k
                wk = w * (dkw * k)
                dbeta = rowsum(y * at(v_all, n, e) - s * zk - dlb)
                extra = jnp.sum(rowsum(wk + s_last * (ds_out * st)), axis=0, keepdims=True)
                dc = rowsum(f + s * (do * qs) - bs * zk - wk)
                dc = dc + jnp.where(row[:, :1] == CH - 1, extra, 0.0)
                packed = jnp.where(col == e, dbeta, packed)
                packed = jnp.where(col == heads + e, dc, packed)
                minus.append(jnp.sum(f, axis=0, keepdims=True))
                dqk_sum = dqk_sum + dpd
                dkk_sum = dkk_sum + beta * dls
                dq = dq + s * dos
                dk = dk + w * dkw - bs * zneg
                dvs[n, e] = beta * y
            by_k = mm(jnp.concatenate([dqk_sum, dkk_sum + dkk_sum.T], axis=0), k)
            dqs[n, h] = dq + by_k[:CH]
            dks[n, h] = dk + mm(dqk_sum.T, q) - by_k[CH:]
        row_grads[j, n] = packed.T[: 2 * heads] - jnp.concatenate([jnp.zeros((heads, CH), f32)] + minus, axis=0)
    mask = [masks[d] for d in range(TAPS - 1)]
    at_col = 0
    for grads, count, taps, body_out, tail_out, y_ref, scale_ref, gain in (
        (dqs, keys, q_taps, q_body, q_tail, qn, q_scale, DK),
        (dks, keys, k_taps, k_body, k_tail, kn, k_scale, 1),
        (dvs, heads, v_taps, v_body, v_tail, None, v_scale, 1),
    ):
        for h in range(count):
            da = jnp.concatenate([grads[n, h] for n in range(blocks)], axis=0)
            if y_ref is not None:
                y = y_ref[j, :, tile(h)]
                da = da - y * (rowsum(y * da) * float(gain))
            full = conv_back(da * scale_ref[j, :, tile(h)], taps[:, tile(h)].astype(f32), mask)
            body_out[j, :, tile(h)] = full[:tokens].astype(bf16)
            tail_out[j, :, tile(h)] = full[tokens - 2 * HALO : tokens]
            spill[j, :, at_col : at_col + CH] = full[tokens:]
            at_col += CH


def fused_kernel(ctxs, steps, *refs):
    swap_ref, a_log, dt_bias, beta_logit, gate_logit, doc_ids = refs[:6]
    raws, taps, sources, refs = refs[6:10], refs[10:13], refs[13:20], refs[20:]
    (out, *grads, beta_grad, gate_grad), refs = refs[:6], refs[6:]
    gots, halos, (beta_got, gate_got, ids_got), refs = refs[:4], refs[4:7], refs[7:10], refs[10:]
    (masks, docs, rows, betas, factors), refs = refs[:5], refs[5:]
    saved, refs = refs[:14], refs[14:]
    (maps, affs, w_buf, w_got, x_buf, y_buf, s_buf, z_buf, z_got), refs = refs[:9], refs[9:]
    bodies, tails, (spill, spill_got, row_grads), refs = refs[:3], refs[3:6], refs[6:9], refs[9:]
    swap_s, swap_r, hop_s, hop_r, pair_s, pair_r, spill_s, spill_r, got_s, got_r, halo_s, halo_r, few_s, few_r = refs
    step = pl.program_id(0)
    heads = w_buf.shape[1]
    tokens = raws[0].shape[0]
    core = lax.axis_index("pair")
    ctx = lax.axis_index("ctx")
    first = core == 0
    mine, other = 2 * core, 2 - 2 * core
    peer_ctx = jnp.where(first, ctx - 1, ctx + 1)
    has_peer = (peer_ctx >= 0) & (peer_ctx < ctxs)
    has_prev = jnp.logical_not(first) | has_peer
    has_next = first | has_peer
    partner = {"pair": 1 - core}
    peer = {"ctx": jnp.clip(peer_ctx, 0, ctxs - 1), "pair": 1 - core}
    following = {"ctx": jnp.clip(ctx + core, 0, ctxs - 1), "pair": 1 - core}
    previous = {"ctx": jnp.clip(ctx - 1 + core, 0, ctxs - 1), "pair": 1 - core}
    swap_flag = swap_ref[0]
    swaps = [jnp.where(first, 0, swap_flag), jnp.where(first, swap_flag, 0)]

    def remote(src, dst, send, recv, device):
        return pltpu.make_async_remote_copy(src, dst, send, recv, device_id=device, device_id_type=pl.DeviceIdType.MESH)

    def swap(j):
        return remote(w_buf.at[j], w_got.at[j], swap_s.at[j], swap_r.at[j], partner)

    def hop(j):
        return remote(x_buf.at[j], y_buf.at[j], hop_s.at[j], hop_r.at[j], peer)

    def pair(j):
        return remote(z_buf.at[j], z_got.at[j], pair_s.at[j], pair_r.at[j], partner)

    def spilled(j):
        return remote(spill.at[j], spill_got.at[j], spill_s.at[j], spill_r.at[j], previous)

    start = pl.multiple_of(jnp.where(first, SWAP, 0), SWAP)

    def exchanged(i, j):
        width = gots[i].shape[2]
        at = pl.multiple_of(j * width, CH)
        return remote(
            sources[i].at[pl.ds(start, SWAP), pl.ds(at, width)], gots[i].at[j], got_s.at[i, j], got_r.at[i, j], partner
        )

    def neighbour(i, j):
        width = halos[i].shape[2]
        at = pl.multiple_of(j * width, CH)
        return remote(
            sources[i].at[pl.ds(tokens - 2 * HALO, 2 * HALO), pl.ds(at, width)], halos[i].at[j], halo_s.at[i, j],
            halo_r.at[i, j], following,
        )

    def logits(i):
        return remote(sources[4 + i].at[:, pl.ds(start, SWAP)], (beta_got, gate_got)[i], few_s.at[i], few_r.at[i], partner)

    ids_copy = remote(sources[6], ids_got, few_s.at[2], few_r.at[2], following)

    def fetch_rows(j):
        for i in range(4):
            exchanged(i, j).start()

        @pl.when(has_next)
        def _():
            for i in range(3):
                neighbour(i, j).start()

    @pl.when(step == 0)
    def _():
        barrier = pltpu.get_barrier_semaphore()
        pl.semaphore_signal(barrier, inc=1, device_id=partner, device_id_type=pl.DeviceIdType.MESH)

        @pl.when(has_peer)
        def _():
            pl.semaphore_signal(barrier, inc=1, device_id=peer, device_id_type=pl.DeviceIdType.MESH)

        pl.semaphore_wait(barrier, jnp.where(has_peer, 2, 1))

        @pl.when(has_next)
        def _():
            ids_copy.start()

        for i in range(2):
            logits(i).start()
        fetch_rows(0)

        @pl.when(has_prev)
        def _():
            ids_copy.wait_recv()

        @pl.when(jnp.logical_not(has_prev))
        def _():
            ids_got[...] = jnp.zeros(ids_got.shape, jnp.int32)
            for halo in halos:
                halo[...] = jnp.zeros(halo.shape, bf16)

        for i in range(2):
            logits(i).wait_recv()
        setup_phase(
            has_prev, swaps, a_log, dt_bias, beta_logit, gate_logit, doc_ids, beta_got, gate_got, ids_got,
            masks, docs, rows, betas, factors,
        )

    def advance(j, at, got):
        mid = [affs[j, e, at] + mm(maps[j, e, at], got[j, e]) for e in range(heads)]
        return mid, [affs[j, e, at + 1] + mm(maps[j, e, at + 1], mid[e]) for e in range(heads)]

    def chains(over, back):
        if over:
            swap(step - 1).wait_recv()
        if back:
            @pl.when(has_peer)
            def _():
                hop(step - 2).wait_recv()

            @pl.when(jnp.logical_not(has_peer))
            def _():
                y_buf[step - 2] = jnp.zeros(y_buf.shape[1:], f32)

        if over:
            mid, end = advance(step - 1, other, w_got)
            for e in range(heads):
                x_buf[step - 1, e] = end[e]
        if back:
            mid, end = advance(step - 2, mine, y_buf)
            for e in range(heads):
                s_buf[step - 2, e] = mid[e]
                z_buf[step - 2, e] = end[e]
        if over:
            @pl.when(has_peer)
            def _():
                hop(step - 1).start()

        if back:
            pair(step - 2).start()

    @pl.when(step == 1)
    def _():
        chains(True, False)

    @pl.when((step >= 2) & (step <= steps))
    def _():
        chains(True, True)

    @pl.when(step == steps + 1)
    def _():
        chains(False, True)

    @pl.when(step < steps)
    def _():
        for i in range(4):
            exchanged(i, step).wait_recv()

        @pl.when(has_prev)
        def _():
            for i in range(3):
                neighbour(i, step).wait_recv()

        @pl.when(step < steps - 1)
        def _():
            fetch_rows(step + 1)

        forward_phase(step, first, swaps, *raws, *taps, *gots, *halos, masks, docs, rows, *saved, maps, affs, w_buf)
        swap(step).start()

    @pl.when((step >= steps) & (step < 2 * steps))
    def _():
        j = step - steps
        pair(j).wait_recv()
        backward_phase(
            j, first, other, *taps, masks, rows, *saved, maps, affs, y_buf, s_buf, z_got, out, *bodies, *tails, spill,
            row_grads,
        )

        @pl.when(has_prev)
        def _():
            spilled(j).start()

    @pl.when(step == 2 * steps)
    def _():
        blocks = tokens // CH
        weights = (iota(0) >= iota(1)).astype(bf16)
        for n in range(blocks):
            dbeta = jnp.concatenate([row_grads[j, n, :heads] for j in range(steps)], axis=0)
            dc = jnp.concatenate([row_grads[j, n, heads:] for j in range(steps)], axis=0)
            beta = betas[n]
            beta_grad[:, tile(n)] = (dbeta * beta * (1.0 - beta)).astype(bf16)
            gate_grad[:, tile(n)] = (summed(dc, weights) * factors[n]).astype(bf16)

    @pl.when(step > steps)
    def _():
        j = step - steps - 1

        @pl.when(has_next)
        def _():
            spilled(j).wait_recv()

        @pl.when(jnp.logical_not(has_next))
        def _():
            spill_got[j] = jnp.zeros(spill_got.shape[1:], f32)

        at = 0
        for grad, body_, tail in zip(grads, bodies, tails):
            width = grad.shape[1]
            last = tail[j]
            last = jnp.concatenate([last[:HALO], last[HALO:] + spill_got[j, :, at : at + width]], axis=0)
            grad[: tokens - 2 * HALO] = body_[j, : tokens - 2 * HALO]
            grad[tokens - 2 * HALO :] = last.astype(bf16)
            at += width

    @pl.when(step == 2 * steps)
    def _():
        for i in range(2):
            logits(i).wait_send()

        @pl.when(has_next)
        def _():
            ids_copy.wait_send()

        for j in range(steps):
            swap(j).wait_send()
            pair(j).wait_send()
            for i in range(4):
                exchanged(i, j).wait_send()

            @pl.when(has_peer)
            def _():
                hop(j).wait_send()

            @pl.when(has_next)
            def _():
                for i in range(3):
                    neighbour(i, j).wait_send()

            @pl.when(has_prev)
            def _():
                spilled(j).wait_send()


def join_kernel(m, a, g, a_in, g_in, a_out, g_out):
    for e in range(m.shape[0]):
        here = m[e]
        a_out[e] = a[e] + mm(here, a_in[e])
        g_out[e] = g[e] + mm(here.T, g_in[e])


def norm_back(dy, a, scale):
    sig = sigmoid(a)
    u = a * sig
    inverse = 1.0 / jnp.sqrt(rowsum(u * u) + GUARD)
    y = u * inverse
    dy = dy * scale
    du = (dy - y * rowsum(y * dy)) * inverse
    return du * (sig + u * (1.0 - sig))


def main_kernel(
    a_q, a_k, a_v, qn, kn, seq_grad, inv, kk_in, qk_in, pdo_in, q_taps, k_taps, v_taps, masks, docs, rows,
    s_in, d_in, out, q_grad, k_grad, v_grad, q_end, k_end, v_end, q_spill, k_spill, v_spill, row_grads,
):
    tokens = a_q.shape[0]
    blocks = tokens // CH
    heads = a_v.shape[1] // CH
    row, col = iota(0), iota(1)
    va = a_v[...]
    v_sig = sigmoid(va)
    v_all = va * v_sig
    info = []
    for n in range(blocks):
        q = qn[n * CH : (n + 1) * CH, :]
        k = kn[n * CH : (n + 1) * CH, :]
        info.append((q, k, q.T, k.T, rows[0, n], columns(rows[0, n])))
    fwd = {}
    carried = [s_in[e] for e in range(heads)]
    for n in range(blocks):
        q, k, q_t, k_t, flat, cols = info[n]
        kq = jnp.concatenate([k, q], axis=0)
        for e in range(heads):
            beta, c, s, w = [cols[:, 4 * e + i : 4 * e + i + 1] for i in range(4)]
            beta_r, c_r, s_r, w_r = [flat[4 * e + i : 4 * e + i + 1, :] for i in range(4)]
            s_last = s_r[:, CH - 1 :]
            v = v_all[n * CH : (n + 1) * CH, e * CH : (e + 1) * CH]
            decay = jnp.exp(jnp.minimum(c - c_r, 0.0)) * docs[n]
            p = decay * qk_in[0, n]
            st = carried[e]
            kqs = mm(kq, st)
            ks, qs = kqs[:CH], kqs[CH:]
            t = inv[0, e, n]
            u = mm(t, beta * (v - s * ks))
            o = s * qs + mm(p, u)
            out[n * CH : (n + 1) * CH, e * CH : (e + 1) * CH] = o.astype(bf16)
            if n + 1 < blocks:
                carried[e] = s_last * st + mm(k_t * w_r, u)
            fwd[n, e] = (st, u, qs, decay, p, v)
    grads = [d_in[e] for e in range(heads)]
    dqs, dks, dvs = [None] * blocks, [None] * blocks, {}
    for n in reversed(range(blocks)):
        q, k, q_t, k_t, flat, cols = info[n]
        packed = jnp.zeros((CH, CH), f32)
        dqk_sum = dkk_sum = dq = dk = 0.0
        for e in range(heads):
            beta, c, s, w = [cols[:, 4 * e + i : 4 * e + i + 1] for i in range(4)]
            beta_r, c_r, s_r, w_r = [flat[4 * e + i : 4 * e + i + 1, :] for i in range(4)]
            s_last = s_r[:, CH - 1 :]
            st, u, qs, decay, p, v = fwd[n, e]
            ds_out = grads[e]
            do_half = seq_grad[n * CH : (n + 1) * CH, e * CH : (e + 1) * CH]
            do = do_half.astype(f32)
            du = pdo_in[0, e, n] + mm(k * w, ds_out)
            y = mm(inv[0, e, n].T, du)
            do_y = jnp.concatenate([do, y], axis=0)
            by_u = mm_nt(do_y, u)
            by_s = mm_nt(do_y, st)
            dp, dl = by_u[:CH], -by_u[CH:]
            dos, z = by_s[:CH], -by_s[CH:]
            dkw = mm_nt(u, ds_out)
            strict = jnp.where(row > col, decay, 0.0)
            bk = strict * kk_in[0, n]
            dlb = dl * bk
            f = dp * p + beta * dlb
            zk = z * k
            wk = w * (dkw * k)
            bs = beta * s
            dbeta = rowsum(y * v + s * zk + dlb)
            extra = jnp.sum(rowsum(wk + s_last * (ds_out * st)), axis=0, keepdims=True)
            dc = rowsum((f - f.T) + s * (do * qs) + bs * zk - wk)
            dc = dc + jnp.where(row[:, :1] == CH - 1, extra, 0.0)
            packed = jnp.where(col == 2 * e, dbeta, packed)
            packed = jnp.where(col == 2 * e + 1, dc, packed)
            dqk_sum = dqk_sum + dp * decay
            dkk_sum = dkk_sum + dl * (beta * strict)
            dq = dq + s * dos
            dk = dk + w * dkw + bs * z
            dvs[n, e] = beta * y
            if n > 0:
                grads[e] = mm_half(q_t * s_r, do_half) + s_last * ds_out - mm(k_t * (beta_r * s_r), y)
        dqs[n] = dq + mm(dqk_sum, k)
        dks[n] = dk + mm(dqk_sum.T, q) + mm(dkk_sum + dkk_sum.T, k)
        row_grads[0, n] = packed.T[: row_grads.shape[2]]
    dq = jnp.concatenate(dqs, axis=0)
    dk = jnp.concatenate(dks, axis=0)
    dv = jnp.concatenate(
        [jnp.concatenate([dvs[n, e] for e in range(heads)], axis=1) for n in range(blocks)], axis=0
    )
    daq = norm_back(dq, a_q[...], SCALE)
    dak = norm_back(dk, a_k[...], 1.0)
    dav = dv * (v_sig + v_all * (1.0 - v_sig))
    for da, taps, grad, end, spill in (
        (daq, q_taps, q_grad, q_end, q_spill),
        (dak, k_taps, k_grad, k_end, k_spill),
        (dav, v_taps, v_grad, v_end, v_spill),
    ):
        full = conv_back(da, taps, masks)
        grad[...] = full[:tokens].astype(bf16)
        end[...] = full[tokens - HALO : tokens]
        spill[...] = full[tokens:]


def shifted(array, by):
    peers = lax.axis_size(SEQ)
    return lax.ppermute(array, SEQ, [(i, i + by) for i in range(peers) if 0 <= i + by < peers])


def tri(upper):
    i = jnp.arange(CH)
    return ((i[:, None] <= i[None, :]) if upper else (i[:, None] >= i[None, :])).astype(f32)


def sds(shape, dtype=f32):
    return jax.ShapeDtypeStruct(shape, dtype)


def staged_call(inputs, hk, hv, tokens, hops):
    blocks = tokens // CH
    rep = hv // hk
    qw = hk * DK
    vw = rep * DK
    col = lambda rows_, width, off=0: pl.BlockSpec((rows_, width), lambda i, off=off, width=width: (0, off // width + i))
    fixed = lambda shape: pl.BlockSpec(shape, lambda i: (0,) * len(shape))
    per = lambda shape: pl.BlockSpec(shape, lambda i: (i,) + (0,) * (len(shape) - 1))
    taps_specs = [col(TAPS, DK), col(TAPS, DK), col(TAPS, vw)]
    common_specs = taps_specs + [
        fixed((TAPS - 1, tokens, CH)),
        fixed((blocks, CH, CH)),
        per((1, blocks, rep * 4, CH)),
    ]
    params = pltpu.CompilerParams(dimension_semantics=("arbitrary",), vmem_limit_bytes=48 * 2**20)
    saved_specs = [
        col(tokens, DK), col(tokens, DK), col(tokens, vw), col(tokens, DK), col(tokens, DK), col(tokens, vw),
        per((1, rep, blocks, CH, CH)), per((1, blocks, CH, CH)), per((1, blocks, CH, CH)),
        per((1, rep, blocks, CH, CH)),
    ]
    saved_shapes = [
        sds((tokens, qw)), sds((tokens, qw)), sds((tokens, hv * DK)), sds((tokens, qw)), sds((tokens, qw)),
        sds((tokens, hv * DK), bf16), sds((hk, rep, blocks, CH, CH)), sds((hk, blocks, CH, CH)),
        sds((hk, blocks, CH, CH)), sds((hk, rep, blocks, CH, CH)),
    ]
    state_spec = per((rep, DK, DK))
    state_shape = sds((hv, DK, DK))
    units = hv * blocks * 2 * 4 * CH**3
    *taps, masks, docs, rows = inputs[12:]
    in_specs = [
        pl.BlockSpec(memory_space=pltpu.SMEM),
        col(tokens, DK), col(tokens, DK), col(tokens, vw), col(tokens, vw),
        col(SWAP, DK), col(SWAP, DK, qw), col(SWAP, vw, 2 * qw), col(SWAP, vw, 2 * qw + hv * DK),
        col(HALO, DK), col(HALO, DK, qw), col(HALO, vw, 2 * qw),
    ] + common_specs
    prepare_cost = pl.CostEstimate(flops=22 * units, bytes_accessed=24 * 2**20, transcendentals=2**20)
    prepared = pl.pallas_call(
        prepare_kernel,
        grid=(hk,),
        in_specs=in_specs,
        out_specs=saved_specs + [state_spec] * 3,
        out_shape=saved_shapes + [state_shape] * 3,
        compiler_params=params,
        cost_estimate=prepare_cost,
        name="prepare",
    )(*inputs)
    saved, (m, a, g) = prepared[:10], prepared[10:]
    join = pl.pallas_call(
        join_kernel,
        grid=(hk,),
        in_specs=[state_spec] * 5,
        out_specs=[state_spec] * 2,
        out_shape=[state_shape] * 2,
        compiler_params=params,
        cost_estimate=pl.CostEstimate(flops=hv * 16 * CH**3, bytes_accessed=7 * 2**20, transcendentals=0),
        name="join",
    )
    s_in, d_in = a, g
    for step in range(hops):
        s_in, d_in = shifted(s_in, 1), shifted(d_in, -1)
        if step < hops - 1:
            s_in, d_in = join(m, a, g, s_in, d_in)

    ends = [col(HALO, DK), col(HALO, DK), col(HALO, vw)]
    end_shapes = [sds((HALO, qw)), sds((HALO, qw)), sds((HALO, hv * DK))]
    return pl.pallas_call(
        main_kernel,
        grid=(hk,),
        in_specs=saved_specs + common_specs + [state_spec] * 2,
        out_specs=[col(tokens, vw), col(tokens, DK), col(tokens, DK), col(tokens, vw)] + ends + ends + [per((1, blocks, 8, CH))],
        out_shape=[
            sds((tokens, hv * DK), bf16), sds((tokens, qw), bf16), sds((tokens, qw), bf16), sds((tokens, hv * DK), bf16)
        ] + end_shapes + end_shapes + [sds((hk, blocks, 8, CH))],
        compiler_params=params,
        cost_estimate=pl.CostEstimate(flops=17 * units, bytes_accessed=24 * 2**20, transcendentals=2**20),
        name="main",
    )(*saved, *taps, masks, docs, rows, s_in, d_in)


def copy_kernel(*refs):
    count = (len(refs) - 1) // 2
    sems = refs[-1]
    copies = []
    for src, dst in zip(refs[:count], refs[count : 2 * count]):
        size = max(16, min(src.shape[0], COPY_BYTES // (2 * src.shape[1])))
        for at in range(0, src.shape[0], size):
            rows = pl.ds(at, size)
            copies.append(pltpu.make_async_copy(src.at[rows], dst.at[rows], sems.at[len(copies)]))
    for copy in copies:
        copy.start()
    for copy in copies:
        copy.wait()


def copied(arrays):
    hbm = pl.BlockSpec(memory_space=pl.ANY)
    return pl.pallas_call(
        copy_kernel,
        in_specs=[hbm] * len(arrays),
        out_specs=[hbm] * len(arrays),
        out_shape=[sds(x.shape, x.dtype) for x in arrays],
        scratch_shapes=[pltpu.SemaphoreType.DMA((64,))],
        name="copies",
    )(*arrays)


def fused_call(
    q_raw, k_raw, v_raw, beta_logit, gate_logit, out_grad, conv_q, conv_k, conv_v, a_log, dt_bias, doc_ids, swap_blocks
):
    tokens, qw = q_raw.shape
    blocks = tokens // CH
    hk = qw // DK
    hv = v_raw.shape[1] // DK
    steps = hk // GROUP
    heads = hv // steps
    gw, vw = GROUP * DK, heads * DK
    doc_ids = doc_ids.reshape(blocks, CH)
    early = lambda i: jnp.minimum(i, steps - 1)
    late = lambda i: jnp.clip(i - steps, 0, steps - 1)
    last = lambda i: jnp.clip(i - steps - 1, 0, steps - 1)
    both = lambda i: jnp.where(i < steps, i, late(i))
    col = lambda when, count, width: pl.BlockSpec((count, width), lambda i: (0, when(i)))
    fixed = lambda shape: pl.BlockSpec(shape, lambda i: (0,) * len(shape))
    smem = pl.BlockSpec(memory_space=pltpu.SMEM)
    hbm = pl.BlockSpec(memory_space=pl.ANY)
    in_specs = [smem] * 3 + [fixed((hv, tokens)), fixed((hv, tokens)), fixed((blocks, CH))]
    in_specs += [col(early, tokens, gw), col(early, tokens, gw), col(early, tokens, vw), col(early, tokens, vw)]
    in_specs += [col(both, TAPS, gw), col(both, TAPS, gw), col(both, TAPS, vw)] + [hbm] * 7
    vm = lambda *shape: pltpu.VMEM(shape, f32)
    half = lambda *shape: pltpu.VMEM(shape, bf16)
    square = lambda *lead: vm(steps, *lead, CH, CH)
    wide = lambda width: vm(steps, tokens, width)
    units = blocks * heads
    sems = lambda *shape: pltpu.SemaphoreType.DMA(shape)
    scratch = [half(steps, SWAP, gw), half(steps, SWAP, gw), half(steps, SWAP, vw), half(steps, SWAP, vw)]
    scratch += [half(steps, 2 * HALO, gw), half(steps, 2 * HALO, gw), half(steps, 2 * HALO, vw)]
    scratch += [half(hv, SWAP), half(hv, SWAP), pltpu.VMEM((blocks, CH), jnp.int32)]
    scratch += [vm(TAPS - 1, tokens, CH), vm(blocks, CH, CH), vm(steps, blocks, KINDS * heads, CH)]
    scratch += [vm(blocks, hv, CH), vm(blocks, hv, CH)]
    scratch += [wide(gw), wide(gw), wide(vw), wide(vw), wide(gw), wide(gw), half(steps, tokens, vw)]
    scratch += [square(units)] * 5 + [square(blocks * GROUP)] * 2 + [square(heads, 4)] * 2 + [square(heads)] * 7
    scratch += [half(steps, tokens, gw), half(steps, tokens, gw), half(steps, tokens, vw)]
    scratch += [vm(steps, 2 * HALO, gw), vm(steps, 2 * HALO, gw), vm(steps, 2 * HALO, vw)]
    scratch += [vm(steps, HALO, 2 * gw + vw)] * 2 + [vm(steps, blocks, 2 * heads, CH)]
    scratch += [sems(steps)] * 8 + [sems(4, steps)] * 2 + [sems(3, steps)] * 2 + [sems(3)] * 2
    return pl.pallas_call(
        functools.partial(fused_kernel, lax.axis_size("ctx"), steps),
        grid=(2 * steps + 1,),
        in_specs=in_specs,
        out_specs=[col(late, tokens, vw), col(last, tokens, gw), col(last, tokens, gw), col(last, tokens, vw)]
        + [fixed((hv, tokens))] * 2,
        out_shape=[
            sds((tokens, hv * DK), bf16), sds((tokens, qw), bf16), sds((tokens, qw), bf16), sds((tokens, hv * DK), bf16),
            sds((hv, tokens), bf16), sds((hv, tokens), bf16),
        ],
        scratch_shapes=scratch,
        compiler_params=pltpu.CompilerParams(
            dimension_semantics=("arbitrary",), vmem_limit_bytes=56 * 2**20, collective_id=0, has_side_effects=True
        ),
        cost_estimate=pl.CostEstimate(
            flops=30 * hv * blocks * 8 * CH**3, bytes_accessed=8 * 2**20, transcendentals=2**21
        ),
        name="fused",
    )(
        swap_blocks, a_log, dt_bias, beta_logit, gate_logit, doc_ids, q_raw, k_raw, v_raw, out_grad, conv_q, conv_k, conv_v,
        q_raw, k_raw, v_raw, out_grad, beta_logit, gate_logit, doc_ids,
    )


def body(
    q_raw, k_raw, v_raw, beta_logit, gate_logit, out_grad, conv_q, conv_k, conv_v, a_log, dt_bias, doc_ids, swap_blocks
):
    tokens = q_raw.shape[0]
    blocks = tokens // CH
    hk = q_raw.shape[1] // DK
    hv = v_raw.shape[1] // DK
    rep = hv // hk
    shards = lax.axis_size(SEQ)
    hops = max(1, shards // DOC_PARTS)
    if hops == lax.axis_size("pair") and blocks == 2 and hk % GROUP == 0:
        return copied(
            fused_call(
                q_raw, k_raw, v_raw, beta_logit, gate_logit, out_grad, conv_q, conv_k, conv_v, a_log, dt_bias, doc_ids,
                swap_blocks,
            )
        )
    core = lax.axis_index("pair")
    swap = swap_blocks[0]
    flags = jnp.stack([jnp.where(core == 1, swap, 0), jnp.where(core == 0, swap, 0)]).astype(jnp.int32)

    start = jnp.where(core == 0, SWAP, 0)
    logits = jnp.concatenate([beta_logit, gate_logit], axis=0)
    bg_send = lax.dynamic_slice_in_dim(logits, start, SWAP, 1)
    send = jnp.concatenate(
        [lax.dynamic_slice_in_dim(x, start, SWAP, 0) for x in (q_raw, k_raw, v_raw, out_grad)], axis=1
    )
    got = lax.ppermute(send, "pair", [(0, 1), (1, 0)])
    send, bg_send, tail_ids, tails = lax.optimization_barrier(
        (send, bg_send, doc_ids[tokens - HALO :], [x[tokens - HALO :] for x in (q_raw, k_raw, v_raw)])
    )
    bg_got = lax.ppermute(bg_send, "pair", [(0, 1), (1, 0)])
    ids_col = jnp.broadcast_to((tail_ids + 1).astype(bf16)[:, None], (HALO, CH))
    tail = jnp.concatenate(tails + [ids_col], axis=1)
    before = shifted(tail, 1)
    own = jnp.concatenate([x[SWAP - HALO : SWAP] for x in (q_raw, k_raw, v_raw)], axis=1)
    chans = own.shape[1]
    halo = jnp.where(flags[0] > 0, own, before[:, :chans]).astype(f32)
    qw = hk * DK

    first = jnp.where(flags[0] > 0, bg_got, logits[:, :SWAP])
    second = jnp.where(flags[1] > 0, bg_got, logits[:, SWAP:])
    logits = jnp.concatenate([first, second], axis=1).astype(f32)
    beta = jax.nn.sigmoid(logits[:hv])
    gate = logits[hv:] + dt_bias[:, None]
    rate = -jnp.exp(a_log)[:, None]
    decay_log = rate * jax.nn.softplus(gate)
    c = jnp.dot(decay_log.reshape(hv * blocks, CH), tri(True), precision=highest).reshape(hv, blocks, CH)
    ids = doc_ids.astype(f32) + 1.0
    ext_ids = jnp.concatenate([before[:, chans].astype(f32), ids])
    doc = ids.reshape(blocks, CH)
    doc_before = ext_ids[HALO - 1 : HALO - 1 + tokens : CH]
    s = jnp.where(doc == doc_before[:, None], jnp.exp(c), 0.0)
    w = jnp.where(doc == doc[:, CH - 1 :], jnp.exp(jnp.minimum(c[:, :, CH - 1 :] - c, 0.0)), 0.0)
    rows = jnp.stack([beta.reshape(hv, blocks, CH), c, s, w], axis=2)
    rows = rows.reshape(hk, rep, blocks, 4, CH).transpose(0, 2, 1, 3, 4).reshape(hk, blocks, rep * 4, CH)
    docs = ((doc[:, :, None] == doc[:, None, :]) & (tri(False) > 0)[None]).astype(f32)
    masks = jnp.stack(
        [
            jnp.broadcast_to((ext_ids[HALO - d : HALO - d + tokens] == ids).astype(f32)[:, None], (tokens, CH))
            for d in range(1, TAPS)
        ]
    )
    taps = [x.astype(f32) for x in (conv_q, conv_k, conv_v)]

    results = staged_call(
        (flags, q_raw, k_raw, v_raw, out_grad, got, got, got, got, halo, halo, halo, *taps, masks, docs, rows), hk, hv,
        tokens, hops,
    )
    layer_out, q_grad, k_grad, v_grad = results[:4]
    spilled = shifted(jnp.concatenate(results[7:10], axis=1), -1)
    ends_out = []
    at = 0
    for grad, end in zip((q_grad, k_grad, v_grad), results[4:7]):
        width = end.shape[1]
        last = (end + spilled[:, at : at + width]).astype(bf16)
        ends_out.append(lax.dynamic_update_slice(grad, last, (tokens - HALO, 0)))
        at += width
    rg = results[10][:, :, : 2 * rep].reshape(hk, blocks, rep, 2, CH).transpose(3, 0, 2, 1, 4)
    dbeta = rg[0].reshape(hv, tokens)
    dg = jnp.dot(rg[1].reshape(hv * blocks, CH), tri(False), precision=highest).reshape(hv, tokens)
    beta_grad = dbeta * beta * (1.0 - beta)
    gate_grad = dg * rate * jax.nn.sigmoid(gate)
    return (layer_out, ends_out[0], ends_out[1], ends_out[2], beta_grad.astype(bf16), gate_grad.astype(bf16))


def solution(mesh):
    rows = P(("groups", "ctx", "pair"), "head")
    rates = P("head", ("groups", "ctx", "pair"))
    taps = P(None, "head")
    return jax.shard_map(
        body,
        mesh=mesh,
        in_specs=(
            rows, rows, rows, rates, rates, rows, taps, taps, taps, P("head"), P("head"),
            P(("groups", "ctx", "pair")), P(("groups", "ctx")),
        ),
        out_specs=(rows, rows, rows, rows, rates, rates),
        check_vma=False,
    )
```

```python
import functools
import math

import jax
import jax.numpy as jnp
from jax import lax
from jax.experimental import pallas as pl
from jax.experimental.pallas import tpu as pltpu
from jax.sharding import PartitionSpec as P

DK = 128
TAPS = 4
CH = 128
SWAP = 128
HALO = 8
GUARD = 1e-06
SCALE = 1.0 / math.sqrt(DK)
DOC_PARTS = 4
GROUP = 2
BASE = 16
KINDS = 5
COPY_BYTES = 2**18

f32 = jnp.float32
bf16 = jnp.bfloat16
highest = lax.Precision.HIGHEST
SEQ = ("ctx", "pair")


def split(x):
    high = x.astype(bf16)
    return high, (x - high.astype(f32)).astype(bf16)


def mm(a, b):
    ah, al = split(a)
    bh, bl = split(b)
    lhs = jnp.concatenate([ah, al], axis=1)
    rhs = jnp.concatenate(
        [jnp.concatenate([bh, bl], axis=1), jnp.concatenate([bh, jnp.zeros_like(bh)], axis=1)], axis=0
    )
    r = lax.dot_general(lhs, rhs, (((1,), (0,)), ((), ())), preferred_element_type=f32)
    n = b.shape[1]
    return r[:, :n] + r[:, n:]


def mm_half(a, b):
    return lax.dot_general(
        jnp.concatenate(split(a), axis=1), jnp.concatenate([b, b], axis=0), (((1,), (0,)), ((), ())),
        preferred_element_type=f32,
    )


def odd_blocks(x, size):
    return jnp.concatenate([x[i : i + size] for i in range(size, CH, 2 * size)], axis=0)


def with_odd(even, odd, size):
    parts = []
    for i in range(0, CH // 2, size):
        parts.append(jnp.zeros((size, CH), odd.dtype) if even is None else even[2 * i : 2 * i + size])
        parts.append(odd[i : i + size])
    return jnp.concatenate(parts, axis=0)


def mm_nt(a, b):
    ah, al = split(a)
    bh, bl = split(b)
    lhs = jnp.concatenate([ah, al], axis=1)
    rhs = jnp.concatenate(
        [jnp.concatenate([bh, bh], axis=1), jnp.concatenate([bl, jnp.zeros_like(bl)], axis=1)], axis=0
    )
    r = lax.dot_general(lhs, rhs, (((1,), (1,)), ((), ())), preferred_element_type=f32)
    n = b.shape[0]
    return r[:, :n] + r[:, n:]


def mm_nt_split(lhs, b):
    bh, bl = split(b)
    rhs = jnp.concatenate(
        [jnp.concatenate([bh, bh], axis=1), jnp.concatenate([bl, jnp.zeros_like(bl)], axis=1)], axis=0
    )
    r = lax.dot_general(lhs, rhs, (((1,), (1,)), ((), ())), preferred_element_type=f32)
    n = b.shape[0]
    return r[:, :n] + r[:, n:]


def iota(axis):
    return lax.broadcasted_iota(jnp.int32, (CH, CH), axis)


def rowsum(x):
    return jnp.sum(x, axis=1, keepdims=True)


def columns(rows):
    return jnp.concatenate([rows, jnp.zeros((CH - rows.shape[0], CH), f32)], axis=0).T


def sigmoid(a):
    return 1.0 / (1.0 + jnp.exp(-a))


def fetch(raw, recv, flags):
    first = raw[:SWAP, :]
    second = raw[SWAP:, :]
    got = recv[...]
    first = jnp.where(flags[0] > 0, got, first)
    second = jnp.where(flags[1] > 0, got, second)
    return jnp.concatenate([first, second], axis=0)


def conv(x, halo, taps, masks):
    ext = jnp.concatenate([halo, x], axis=0)
    width = x.shape[1] // CH
    total = taps[TAPS - 1 : TAPS, :] * x
    for d in range(1, TAPS):
        moved = pltpu.roll(ext, d, 0)[HALO:, :]
        mask = masks[d - 1]
        if width > 1:
            mask = jnp.concatenate([mask] * width, axis=1)
        total = total + taps[TAPS - 1 - d : TAPS - d, :] * (moved * mask)
    return total


def conv_back(da, taps, masks):
    width = da.shape[1] // CH
    zeros = jnp.zeros((HALO, da.shape[1]), f32)
    total = taps[TAPS - 1 : TAPS, :] * jnp.concatenate([da, zeros], axis=0)
    size = total.shape[0]
    for d in range(1, TAPS):
        mask = masks[d - 1]
        if width > 1:
            mask = jnp.concatenate([mask] * width, axis=1)
        ext = jnp.concatenate([da * mask, zeros], axis=0)
        total = total + taps[TAPS - 1 - d : TAPS - d, :] * pltpu.roll(ext, size - d, 0)
    return total


def local_maps(
    flags, q_raw, k_raw, v_raw, g_raw, q_got, k_got, v_got, g_got, q_halo, k_halo, v_halo,
    q_taps, k_taps, v_taps, masks, docs, rows,
    a_q, a_k, a_v, qn_out, kn_out, seq_grad, inv_out, kk_out, qk_out, pdo_out,
):
    blocks = q_raw.shape[0] // CH
    qa = conv(fetch(q_raw, q_got, flags).astype(f32), q_halo[...], q_taps, masks)
    ka = conv(fetch(k_raw, k_got, flags).astype(f32), k_halo[...], k_taps, masks)
    va = conv(fetch(v_raw, v_got, flags).astype(f32), v_halo[...], v_taps, masks)
    a_q[...] = qa
    a_k[...] = ka
    a_v[...] = va
    gs = fetch(g_raw, g_got, flags)
    seq_grad[...] = gs
    do_all = gs
    qu = qa * sigmoid(qa)
    ku = ka * sigmoid(ka)
    v_all = va * sigmoid(va)
    qn = qu * (SCALE / jnp.sqrt(rowsum(qu * qu) + GUARD))
    kn = ku * (1.0 / jnp.sqrt(rowsum(ku * ku) + GUARD))
    qn_out[...] = qn
    kn_out[...] = kn
    row, col = iota(0), iota(1)
    eye = (row == col).astype(f32)
    heads = v_raw.shape[1] // CH
    state = []
    for n in range(blocks):
        q = qn[n * CH : (n + 1) * CH]
        k = kn[n * CH : (n + 1) * CH]
        both = mm_nt(jnp.concatenate([k, q], axis=0), k)
        kk, qk = both[:CH], both[CH:]
        kk_out[0, n] = kk
        qk_out[0, n] = qk
        q_t, k_t = q.T, k.T
        flat = rows[0, n]
        cols = columns(flat)
        for e in range(heads):
            beta, c, s, w = [cols[:, 4 * e + i : 4 * e + i + 1] for i in range(4)]
            beta_r, c_r, s_r, w_r = [flat[4 * e + i : 4 * e + i + 1, :] for i in range(4)]
            s_last = s_r[:, CH - 1 :]
            decay = jnp.exp(jnp.minimum(c - c_r, 0.0)) * docs[n]
            low = jnp.where(row > col, beta * decay * kk, 0.0)
            do = do_all[n * CH : (n + 1) * CH, e * CH : (e + 1) * CH]
            v = v_all[n * CH : (n + 1) * CH, e * CH : (e + 1) * CH]
            state.append((n, e, low, decay * qk, do, v, k * w, (beta_r * s_r) * k_t, beta * s * k, s_r * q_t, beta * v, s_last))
    inv = []
    for item in state:
        inv.append(eye - jnp.where((row >> 1) == (col >> 1), item[2], 0.0))
    size = 1
    while (2 << size) <= CH:
        near = ((row >> (size + 1)) == (col >> (size + 1))) & ((row >> size) != (col >> size))
        width = 1 << size
        if width < 8:
            half = [mm(jnp.where(near, item[2], 0.0), t) for item, t in zip(state, inv)]
            inv = [t - mm(t, h) for t, h in zip(inv, half)]
        else:
            half = [mm(odd_blocks(jnp.where(near, item[2], 0.0), width), t) for item, t in zip(state, inv)]
            odds = [odd_blocks(t, width) for t in inv]
            odds = [t - mm(t, with_odd(None, h, width)) for t, h in zip(odds, half)]
            inv = [with_odd(t, o, width) for t, o in zip(inv, odds)]
        size += 1
    maps = {}
    for item, t in zip(state, inv):
        n, e, low, p, do, v, kw, bsk_t, bsk, sq_t, bv, s_last = item
        inv_out[0, e, n] = t
        pdo = mm_half(p.T, do)
        pdo_out[0, e, n] = pdo
        t_t = t.T
        b = mm(t_t, kw)
        cc = mm(t_t, pdo)
        b_t = b.T
        m = s_last * eye - mm(b_t, bsk)
        a = mm(b_t, bv)
        g = mm_half(sq_t, do) - mm(bsk_t, cc)
        maps[n, e] = (m, a, g)
    results = []
    for e in range(heads):
        m, a, g = maps[0, e]
        for n in range(1, blocks):
            m2, a2, g2 = maps[n, e]
            g = g + mm(m.T, g2)
            a = mm(m2, a) + a2
            m = mm(m2, m)
        results.append((m, a, g))
    return results


def prepare_kernel(*refs):
    m_out, a_out, g_out = refs[-3:]
    for e, (m, a, g) in enumerate(local_maps(*refs[:-3])):
        m_out[e] = m
        a_out[e] = a
        g_out[e] = g


def inverse_blocks(lows, size, fillers):
    regs = size // 8
    lane = lax.broadcasted_iota(jnp.int32, (8, CH), 1)
    sub = lax.broadcasted_iota(jnp.int32, (8, CH), 0)
    base = lane - lax.rem(lane, size)
    packed, inv = [], []
    for low in lows:
        rows_, eyes = [], []
        for r in range(regs):
            acc = low[8 * r : 8 * r + 8]
            for at in range(size, CH, size):
                acc = jnp.where(lane >= at, low[at + 8 * r : at + 8 * r + 8], acc)
            rows_.append(acc)
            eyes.append((lane - base == sub + 8 * r).astype(f32))
        packed.append(rows_)
        inv.append(eyes)
    fillers = list(fillers)
    every = max(1, (size - 1) // max(1, len(fillers)))
    for j in range(size - 1):
        here = j // 8
        index = base + j
        for low, t in zip(packed, inv):
            line = jnp.broadcast_to(t[here][j % 8 : j % 8 + 1], (8, CH))
            for r in range(here if j % 8 < 7 else here + 1, regs):
                t[r] = t[r] - jnp.take_along_axis(low[r], index, axis=1, mode="promise_in_bounds") * line
        if fillers and j % every == 0:
            fillers.pop(0)()
    for filler in fillers:
        filler()
    return [
        jnp.concatenate([jnp.where(base == at, x, 0.0) for at in range(0, CH, size) for x in t], axis=0) for t in inv
    ]


def head_scalars(cols, flat, e, heads):
    return (
        [cols[:, i * heads + e : i * heads + e + 1] for i in range(KINDS)],
        [flat[i * heads + e : i * heads + e + 1, :] for i in range(KINDS)],
    )


def part(x, n, h):
    return x[n * CH : (n + 1) * CH, h * CH : (h + 1) * CH]


def tile(h):
    return slice(h * CH, (h + 1) * CH)


def summed(x, weights):
    high = x.astype(bf16)
    rest = x - high.astype(f32)
    middle = rest.astype(bf16)
    low = (rest - middle.astype(f32)).astype(bf16)
    n = x.shape[0]
    r = lax.dot_general(
        jnp.concatenate([high, middle, low], axis=0), weights, (((1,), (0,)), ((), ())), preferred_element_type=f32
    )
    return r[:n] + r[n : 2 * n] + r[2 * n :]


def per_head(ref, count):
    row = lax.broadcasted_iota(jnp.int32, (count, CH), 0)
    total = jnp.zeros((count, CH), f32)
    for h in range(count):
        total = jnp.where(row == h, ref[h], total)
    return total


def setup_phase(
    has_prev, swaps, a_log, dt_bias, beta_logit, gate_logit, doc_ids, beta_got, gate_got, ids_got,
    masks, docs, rows, betas, factors,
):
    blocks = doc_ids.shape[0]
    steps = rows.shape[0]
    hv = beta_logit.shape[0]
    heads = hv // steps
    row, col = iota(0), iota(1)
    before = jnp.where(has_prev, ids_got[blocks - 1 :].astype(f32) + 1.0, 0.0)
    ids = jnp.concatenate(
        [before, doc_ids[...].astype(f32) + 1.0, jnp.zeros((8 - 1 - blocks, CH), f32)], axis=0
    )
    lane = lax.broadcasted_iota(jnp.int32, (8, CH), 1)
    same = []
    for d in range(1, TAPS):
        moved = pltpu.roll(ids, d, 1)
        moved = jnp.where(lane < d, pltpu.roll(moved, 1, 0), moved)
        same.append((moved == ids).astype(f32))
    rate = -jnp.exp(per_head(a_log, hv))
    bias = per_head(dt_bias, hv)
    logs = []
    for n in range(blocks):
        cols = columns(jnp.concatenate([x[n + 1 : n + 2] for x in same] + [ids[n + 1 : n + 2]], axis=0))
        for d in range(TAPS - 1):
            masks[d, n * CH : (n + 1) * CH] = jnp.broadcast_to(cols[:, d : d + 1], (CH, CH))
        here = (cols[:, TAPS - 1 : TAPS] == ids[n + 1 : n + 2]) & (row >= col)
        docs[n] = jnp.where(here, 1.0, 0.0)
        beta = jnp.where(swaps[n] > 0, beta_got[...], beta_logit[:, tile(n)]).astype(f32)
        gate = jnp.where(swaps[n] > 0, gate_got[...], gate_logit[:, tile(n)]).astype(f32) + bias
        betas[n] = sigmoid(beta)
        factors[n] = rate * sigmoid(gate)
        logs.append(rate * (jnp.maximum(gate, 0.0) + jnp.log1p(jnp.exp(-jnp.abs(gate)))))
    sums = summed(jnp.concatenate(logs, axis=0), (row <= col).astype(bf16))
    for n in range(blocks):
        doc = ids[n + 1 : n + 2]
        c = sums[n * hv : (n + 1) * hv]
        s = jnp.where(doc == ids[n : n + 1, CH - 1 :], jnp.exp(c), 0.0)
        w = jnp.where(doc == doc[:, CH - 1 :], jnp.exp(jnp.minimum(c[:, CH - 1 :] - c, 0.0)), 0.0)
        beta = betas[n]
        for i, x in enumerate((beta, c, s, w, beta * s)):
            for j in range(steps):
                rows[j, n, i * heads : (i + 1) * heads] = x[j * heads : (j + 1) * heads]


def forward_phase(
    j, first, swaps, q_raw, k_raw, v_raw, g_raw, q_taps, k_taps, v_taps,
    q_got, k_got, v_got, g_got, q_halo, k_halo, v_halo, masks, docs, rows,
    q_scale, k_scale, v_scale, v_out, qn_out, kn_out, grad_out,
    inv_out, decay_out, ub_out, ws_out, pdo_out, kk_out, qk_out, maps, affs, w_buf,
):
    keys = q_raw.shape[1] // CH
    heads = v_raw.shape[1] // CH
    rep = heads // keys
    blocks = q_raw.shape[0] // CH
    mask = [masks[d] for d in range(TAPS - 1)]
    tail = 2 * HALO

    def fetched(raw, got, h):
        parts = [jnp.where(swaps[n] > 0, got[j, :, tile(h)], raw[n * CH : (n + 1) * CH, tile(h)]) for n in range(blocks)]
        return jnp.concatenate(parts, axis=0)

    def activate(raw, got, halo, taps, h):
        own = raw[SWAP - tail : SWAP, tile(h)]
        before = jnp.where(swaps[0] > 0, own, halo[j, :, tile(h)]).astype(f32)[HALO:]
        x = conv(fetched(raw, got, h).astype(f32), before, taps[:, tile(h)], mask)
        sig = sigmoid(x)
        u = x * sig
        return u, sig + u * (1.0 - sig)

    def unit(raw, got, halo, taps, h, scale, out, scale_out):
        u, slope = activate(raw, got, halo, taps, h)
        factor = scale / jnp.sqrt(rowsum(u * u) + GUARD)
        y = u * factor
        out[j, :, tile(h)] = y
        scale_out[j, :, tile(h)] = slope * factor
        return y

    kn = [unit(k_raw, k_got, k_halo, k_taps, h, 1.0, kn_out, k_scale) for h in range(keys)]
    qn = [unit(q_raw, q_got, q_halo, q_taps, h, SCALE, qn_out, q_scale) for h in range(keys)]
    row, col = iota(0), iota(1)
    eye = (row == col).astype(f32)
    units = []
    for n in range(blocks):
        flat = rows[j, n]
        cols = columns(flat)
        for h in range(keys):
            q, k = qn[h][n * CH : (n + 1) * CH], kn[h][n * CH : (n + 1) * CH]
            both = mm_nt(jnp.concatenate([k, q], axis=0), k)
            kk, qk = both[:CH], both[CH:]
            kk_out[j, n * keys + h] = kk
            qk_out[j, n * keys + h] = qk
            q_t, k_t = q.T, k.T
            for e in range(h * rep, (h + 1) * rep):
                (beta, c, s, w, bs), (beta_r, c_r, s_r, w_r, bs_r) = head_scalars(cols, flat, e, heads)
                decay = jnp.exp(jnp.minimum(c - c_r, 0.0)) * docs[n]
                decay_out[j, n * heads + e] = decay
                low = jnp.where(row > col, beta * decay * kk, 0.0)
                units.append((n, e, low, decay * qk, beta, bs * k, k_t * w_r, s_r * q_t, s_r[:, CH - 1 :]))
    values, by_do = {}, {}

    def value(e):
        u, slope = activate(v_raw, v_got, v_halo, v_taps, e)
        v_out[j, :, tile(e)] = u
        v_scale[j, :, tile(e)] = slope
        values[e] = u

    def output(u):
        n, e, p, sq_t = u[0], u[1], u[3], u[7]
        do = jnp.where(swaps[n] > 0, g_got[j, :, tile(e)], g_raw[n * CH : (n + 1) * CH, tile(e)])
        grad_out[j, n * CH : (n + 1) * CH, tile(e)] = do
        by_do[n, e] = mm_half(jnp.concatenate([p.T, sq_t], axis=0), do)
        pdo_out[j, n * heads + e] = by_do[n, e][:CH]

    fillers = [functools.partial(output, u) for u in units] + [functools.partial(value, e) for e in range(heads)]
    inv = inverse_blocks([u[2] for u in units], BASE, fillers)
    size = BASE.bit_length() - 1
    while (1 << size) < CH:
        near = ((row >> (size + 1)) == (col >> (size + 1))) & ((row >> size) != (col >> size))
        width = 1 << size
        half = [mm(odd_blocks(jnp.where(near, u[2], 0.0), width), t) for u, t in zip(units, inv)]
        odds = [odd_blocks(t, width) for t in inv]
        odds = [t - mm(t, with_odd(None, h, width)) for t, h in zip(odds, half)]
        inv = [with_odd(t, o, width) for t, o in zip(inv, odds)]
        size += 1
    solved = []
    for (n, e, low, p, beta, bsk, kw_t, sq_t, s_last), t in zip(units, inv):
        inv_out[j, n * heads + e] = t
        ub = mm(t, beta * values[e][n * CH : (n + 1) * CH])
        ws = mm(t, bsk)
        ub_out[j, n * heads + e] = ub
        ws_out[j, n * heads + e] = ws
        solved.append((ub, ws))
    result = {}
    for (n, e, low, p, beta, bsk, kw_t, sq_t, s_last), (ub, ws) in zip(units, solved):
        a = mm(kw_t, ub)
        m = s_last * eye - mm(kw_t, ws)
        g = by_do[n, e][CH:] - mm(ws.T, by_do[n, e][:CH])
        result[n, e] = (m, m.T, a, g)
    for e in range(heads):
        m0, m0_t, a0, g0 = result[0, e]
        m1, m1_t, a1, g1 = result[1, e]
        for i, x in enumerate((m0, m1, m1_t, m0_t)):
            maps[j, e, i] = x
        for i, x in enumerate((a0, a1, g1, g0)):
            affs[j, e, i] = x
        w_buf[j, e] = jnp.where(first, a1, g0) + mm(jnp.where(first, m1, m0_t), jnp.where(first, a0, g1))


def backward_phase(
    j, first, other, q_taps, k_taps, v_taps, masks, rows,
    q_scale, k_scale, v_scale, v_all, qn, kn, seq_grad, inv, decays, ub_in, ws_in, pdo_in, kk_in, qk_in,
    maps, affs, y_buf, s_buf, z_got, out, q_body, k_body, v_body, q_tail, k_tail, v_tail, spill, row_grads,
):
    tokens = qn.shape[1]
    blocks = tokens // CH
    keys = qn.shape[2] // CH
    heads = v_all.shape[2] // CH
    rep = heads // keys
    row, col = iota(0), iota(1)
    states, leaving = [], []
    for e in range(heads):
        y, s1, z = y_buf[j, e], s_buf[j, e], z_got[j, e]
        t1 = affs[j, e, other] + mm(maps[j, e, other], z)
        states.append((jnp.where(first, y, z), jnp.where(first, s1, t1)))
        leaving.append((jnp.where(first, t1, s1), jnp.where(first, z, y)))
    info = []
    for n in range(blocks):
        flat = rows[j, n]
        info.append((flat, columns(flat)))
    order = [(n, e) for n in range(blocks) for e in range(heads)]
    work = {}

    def at(ref, n, h):
        return ref[j, n * CH : (n + 1) * CH, tile(h)]

    for n, e in order:
        flat, cols = info[n]
        (beta, c, s, w, bs), rs = head_scalars(cols, flat, e, heads)
        i = n * heads + e
        q, k = at(qn, n, e // rep), at(kn, n, e // rep)
        st, ds_out = states[e][n], leaving[e][n]
        by_st = mm(jnp.concatenate([ws_in[j, i], q], axis=0), st)
        u = ub_in[j, i] - by_st[:CH]
        du = pdo_in[j, i] + mm(k * w, ds_out)
        work[n, e] = (by_st[CH:], u, du)
    for n, e in order:
        flat, cols = info[n]
        (beta, c, s, w, bs), rs = head_scalars(cols, flat, e, heads)
        i = n * heads + e
        qs, u, du = work[n, e]
        o = s * qs + mm(decays[j, i] * qk_in[j, n * keys + e // rep], u)
        out[n * CH : (n + 1) * CH, tile(e)] = o.astype(bf16)
        work[n, e] = (qs, u, mm(inv[j, i].T, du))
    dqs, dks, dvs = {}, {}, {}
    none = jnp.zeros((CH, CH), bf16)
    for n in range(blocks):
        flat, cols = info[n]
        packed = jnp.zeros((CH, CH), f32)
        minus = []
        for h in range(keys):
            q, k = at(qn, n, h), at(kn, n, h)
            kk, qk = kk_in[j, n * keys + h], qk_in[j, n * keys + h]
            dqk_sum = dkk_sum = dq = dk = 0.0
            for e in range(h * rep, (h + 1) * rep):
                (beta, c, s, w, bs), rs = head_scalars(cols, flat, e, heads)
                s_last = rs[2][:, CH - 1 :]
                i = n * heads + e
                qs, u, y = work[n, e]
                st, ds_out = states[e][n], leaving[e][n]
                do_half = at(seq_grad, n, e)
                do = do_half.astype(f32)
                y_high, y_low = split(y)
                do_y = jnp.concatenate(
                    [jnp.concatenate([do_half, y_high], axis=0), jnp.concatenate([none, y_low], axis=0)], axis=1
                )
                by_u = mm_nt_split(do_y, u)
                by_s = mm_nt_split(do_y, st)
                dos, zneg = by_s[:CH], by_s[CH:]
                dkw = mm_nt(u, ds_out)
                decay = decays[j, i]
                dpd = by_u[:CH] * decay
                dls = by_u[CH:] * jnp.where(row > col, decay, 0.0)
                dlb = dls * kk
                f = dpd * qk - beta * dlb
                zk = zneg * k
                wk = w * (dkw * k)
                dbeta = rowsum(y * at(v_all, n, e) - s * zk - dlb)
                extra = jnp.sum(rowsum(wk + s_last * (ds_out * st)), axis=0, keepdims=True)
                dc = rowsum(f + s * (do * qs) - bs * zk - wk)
                dc = dc + jnp.where(row[:, :1] == CH - 1, extra, 0.0)
                packed = jnp.where(col == e, dbeta, packed)
                packed = jnp.where(col == heads + e, dc, packed)
                minus.append(jnp.sum(f, axis=0, keepdims=True))
                dqk_sum = dqk_sum + dpd
                dkk_sum = dkk_sum + beta * dls
                dq = dq + s * dos
                dk = dk + w * dkw - bs * zneg
                dvs[n, e] = beta * y
            by_k = mm(jnp.concatenate([dqk_sum, dkk_sum + dkk_sum.T], axis=0), k)
            dqs[n, h] = dq + by_k[:CH]
            dks[n, h] = dk + mm(dqk_sum.T, q) - by_k[CH:]
        row_grads[j, n] = packed.T[: 2 * heads] - jnp.concatenate([jnp.zeros((heads, CH), f32)] + minus, axis=0)
    mask = [masks[d] for d in range(TAPS - 1)]
    at_col = 0
    for grads, count, taps, body_out, tail_out, y_ref, scale_ref, gain in (
        (dqs, keys, q_taps, q_body, q_tail, qn, q_scale, DK),
        (dks, keys, k_taps, k_body, k_tail, kn, k_scale, 1),
        (dvs, heads, v_taps, v_body, v_tail, None, v_scale, 1),
    ):
        for h in range(count):
            da = jnp.concatenate([grads[n, h] for n in range(blocks)], axis=0)
            if y_ref is not None:
                y = y_ref[j, :, tile(h)]
                da = da - y * (rowsum(y * da) * float(gain))
            full = conv_back(da * scale_ref[j, :, tile(h)], taps[:, tile(h)], mask)
            body_out[j, :, tile(h)] = full[:tokens].astype(bf16)
            tail_out[j, :, tile(h)] = full[tokens - 2 * HALO : tokens]
            spill[j, :, at_col : at_col + CH] = full[tokens:]
            at_col += CH


def fused_kernel(ctxs, steps, *refs):
    swap_ref, a_log, dt_bias, beta_logit, gate_logit, doc_ids = refs[:6]
    taps, sources, refs = refs[6:9], refs[9:16], refs[16:]
    results, beta_grad, gate_grad, refs = refs[:4], refs[4], refs[5], refs[6:]
    raws, tap_rows, out, refs = refs[:4], refs[4:7], refs[7], refs[8:]
    gots, halos, (beta_got, gate_got, ids_got), refs = refs[:4], refs[4:7], refs[7:10], refs[10:]
    (masks, docs, rows, betas, factors), refs = refs[:5], refs[5:]
    saved, refs = refs[:14], refs[14:]
    (maps, affs, w_buf, w_got, x_buf, y_buf, s_buf, z_buf, z_got), refs = refs[:9], refs[9:]
    bodies, tails, (spill, spill_got, row_grads), refs = refs[:3], refs[3:6], refs[6:9], refs[9:]
    load_s, store_s, refs = refs[0], refs[1], refs[2:]
    swap_s, swap_r, hop_s, hop_r, pair_s, pair_r, spill_s, spill_r, got_s, got_r, halo_s, halo_r, few_s, few_r = refs
    step = pl.program_id(0)
    heads = w_buf.shape[1]
    tokens = raws[0].shape[1]
    core = lax.axis_index("pair")
    ctx = lax.axis_index("ctx")
    first = core == 0
    mine, other = 2 * core, 2 - 2 * core
    peer_ctx = jnp.where(first, ctx - 1, ctx + 1)
    has_peer = (peer_ctx >= 0) & (peer_ctx < ctxs)
    has_prev = jnp.logical_not(first) | has_peer
    has_next = first | has_peer
    partner = {"pair": 1 - core}
    peer = {"ctx": jnp.clip(peer_ctx, 0, ctxs - 1), "pair": 1 - core}
    following = {"ctx": jnp.clip(ctx + core, 0, ctxs - 1), "pair": 1 - core}
    previous = {"ctx": jnp.clip(ctx - 1 + core, 0, ctxs - 1), "pair": 1 - core}
    swap_flag = swap_ref[0]
    swaps = [jnp.where(first, 0, swap_flag), jnp.where(first, swap_flag, 0)]

    def remote(src, dst, send, recv, device):
        return pltpu.make_async_remote_copy(src, dst, send, recv, device_id=device, device_id_type=pl.DeviceIdType.MESH)

    def swap(j):
        return remote(w_buf.at[j], w_got.at[j], swap_s.at[j], swap_r.at[j], partner)

    def hop(j):
        return remote(x_buf.at[j], y_buf.at[j], hop_s.at[j], hop_r.at[j], peer)

    def pair(j):
        return remote(z_buf.at[j], z_got.at[j], pair_s.at[j], pair_r.at[j], partner)

    def spilled(j):
        return remote(spill.at[j], spill_got.at[j], spill_s.at[j], spill_r.at[j], previous)

    start = pl.multiple_of(jnp.where(first, SWAP, 0), SWAP)

    def exchanged(i, j):
        width = gots[i].shape[2]
        at = pl.multiple_of(j * width, CH)
        return remote(
            sources[i].at[pl.ds(start, SWAP), pl.ds(at, width)], gots[i].at[j], got_s.at[i, j], got_r.at[i, j], partner
        )

    def neighbour(i, j):
        width = halos[i].shape[2]
        at = pl.multiple_of(j * width, CH)
        return remote(
            sources[i].at[pl.ds(tokens - 2 * HALO, 2 * HALO), pl.ds(at, width)], halos[i].at[j], halo_s.at[i, j],
            halo_r.at[i, j], following,
        )

    def loaded(i, j):
        width = raws[i].shape[2]
        at = pl.multiple_of(j * width, CH)
        return pltpu.make_async_copy(sources[i].at[:, pl.ds(at, width)], raws[i].at[j], load_s.at[i, j])

    def stored(i, j):
        held = (out, *bodies)[i]
        width = held.shape[2]
        at = pl.multiple_of(j * width, CH)
        return pltpu.make_async_copy(held.at[j], results[i].at[:, pl.ds(at, width)], store_s.at[i, j])

    def logits(i):
        return remote(sources[4 + i].at[:, pl.ds(start, SWAP)], (beta_got, gate_got)[i], few_s.at[i], few_r.at[i], partner)

    ids_copy = remote(sources[6], ids_got, few_s.at[2], few_r.at[2], following)

    def fetch_rows(j):
        for i in range(4):
            exchanged(i, j).start()

        @pl.when(has_next)
        def _():
            for i in range(3):
                neighbour(i, j).start()

    @pl.when(step == 0)
    def _():
        for i in range(4):
            loaded(i, 0).start()
        barrier = pltpu.get_barrier_semaphore()
        pl.semaphore_signal(barrier, inc=1, device_id=partner, device_id_type=pl.DeviceIdType.MESH)

        @pl.when(has_peer)
        def _():
            pl.semaphore_signal(barrier, inc=1, device_id=peer, device_id_type=pl.DeviceIdType.MESH)

        pl.semaphore_wait(barrier, jnp.where(has_peer, 2, 1))

        @pl.when(has_next)
        def _():
            ids_copy.start()

        for i in range(2):
            logits(i).start()
        fetch_rows(0)

        for j in range(1, steps):
            for i in range(4):
                loaded(i, j).start()
        for i in range(3):
            width = tap_rows[i].shape[2]
            for j in range(steps):
                tap_rows[i][j] = taps[i][:, j * width : (j + 1) * width].astype(f32)

        @pl.when(has_prev)
        def _():
            ids_copy.wait_recv()

        @pl.when(jnp.logical_not(has_prev))
        def _():
            ids_got[...] = jnp.zeros(ids_got.shape, jnp.int32)
            for halo in halos:
                halo[...] = jnp.zeros(halo.shape, bf16)

        for i in range(2):
            logits(i).wait_recv()
        setup_phase(
            has_prev, swaps, a_log, dt_bias, beta_logit, gate_logit, doc_ids, beta_got, gate_got, ids_got,
            masks, docs, rows, betas, factors,
        )

    def advance(j, at, got):
        mid = [affs[j, e, at] + mm(maps[j, e, at], got[j, e]) for e in range(heads)]
        return mid, [affs[j, e, at + 1] + mm(maps[j, e, at + 1], mid[e]) for e in range(heads)]

    def chains(over, back):
        if over:
            swap(step - 1).wait_recv()
        if back:
            @pl.when(has_peer)
            def _():
                hop(step - 2).wait_recv()

            @pl.when(jnp.logical_not(has_peer))
            def _():
                y_buf[step - 2] = jnp.zeros(y_buf.shape[1:], f32)

        if over:
            mid, end = advance(step - 1, other, w_got)
            for e in range(heads):
                x_buf[step - 1, e] = end[e]
        if back:
            mid, end = advance(step - 2, mine, y_buf)
            for e in range(heads):
                s_buf[step - 2, e] = mid[e]
                z_buf[step - 2, e] = end[e]
        if over:
            @pl.when(has_peer)
            def _():
                hop(step - 1).start()

        if back:
            pair(step - 2).start()

    @pl.when(step < steps)
    def _():
        for i in range(4):
            loaded(i, step).wait()
            exchanged(i, step).wait_recv()

        @pl.when(has_prev)
        def _():
            for i in range(3):
                neighbour(i, step).wait_recv()

        @pl.when(step < steps - 1)
        def _():
            fetch_rows(step + 1)

        forward_phase(
            step, first, swaps, *[x.at[step] for x in raws], *[x.at[step] for x in tap_rows], *gots, *halos, masks, docs,
            rows, *saved, maps, affs, w_buf,
        )
        swap(step).start()

    @pl.when((step >= steps) & (step < 2 * steps))
    def _():
        j = step - steps
        pair(j).wait_recv()
        backward_phase(
            j, first, other, *[x.at[j] for x in tap_rows], masks, rows, *saved, maps, affs, y_buf, s_buf, z_got, out.at[j],
            *bodies, *tails, spill, row_grads,
        )
        stored(0, j).start()

        @pl.when(has_prev)
        def _():
            spilled(j).start()

    @pl.when(step == 1)
    def _():
        chains(True, False)

    @pl.when((step >= 2) & (step <= steps))
    def _():
        chains(True, True)

    @pl.when(step == steps + 1)
    def _():
        chains(False, True)

    @pl.when(step == 2 * steps)
    def _():
        blocks = tokens // CH
        weights = (iota(0) >= iota(1)).astype(bf16)
        for n in range(blocks):
            dbeta = jnp.concatenate([row_grads[j, n, :heads] for j in range(steps)], axis=0)
            dc = jnp.concatenate([row_grads[j, n, heads:] for j in range(steps)], axis=0)
            beta = betas[n]
            beta_grad[:, tile(n)] = (dbeta * beta * (1.0 - beta)).astype(bf16)
            gate_grad[:, tile(n)] = (summed(dc, weights) * factors[n]).astype(bf16)

    @pl.when(step > steps)
    def _():
        j = step - steps - 1

        @pl.when(has_next)
        def _():
            spilled(j).wait_recv()

        @pl.when(jnp.logical_not(has_next))
        def _():
            spill_got[j] = jnp.zeros(spill_got.shape[1:], f32)

        at = 0
        for i, (held, tail) in enumerate(zip(bodies, tails)):
            width = held.shape[2]
            last = tail[j]
            last = jnp.concatenate([last[:HALO], last[HALO:] + spill_got[j, :, at : at + width]], axis=0)
            held[j, tokens - 2 * HALO :] = last.astype(bf16)
            stored(i + 1, j).start()
            at += width

    @pl.when(step == 2 * steps)
    def _():
        for i in range(2):
            logits(i).wait_send()

        @pl.when(has_next)
        def _():
            ids_copy.wait_send()

        for j in range(steps):
            swap(j).wait_send()
            pair(j).wait_send()
            for i in range(4):
                stored(i, j).wait()
                exchanged(i, j).wait_send()

            @pl.when(has_peer)
            def _():
                hop(j).wait_send()

            @pl.when(has_next)
            def _():
                for i in range(3):
                    neighbour(i, j).wait_send()

            @pl.when(has_prev)
            def _():
                spilled(j).wait_send()


def join_kernel(m, a, g, a_in, g_in, a_out, g_out):
    for e in range(m.shape[0]):
        here = m[e]
        a_out[e] = a[e] + mm(here, a_in[e])
        g_out[e] = g[e] + mm(here.T, g_in[e])


def norm_back(dy, a, scale):
    sig = sigmoid(a)
    u = a * sig
    inverse = 1.0 / jnp.sqrt(rowsum(u * u) + GUARD)
    y = u * inverse
    dy = dy * scale
    du = (dy - y * rowsum(y * dy)) * inverse
    return du * (sig + u * (1.0 - sig))


def main_kernel(
    a_q, a_k, a_v, qn, kn, seq_grad, inv, kk_in, qk_in, pdo_in, q_taps, k_taps, v_taps, masks, docs, rows,
    s_in, d_in, out, q_grad, k_grad, v_grad, q_end, k_end, v_end, q_spill, k_spill, v_spill, row_grads,
):
    tokens = a_q.shape[0]
    blocks = tokens // CH
    heads = a_v.shape[1] // CH
    row, col = iota(0), iota(1)
    va = a_v[...]
    v_sig = sigmoid(va)
    v_all = va * v_sig
    info = []
    for n in range(blocks):
        q = qn[n * CH : (n + 1) * CH, :]
        k = kn[n * CH : (n + 1) * CH, :]
        info.append((q, k, q.T, k.T, rows[0, n], columns(rows[0, n])))
    fwd = {}
    carried = [s_in[e] for e in range(heads)]
    for n in range(blocks):
        q, k, q_t, k_t, flat, cols = info[n]
        kq = jnp.concatenate([k, q], axis=0)
        for e in range(heads):
            beta, c, s, w = [cols[:, 4 * e + i : 4 * e + i + 1] for i in range(4)]
            beta_r, c_r, s_r, w_r = [flat[4 * e + i : 4 * e + i + 1, :] for i in range(4)]
            s_last = s_r[:, CH - 1 :]
            v = v_all[n * CH : (n + 1) * CH, e * CH : (e + 1) * CH]
            decay = jnp.exp(jnp.minimum(c - c_r, 0.0)) * docs[n]
            p = decay * qk_in[0, n]
            st = carried[e]
            kqs = mm(kq, st)
            ks, qs = kqs[:CH], kqs[CH:]
            t = inv[0, e, n]
            u = mm(t, beta * (v - s * ks))
            o = s * qs + mm(p, u)
            out[n * CH : (n + 1) * CH, e * CH : (e + 1) * CH] = o.astype(bf16)
            if n + 1 < blocks:
                carried[e] = s_last * st + mm(k_t * w_r, u)
            fwd[n, e] = (st, u, qs, decay, p, v)
    grads = [d_in[e] for e in range(heads)]
    dqs, dks, dvs = [None] * blocks, [None] * blocks, {}
    for n in reversed(range(blocks)):
        q, k, q_t, k_t, flat, cols = info[n]
        packed = jnp.zeros((CH, CH), f32)
        dqk_sum = dkk_sum = dq = dk = 0.0
        for e in range(heads):
            beta, c, s, w = [cols[:, 4 * e + i : 4 * e + i + 1] for i in range(4)]
            beta_r, c_r, s_r, w_r = [flat[4 * e + i : 4 * e + i + 1, :] for i in range(4)]
            s_last = s_r[:, CH - 1 :]
            st, u, qs, decay, p, v = fwd[n, e]
            ds_out = grads[e]
            do_half = seq_grad[n * CH : (n + 1) * CH, e * CH : (e + 1) * CH]
            do = do_half.astype(f32)
            du = pdo_in[0, e, n] + mm(k * w, ds_out)
            y = mm(inv[0, e, n].T, du)
            do_y = jnp.concatenate([do, y], axis=0)
            by_u = mm_nt(do_y, u)
            by_s = mm_nt(do_y, st)
            dp, dl = by_u[:CH], -by_u[CH:]
            dos, z = by_s[:CH], -by_s[CH:]
            dkw = mm_nt(u, ds_out)
            strict = jnp.where(row > col, decay, 0.0)
            bk = strict * kk_in[0, n]
            dlb = dl * bk
            f = dp * p + beta * dlb
            zk = z * k
            wk = w * (dkw * k)
            bs = beta * s
            dbeta = rowsum(y * v + s * zk + dlb)
            extra = jnp.sum(rowsum(wk + s_last * (ds_out * st)), axis=0, keepdims=True)
            dc = rowsum((f - f.T) + s * (do * qs) + bs * zk - wk)
            dc = dc + jnp.where(row[:, :1] == CH - 1, extra, 0.0)
            packed = jnp.where(col == 2 * e, dbeta, packed)
            packed = jnp.where(col == 2 * e + 1, dc, packed)
            dqk_sum = dqk_sum + dp * decay
            dkk_sum = dkk_sum + dl * (beta * strict)
            dq = dq + s * dos
            dk = dk + w * dkw + bs * z
            dvs[n, e] = beta * y
            if n > 0:
                grads[e] = mm_half(q_t * s_r, do_half) + s_last * ds_out - mm(k_t * (beta_r * s_r), y)
        dqs[n] = dq + mm(dqk_sum, k)
        dks[n] = dk + mm(dqk_sum.T, q) + mm(dkk_sum + dkk_sum.T, k)
        row_grads[0, n] = packed.T[: row_grads.shape[2]]
    dq = jnp.concatenate(dqs, axis=0)
    dk = jnp.concatenate(dks, axis=0)
    dv = jnp.concatenate(
        [jnp.concatenate([dvs[n, e] for e in range(heads)], axis=1) for n in range(blocks)], axis=0
    )
    daq = norm_back(dq, a_q[...], SCALE)
    dak = norm_back(dk, a_k[...], 1.0)
    dav = dv * (v_sig + v_all * (1.0 - v_sig))
    for da, taps, grad, end, spill in (
        (daq, q_taps, q_grad, q_end, q_spill),
        (dak, k_taps, k_grad, k_end, k_spill),
        (dav, v_taps, v_grad, v_end, v_spill),
    ):
        full = conv_back(da, taps, masks)
        grad[...] = full[:tokens].astype(bf16)
        end[...] = full[tokens - HALO : tokens]
        spill[...] = full[tokens:]


def shifted(array, by):
    peers = lax.axis_size(SEQ)
    return lax.ppermute(array, SEQ, [(i, i + by) for i in range(peers) if 0 <= i + by < peers])


def tri(upper):
    i = jnp.arange(CH)
    return ((i[:, None] <= i[None, :]) if upper else (i[:, None] >= i[None, :])).astype(f32)


def sds(shape, dtype=f32):
    return jax.ShapeDtypeStruct(shape, dtype)


def staged_call(inputs, hk, hv, tokens, hops):
    blocks = tokens // CH
    rep = hv // hk
    qw = hk * DK
    vw = rep * DK
    col = lambda rows_, width, off=0: pl.BlockSpec((rows_, width), lambda i, off=off, width=width: (0, off // width + i))
    fixed = lambda shape: pl.BlockSpec(shape, lambda i: (0,) * len(shape))
    per = lambda shape: pl.BlockSpec(shape, lambda i: (i,) + (0,) * (len(shape) - 1))
    taps_specs = [col(TAPS, DK), col(TAPS, DK), col(TAPS, vw)]
    common_specs = taps_specs + [
        fixed((TAPS - 1, tokens, CH)),
        fixed((blocks, CH, CH)),
        per((1, blocks, rep * 4, CH)),
    ]
    params = pltpu.CompilerParams(dimension_semantics=("arbitrary",), vmem_limit_bytes=48 * 2**20)
    saved_specs = [
        col(tokens, DK), col(tokens, DK), col(tokens, vw), col(tokens, DK), col(tokens, DK), col(tokens, vw),
        per((1, rep, blocks, CH, CH)), per((1, blocks, CH, CH)), per((1, blocks, CH, CH)),
        per((1, rep, blocks, CH, CH)),
    ]
    saved_shapes = [
        sds((tokens, qw)), sds((tokens, qw)), sds((tokens, hv * DK)), sds((tokens, qw)), sds((tokens, qw)),
        sds((tokens, hv * DK), bf16), sds((hk, rep, blocks, CH, CH)), sds((hk, blocks, CH, CH)),
        sds((hk, blocks, CH, CH)), sds((hk, rep, blocks, CH, CH)),
    ]
    state_spec = per((rep, DK, DK))
    state_shape = sds((hv, DK, DK))
    units = hv * blocks * 2 * 4 * CH**3
    *taps, masks, docs, rows = inputs[12:]
    in_specs = [
        pl.BlockSpec(memory_space=pltpu.SMEM),
        col(tokens, DK), col(tokens, DK), col(tokens, vw), col(tokens, vw),
        col(SWAP, DK), col(SWAP, DK, qw), col(SWAP, vw, 2 * qw), col(SWAP, vw, 2 * qw + hv * DK),
        col(HALO, DK), col(HALO, DK, qw), col(HALO, vw, 2 * qw),
    ] + common_specs
    prepare_cost = pl.CostEstimate(flops=22 * units, bytes_accessed=24 * 2**20, transcendentals=2**20)
    prepared = pl.pallas_call(
        prepare_kernel,
        grid=(hk,),
        in_specs=in_specs,
        out_specs=saved_specs + [state_spec] * 3,
        out_shape=saved_shapes + [state_shape] * 3,
        compiler_params=params,
        cost_estimate=prepare_cost,
        name="prepare",
    )(*inputs)
    saved, (m, a, g) = prepared[:10], prepared[10:]
    join = pl.pallas_call(
        join_kernel,
        grid=(hk,),
        in_specs=[state_spec] * 5,
        out_specs=[state_spec] * 2,
        out_shape=[state_shape] * 2,
        compiler_params=params,
        cost_estimate=pl.CostEstimate(flops=hv * 16 * CH**3, bytes_accessed=7 * 2**20, transcendentals=0),
        name="join",
    )
    s_in, d_in = a, g
    for step in range(hops):
        s_in, d_in = shifted(s_in, 1), shifted(d_in, -1)
        if step < hops - 1:
            s_in, d_in = join(m, a, g, s_in, d_in)

    ends = [col(HALO, DK), col(HALO, DK), col(HALO, vw)]
    end_shapes = [sds((HALO, qw)), sds((HALO, qw)), sds((HALO, hv * DK))]
    return pl.pallas_call(
        main_kernel,
        grid=(hk,),
        in_specs=saved_specs + common_specs + [state_spec] * 2,
        out_specs=[col(tokens, vw), col(tokens, DK), col(tokens, DK), col(tokens, vw)] + ends + ends + [per((1, blocks, 8, CH))],
        out_shape=[
            sds((tokens, hv * DK), bf16), sds((tokens, qw), bf16), sds((tokens, qw), bf16), sds((tokens, hv * DK), bf16)
        ] + end_shapes + end_shapes + [sds((hk, blocks, 8, CH))],
        compiler_params=params,
        cost_estimate=pl.CostEstimate(flops=17 * units, bytes_accessed=24 * 2**20, transcendentals=2**20),
        name="main",
    )(*saved, *taps, masks, docs, rows, s_in, d_in)


def copy_kernel(*refs):
    count = (len(refs) - 2) // 3
    held = refs[2 * count : 3 * count]
    in_sems, out_sems = refs[3 * count :]
    pieces = []
    for src, dst, mid in zip(refs[:count], refs[count : 2 * count], held):
        size = max(16, min(src.shape[0], COPY_BYTES // (2 * src.shape[1])))
        for at in range(0, src.shape[0], size):
            rows, i = pl.ds(at, size), len(pieces)
            pieces.append((
                pltpu.make_async_copy(src.at[rows], mid.at[rows], in_sems.at[i]),
                pltpu.make_async_copy(mid.at[rows], dst.at[rows], out_sems.at[i]),
            ))
    for load, store in pieces:
        load.start()
    for load, store in pieces:
        load.wait()
        store.start()
    for load, store in pieces:
        store.wait()


def copied(arrays):
    hbm = pl.BlockSpec(memory_space=pl.ANY)
    return pl.pallas_call(
        copy_kernel,
        in_specs=[hbm] * len(arrays),
        out_specs=[hbm] * len(arrays),
        out_shape=[sds(x.shape, x.dtype) for x in arrays],
        scratch_shapes=[pltpu.VMEM(x.shape, x.dtype) for x in arrays] + [pltpu.SemaphoreType.DMA((32,))] * 2,
        name="copies",
    )(*arrays)


def fused_call(
    q_raw, k_raw, v_raw, beta_logit, gate_logit, out_grad, conv_q, conv_k, conv_v, a_log, dt_bias, doc_ids, swap_blocks
):
    tokens, qw = q_raw.shape
    blocks = tokens // CH
    hk = qw // DK
    hv = v_raw.shape[1] // DK
    steps = hk // GROUP
    heads = hv // steps
    gw, vw = GROUP * DK, heads * DK
    doc_ids = doc_ids.reshape(blocks, CH)
    fixed = lambda shape: pl.BlockSpec(shape, lambda i: (0,) * len(shape))
    smem = pl.BlockSpec(memory_space=pltpu.SMEM)
    hbm = pl.BlockSpec(memory_space=pl.ANY)
    in_specs = [smem] * 3 + [fixed(x.shape) for x in (beta_logit, gate_logit, doc_ids, conv_q, conv_k, conv_v)] + [hbm] * 7
    vm = lambda *shape: pltpu.VMEM(shape, f32)
    half = lambda *shape: pltpu.VMEM(shape, bf16)
    square = lambda *lead: vm(steps, *lead, CH, CH)
    wide = lambda width: vm(steps, tokens, width)
    units = blocks * heads
    sems = lambda *shape: pltpu.SemaphoreType.DMA(shape)
    scratch = [half(steps, tokens, gw), half(steps, tokens, gw), half(steps, tokens, vw), half(steps, tokens, vw)]
    scratch += [vm(steps, TAPS, gw), vm(steps, TAPS, gw), vm(steps, TAPS, vw), half(steps, tokens, vw)]
    scratch += [half(steps, SWAP, gw), half(steps, SWAP, gw), half(steps, SWAP, vw), half(steps, SWAP, vw)]
    scratch += [half(steps, 2 * HALO, gw), half(steps, 2 * HALO, gw), half(steps, 2 * HALO, vw)]
    scratch += [half(hv, SWAP), half(hv, SWAP), pltpu.VMEM((blocks, CH), jnp.int32)]
    scratch += [vm(TAPS - 1, tokens, CH), vm(blocks, CH, CH), vm(steps, blocks, KINDS * heads, CH)]
    scratch += [vm(blocks, hv, CH), vm(blocks, hv, CH)]
    scratch += [wide(gw), wide(gw), wide(vw), wide(vw), wide(gw), wide(gw), half(steps, tokens, vw)]
    scratch += [square(units)] * 5 + [square(blocks * GROUP)] * 2 + [square(heads, 4)] * 2 + [square(heads)] * 7
    scratch += [half(steps, tokens, gw), half(steps, tokens, gw), half(steps, tokens, vw)]
    scratch += [vm(steps, 2 * HALO, gw), vm(steps, 2 * HALO, gw), vm(steps, 2 * HALO, vw)]
    scratch += [vm(steps, HALO, 2 * gw + vw)] * 2 + [vm(steps, blocks, 2 * heads, CH)]
    scratch += [sems(4, steps)] * 2 + [sems(steps)] * 8 + [sems(4, steps)] * 2 + [sems(3, steps)] * 2 + [sems(3)] * 2
    return pl.pallas_call(
        functools.partial(fused_kernel, lax.axis_size("ctx"), steps),
        grid=(2 * steps + 1,),
        in_specs=in_specs,
        out_specs=[hbm] * 4 + [fixed((hv, tokens))] * 2,
        out_shape=[
            sds((tokens, hv * DK), bf16), sds((tokens, qw), bf16), sds((tokens, qw), bf16), sds((tokens, hv * DK), bf16),
            sds((hv, tokens), bf16), sds((hv, tokens), bf16),
        ],
        scratch_shapes=scratch,
        compiler_params=pltpu.CompilerParams(
            dimension_semantics=("arbitrary",), vmem_limit_bytes=56 * 2**20, collective_id=0, has_side_effects=True
        ),
        cost_estimate=pl.CostEstimate(
            flops=30 * hv * blocks * 8 * CH**3, bytes_accessed=8 * 2**20, transcendentals=2**21
        ),
        name="fused",
    )(
        swap_blocks, a_log, dt_bias, beta_logit, gate_logit, doc_ids, conv_q, conv_k, conv_v,
        q_raw, k_raw, v_raw, out_grad, beta_logit, gate_logit, doc_ids,
    )


def body(
    q_raw, k_raw, v_raw, beta_logit, gate_logit, out_grad, conv_q, conv_k, conv_v, a_log, dt_bias, doc_ids, swap_blocks
):
    tokens = q_raw.shape[0]
    blocks = tokens // CH
    hk = q_raw.shape[1] // DK
    hv = v_raw.shape[1] // DK
    rep = hv // hk
    shards = lax.axis_size(SEQ)
    hops = max(1, shards // DOC_PARTS)
    if hops == lax.axis_size("pair") and blocks == 2 and hk % GROUP == 0:
        return copied(
            fused_call(
                q_raw, k_raw, v_raw, beta_logit, gate_logit, out_grad, conv_q, conv_k, conv_v, a_log, dt_bias, doc_ids,
                swap_blocks,
            )
        )
    core = lax.axis_index("pair")
    swap = swap_blocks[0]
    flags = jnp.stack([jnp.where(core == 1, swap, 0), jnp.where(core == 0, swap, 0)]).astype(jnp.int32)

    start = jnp.where(core == 0, SWAP, 0)
    logits = jnp.concatenate([beta_logit, gate_logit], axis=0)
    bg_send = lax.dynamic_slice_in_dim(logits, start, SWAP, 1)
    send = jnp.concatenate(
        [lax.dynamic_slice_in_dim(x, start, SWAP, 0) for x in (q_raw, k_raw, v_raw, out_grad)], axis=1
    )
    got = lax.ppermute(send, "pair", [(0, 1), (1, 0)])
    send, bg_send, tail_ids, tails = lax.optimization_barrier(
        (send, bg_send, doc_ids[tokens - HALO :], [x[tokens - HALO :] for x in (q_raw, k_raw, v_raw)])
    )
    bg_got = lax.ppermute(bg_send, "pair", [(0, 1), (1, 0)])
    ids_col = jnp.broadcast_to((tail_ids + 1).astype(bf16)[:, None], (HALO, CH))
    tail = jnp.concatenate(tails + [ids_col], axis=1)
    before = shifted(tail, 1)
    own = jnp.concatenate([x[SWAP - HALO : SWAP] for x in (q_raw, k_raw, v_raw)], axis=1)
    chans = own.shape[1]
    halo = jnp.where(flags[0] > 0, own, before[:, :chans]).astype(f32)
    qw = hk * DK

    first = jnp.where(flags[0] > 0, bg_got, logits[:, :SWAP])
    second = jnp.where(flags[1] > 0, bg_got, logits[:, SWAP:])
    logits = jnp.concatenate([first, second], axis=1).astype(f32)
    beta = jax.nn.sigmoid(logits[:hv])
    gate = logits[hv:] + dt_bias[:, None]
    rate = -jnp.exp(a_log)[:, None]
    decay_log = rate * jax.nn.softplus(gate)
    c = jnp.dot(decay_log.reshape(hv * blocks, CH), tri(True), precision=highest).reshape(hv, blocks, CH)
    ids = doc_ids.astype(f32) + 1.0
    ext_ids = jnp.concatenate([before[:, chans].astype(f32), ids])
    doc = ids.reshape(blocks, CH)
    doc_before = ext_ids[HALO - 1 : HALO - 1 + tokens : CH]
    s = jnp.where(doc == doc_before[:, None], jnp.exp(c), 0.0)
    w = jnp.where(doc == doc[:, CH - 1 :], jnp.exp(jnp.minimum(c[:, :, CH - 1 :] - c, 0.0)), 0.0)
    rows = jnp.stack([beta.reshape(hv, blocks, CH), c, s, w], axis=2)
    rows = rows.reshape(hk, rep, blocks, 4, CH).transpose(0, 2, 1, 3, 4).reshape(hk, blocks, rep * 4, CH)
    docs = ((doc[:, :, None] == doc[:, None, :]) & (tri(False) > 0)[None]).astype(f32)
    masks = jnp.stack(
        [
            jnp.broadcast_to((ext_ids[HALO - d : HALO - d + tokens] == ids).astype(f32)[:, None], (tokens, CH))
            for d in range(1, TAPS)
        ]
    )
    taps = [x.astype(f32) for x in (conv_q, conv_k, conv_v)]

    results = staged_call(
        (flags, q_raw, k_raw, v_raw, out_grad, got, got, got, got, halo, halo, halo, *taps, masks, docs, rows), hk, hv,
        tokens, hops,
    )
    layer_out, q_grad, k_grad, v_grad = results[:4]
    spilled = shifted(jnp.concatenate(results[7:10], axis=1), -1)
    ends_out = []
    at = 0
    for grad, end in zip((q_grad, k_grad, v_grad), results[4:7]):
        width = end.shape[1]
        last = (end + spilled[:, at : at + width]).astype(bf16)
        ends_out.append(lax.dynamic_update_slice(grad, last, (tokens - HALO, 0)))
        at += width
    rg = results[10][:, :, : 2 * rep].reshape(hk, blocks, rep, 2, CH).transpose(3, 0, 2, 1, 4)
    dbeta = rg[0].reshape(hv, tokens)
    dg = jnp.dot(rg[1].reshape(hv * blocks, CH), tri(False), precision=highest).reshape(hv, tokens)
    beta_grad = dbeta * beta * (1.0 - beta)
    gate_grad = dg * rate * jax.nn.sigmoid(gate)
    return (layer_out, ends_out[0], ends_out[1], ends_out[2], beta_grad.astype(bf16), gate_grad.astype(bf16))


def solution(mesh):
    rows = P(("groups", "ctx", "pair"), "head")
    rates = P("head", ("groups", "ctx", "pair"))
    taps = P(None, "head")
    return jax.shard_map(
        body,
        mesh=mesh,
        in_specs=(
            rows, rows, rows, rates, rates, rows, taps, taps, taps, P("head"), P("head"),
            P(("groups", "ctx", "pair")), P(("groups", "ctx")),
        ),
        out_specs=(rows, rows, rows, rows, rates, rates),
        check_vma=False,
    )
```

```python
import functools
import math

import jax
import jax.numpy as jnp
from jax import lax
from jax.experimental import pallas as pl
from jax.experimental.pallas import tpu as pltpu
from jax.sharding import PartitionSpec as P

DK = 128
TAPS = 4
CH = 128
SWAP = 128
HALO = 8
GUARD = 1e-06
SCALE = 1.0 / math.sqrt(DK)
DOC_PARTS = 4
GROUP = 2
BASE = 16
KINDS = 5
COPY_BYTES = 2**18

f32 = jnp.float32
bf16 = jnp.bfloat16
highest = lax.Precision.HIGHEST
SEQ = ("ctx", "pair")


def split(x):
    high = x.astype(bf16)
    return high, (x - high.astype(f32)).astype(bf16)


def mm(a, b):
    ah, al = split(a)
    bh, bl = split(b)
    lhs = jnp.concatenate([ah, al], axis=1)
    rhs = jnp.concatenate(
        [jnp.concatenate([bh, bl], axis=1), jnp.concatenate([bh, jnp.zeros_like(bh)], axis=1)], axis=0
    )
    r = lax.dot_general(lhs, rhs, (((1,), (0,)), ((), ())), preferred_element_type=f32)
    n = b.shape[1]
    return r[:, :n] + r[:, n:]


def mm_half(a, b):
    return lax.dot_general(
        jnp.concatenate(split(a), axis=1), jnp.concatenate([b, b], axis=0), (((1,), (0,)), ((), ())),
        preferred_element_type=f32,
    )


def odd_blocks(x, size):
    return jnp.concatenate([x[i : i + size] for i in range(size, CH, 2 * size)], axis=0)


def with_odd(even, odd, size):
    parts = []
    for i in range(0, CH // 2, size):
        parts.append(jnp.zeros((size, CH), odd.dtype) if even is None else even[2 * i : 2 * i + size])
        parts.append(odd[i : i + size])
    return jnp.concatenate(parts, axis=0)


def mm_nt(a, b):
    ah, al = split(a)
    bh, bl = split(b)
    lhs = jnp.concatenate([ah, al], axis=1)
    rhs = jnp.concatenate(
        [jnp.concatenate([bh, bh], axis=1), jnp.concatenate([bl, jnp.zeros_like(bl)], axis=1)], axis=0
    )
    r = lax.dot_general(lhs, rhs, (((1,), (1,)), ((), ())), preferred_element_type=f32)
    n = b.shape[0]
    return r[:, :n] + r[:, n:]


def mm_nt_split(lhs, b):
    bh, bl = split(b)
    rhs = jnp.concatenate(
        [jnp.concatenate([bh, bh], axis=1), jnp.concatenate([bl, jnp.zeros_like(bl)], axis=1)], axis=0
    )
    r = lax.dot_general(lhs, rhs, (((1,), (1,)), ((), ())), preferred_element_type=f32)
    n = b.shape[0]
    return r[:, :n] + r[:, n:]


def iota(axis):
    return lax.broadcasted_iota(jnp.int32, (CH, CH), axis)


def rowsum(x):
    return jnp.sum(x, axis=1, keepdims=True)


def columns(rows):
    return jnp.concatenate([rows, jnp.zeros((CH - rows.shape[0], CH), f32)], axis=0).T


def sigmoid(a):
    return 1.0 / (1.0 + jnp.exp(-a))


def fetch(raw, recv, flags):
    first = raw[:SWAP, :]
    second = raw[SWAP:, :]
    got = recv[...]
    first = jnp.where(flags[0] > 0, got, first)
    second = jnp.where(flags[1] > 0, got, second)
    return jnp.concatenate([first, second], axis=0)


def conv(x, halo, taps, masks):
    ext = jnp.concatenate([halo, x], axis=0)
    width = x.shape[1] // CH
    total = taps[TAPS - 1 : TAPS, :] * x
    for d in range(1, TAPS):
        moved = pltpu.roll(ext, d, 0)[HALO:, :]
        mask = masks[d - 1]
        if width > 1:
            mask = jnp.concatenate([mask] * width, axis=1)
        total = total + taps[TAPS - 1 - d : TAPS - d, :] * (moved * mask)
    return total


def conv_back(da, taps, masks):
    width = da.shape[1] // CH
    zeros = jnp.zeros((HALO, da.shape[1]), f32)
    total = taps[TAPS - 1 : TAPS, :] * jnp.concatenate([da, zeros], axis=0)
    size = total.shape[0]
    for d in range(1, TAPS):
        mask = masks[d - 1]
        if width > 1:
            mask = jnp.concatenate([mask] * width, axis=1)
        ext = jnp.concatenate([da * mask, zeros], axis=0)
        total = total + taps[TAPS - 1 - d : TAPS - d, :] * pltpu.roll(ext, size - d, 0)
    return total


def local_maps(
    flags, q_raw, k_raw, v_raw, g_raw, q_got, k_got, v_got, g_got, q_halo, k_halo, v_halo,
    q_taps, k_taps, v_taps, masks, docs, rows,
    a_q, a_k, a_v, qn_out, kn_out, seq_grad, inv_out, kk_out, qk_out, pdo_out,
):
    blocks = q_raw.shape[0] // CH
    qa = conv(fetch(q_raw, q_got, flags).astype(f32), q_halo[...], q_taps, masks)
    ka = conv(fetch(k_raw, k_got, flags).astype(f32), k_halo[...], k_taps, masks)
    va = conv(fetch(v_raw, v_got, flags).astype(f32), v_halo[...], v_taps, masks)
    a_q[...] = qa
    a_k[...] = ka
    a_v[...] = va
    gs = fetch(g_raw, g_got, flags)
    seq_grad[...] = gs
    do_all = gs
    qu = qa * sigmoid(qa)
    ku = ka * sigmoid(ka)
    v_all = va * sigmoid(va)
    qn = qu * (SCALE / jnp.sqrt(rowsum(qu * qu) + GUARD))
    kn = ku * (1.0 / jnp.sqrt(rowsum(ku * ku) + GUARD))
    qn_out[...] = qn
    kn_out[...] = kn
    row, col = iota(0), iota(1)
    eye = (row == col).astype(f32)
    heads = v_raw.shape[1] // CH
    state = []
    for n in range(blocks):
        q = qn[n * CH : (n + 1) * CH]
        k = kn[n * CH : (n + 1) * CH]
        both = mm_nt(jnp.concatenate([k, q], axis=0), k)
        kk, qk = both[:CH], both[CH:]
        kk_out[0, n] = kk
        qk_out[0, n] = qk
        q_t, k_t = q.T, k.T
        flat = rows[0, n]
        cols = columns(flat)
        for e in range(heads):
            beta, c, s, w = [cols[:, 4 * e + i : 4 * e + i + 1] for i in range(4)]
            beta_r, c_r, s_r, w_r = [flat[4 * e + i : 4 * e + i + 1, :] for i in range(4)]
            s_last = s_r[:, CH - 1 :]
            decay = jnp.exp(jnp.minimum(c - c_r, 0.0)) * docs[n]
            low = jnp.where(row > col, beta * decay * kk, 0.0)
            do = do_all[n * CH : (n + 1) * CH, e * CH : (e + 1) * CH]
            v = v_all[n * CH : (n + 1) * CH, e * CH : (e + 1) * CH]
            state.append((n, e, low, decay * qk, do, v, k * w, (beta_r * s_r) * k_t, beta * s * k, s_r * q_t, beta * v, s_last))
    inv = []
    for item in state:
        inv.append(eye - jnp.where((row >> 1) == (col >> 1), item[2], 0.0))
    size = 1
    while (2 << size) <= CH:
        near = ((row >> (size + 1)) == (col >> (size + 1))) & ((row >> size) != (col >> size))
        width = 1 << size
        if width < 8:
            half = [mm(jnp.where(near, item[2], 0.0), t) for item, t in zip(state, inv)]
            inv = [t - mm(t, h) for t, h in zip(inv, half)]
        else:
            half = [mm(odd_blocks(jnp.where(near, item[2], 0.0), width), t) for item, t in zip(state, inv)]
            odds = [odd_blocks(t, width) for t in inv]
            odds = [t - mm(t, with_odd(None, h, width)) for t, h in zip(odds, half)]
            inv = [with_odd(t, o, width) for t, o in zip(inv, odds)]
        size += 1
    maps = {}
    for item, t in zip(state, inv):
        n, e, low, p, do, v, kw, bsk_t, bsk, sq_t, bv, s_last = item
        inv_out[0, e, n] = t
        pdo = mm_half(p.T, do)
        pdo_out[0, e, n] = pdo
        t_t = t.T
        b = mm(t_t, kw)
        cc = mm(t_t, pdo)
        b_t = b.T
        m = s_last * eye - mm(b_t, bsk)
        a = mm(b_t, bv)
        g = mm_half(sq_t, do) - mm(bsk_t, cc)
        maps[n, e] = (m, a, g)
    results = []
    for e in range(heads):
        m, a, g = maps[0, e]
        for n in range(1, blocks):
            m2, a2, g2 = maps[n, e]
            g = g + mm(m.T, g2)
            a = mm(m2, a) + a2
            m = mm(m2, m)
        results.append((m, a, g))
    return results


def prepare_kernel(*refs):
    m_out, a_out, g_out = refs[-3:]
    for e, (m, a, g) in enumerate(local_maps(*refs[:-3])):
        m_out[e] = m
        a_out[e] = a
        g_out[e] = g


def inverse_blocks(lows, size, fillers):
    regs = size // 8
    lane = lax.broadcasted_iota(jnp.int32, (8, CH), 1)
    sub = lax.broadcasted_iota(jnp.int32, (8, CH), 0)
    base = lane - lax.rem(lane, size)
    packed, inv = [], []
    for low in lows:
        rows_, eyes = [], []
        for r in range(regs):
            acc = low[8 * r : 8 * r + 8]
            for at in range(size, CH, size):
                acc = jnp.where(lane >= at, low[at + 8 * r : at + 8 * r + 8], acc)
            rows_.append(acc)
            eyes.append((lane - base == sub + 8 * r).astype(f32))
        packed.append(rows_)
        inv.append(eyes)
    fillers = list(fillers)
    every = max(1, (size - 1) // max(1, len(fillers)))
    for j in range(size - 1):
        here = j // 8
        index = base + j
        for low, t in zip(packed, inv):
            line = jnp.broadcast_to(t[here][j % 8 : j % 8 + 1], (8, CH))
            for r in range(here if j % 8 < 7 else here + 1, regs):
                t[r] = t[r] - jnp.take_along_axis(low[r], index, axis=1, mode="promise_in_bounds") * line
        if fillers and j % every == 0:
            fillers.pop(0)()
    for filler in fillers:
        filler()
    return [
        jnp.concatenate([jnp.where(base == at, x, 0.0) for at in range(0, CH, size) for x in t], axis=0) for t in inv
    ]


def head_scalars(cols, flat, e, heads):
    return (
        [cols[:, i * heads + e : i * heads + e + 1] for i in range(KINDS)],
        [flat[i * heads + e : i * heads + e + 1, :] for i in range(KINDS)],
    )


def part(x, n, h):
    return x[n * CH : (n + 1) * CH, h * CH : (h + 1) * CH]


def tile(h):
    return slice(h * CH, (h + 1) * CH)


def summed(x, weights):
    high = x.astype(bf16)
    rest = x - high.astype(f32)
    middle = rest.astype(bf16)
    low = (rest - middle.astype(f32)).astype(bf16)
    n = x.shape[0]
    r = lax.dot_general(
        jnp.concatenate([high, middle, low], axis=0), weights, (((1,), (0,)), ((), ())), preferred_element_type=f32
    )
    return r[:n] + r[n : 2 * n] + r[2 * n :]


def per_head(ref, count):
    row = lax.broadcasted_iota(jnp.int32, (count, CH), 0)
    total = jnp.zeros((count, CH), f32)
    for h in range(count):
        total = jnp.where(row == h, ref[h], total)
    return total


def setup_phase(
    has_prev, swaps, a_log, dt_bias, beta_logit, gate_logit, doc_ids, beta_got, gate_got, ids_got,
    masks, docs, rows, betas, factors,
):
    blocks = doc_ids.shape[0]
    steps = rows.shape[0]
    hv = beta_logit.shape[0]
    heads = hv // steps
    row, col = iota(0), iota(1)
    before = jnp.where(has_prev, ids_got[blocks - 1 :].astype(f32) + 1.0, 0.0)
    ids = jnp.concatenate(
        [before, doc_ids[...].astype(f32) + 1.0, jnp.zeros((8 - 1 - blocks, CH), f32)], axis=0
    )
    lane = lax.broadcasted_iota(jnp.int32, (8, CH), 1)
    same = []
    for d in range(1, TAPS):
        moved = pltpu.roll(ids, d, 1)
        moved = jnp.where(lane < d, pltpu.roll(moved, 1, 0), moved)
        same.append((moved == ids).astype(f32))
    rate = -jnp.exp(per_head(a_log, hv))
    bias = per_head(dt_bias, hv)
    logs = []
    for n in range(blocks):
        cols = columns(jnp.concatenate([x[n + 1 : n + 2] for x in same] + [ids[n + 1 : n + 2]], axis=0))
        for d in range(TAPS - 1):
            masks[d, n * CH : (n + 1) * CH] = jnp.broadcast_to(cols[:, d : d + 1], (CH, CH))
        here = (cols[:, TAPS - 1 : TAPS] == ids[n + 1 : n + 2]) & (row >= col)
        docs[n] = jnp.where(here, 1.0, 0.0)
        beta = jnp.where(swaps[n] > 0, beta_got[...], beta_logit[:, tile(n)]).astype(f32)
        gate = jnp.where(swaps[n] > 0, gate_got[...], gate_logit[:, tile(n)]).astype(f32) + bias
        betas[n] = sigmoid(beta)
        factors[n] = rate * sigmoid(gate)
        logs.append(rate * (jnp.maximum(gate, 0.0) + jnp.log1p(jnp.exp(-jnp.abs(gate)))))
    sums = summed(jnp.concatenate(logs, axis=0), (row <= col).astype(bf16))
    for n in range(blocks):
        doc = ids[n + 1 : n + 2]
        c = sums[n * hv : (n + 1) * hv]
        s = jnp.where(doc == ids[n : n + 1, CH - 1 :], jnp.exp(c), 0.0)
        w = jnp.where(doc == doc[:, CH - 1 :], jnp.exp(jnp.minimum(c[:, CH - 1 :] - c, 0.0)), 0.0)
        beta = betas[n]
        for i, x in enumerate((beta, c, s, w, beta * s)):
            for j in range(steps):
                rows[j, n, i * heads : (i + 1) * heads] = x[j * heads : (j + 1) * heads]


def forward_phase(
    j, first, swaps, q_raw, k_raw, v_raw, g_raw, q_taps, k_taps, v_taps,
    q_got, k_got, v_got, g_got, q_halo, k_halo, v_halo, masks, docs, rows,
    q_scale, k_scale, v_scale, v_out, qn_out, kn_out, grad_out,
    inv_out, decay_out, ub_out, ws_out, pdo_out, kk_out, qk_out, maps, affs, w_buf,
):
    keys = q_raw.shape[1] // CH
    heads = v_raw.shape[1] // CH
    rep = heads // keys
    blocks = q_raw.shape[0] // CH
    mask = [masks[d] for d in range(TAPS - 1)]
    tail = 2 * HALO

    def fetched(raw, got, h):
        parts = [jnp.where(swaps[n] > 0, got[j, :, tile(h)], raw[n * CH : (n + 1) * CH, tile(h)]) for n in range(blocks)]
        return jnp.concatenate(parts, axis=0)

    def activate(raw, got, halo, taps, h):
        own = raw[SWAP - tail : SWAP, tile(h)]
        before = jnp.where(swaps[0] > 0, own, halo[j, :, tile(h)]).astype(f32)[HALO:]
        x = conv(fetched(raw, got, h).astype(f32), before, taps[:, tile(h)], mask)
        sig = sigmoid(x)
        u = x * sig
        return u, sig + u * (1.0 - sig)

    def unit(raw, got, halo, taps, h, scale, out, scale_out):
        u, slope = activate(raw, got, halo, taps, h)
        factor = scale / jnp.sqrt(rowsum(u * u) + GUARD)
        y = u * factor
        out[j, :, tile(h)] = y
        scale_out[j, :, tile(h)] = slope * factor
        return y

    kn = [unit(k_raw, k_got, k_halo, k_taps, h, 1.0, kn_out, k_scale) for h in range(keys)]
    qn = [unit(q_raw, q_got, q_halo, q_taps, h, SCALE, qn_out, q_scale) for h in range(keys)]
    row, col = iota(0), iota(1)
    eye = (row == col).astype(f32)
    units = []
    for n in range(blocks):
        flat = rows[j, n]
        cols = columns(flat)
        for h in range(keys):
            q, k = qn[h][n * CH : (n + 1) * CH], kn[h][n * CH : (n + 1) * CH]
            both = mm_nt(jnp.concatenate([k, q], axis=0), k)
            kk, qk = both[:CH], both[CH:]
            kk_out[j, n * keys + h] = kk
            qk_out[j, n * keys + h] = qk
            q_t, k_t = q.T, k.T
            for e in range(h * rep, (h + 1) * rep):
                (beta, c, s, w, bs), (beta_r, c_r, s_r, w_r, bs_r) = head_scalars(cols, flat, e, heads)
                decay = jnp.exp(jnp.minimum(c - c_r, 0.0)) * docs[n]
                decay_out[j, n * heads + e] = decay
                low = jnp.where(row > col, beta * decay * kk, 0.0)
                units.append((n, e, low, decay * qk, beta, bs * k, k_t * w_r, s_r * q_t, s_r[:, CH - 1 :]))
    values, by_do = {}, {}

    def value(e):
        u, slope = activate(v_raw, v_got, v_halo, v_taps, e)
        v_out[j, :, tile(e)] = u
        v_scale[j, :, tile(e)] = slope
        values[e] = u

    def output(u):
        n, e, p, sq_t = u[0], u[1], u[3], u[7]
        do = jnp.where(swaps[n] > 0, g_got[j, :, tile(e)], g_raw[n * CH : (n + 1) * CH, tile(e)])
        grad_out[j, n * CH : (n + 1) * CH, tile(e)] = do
        by_do[n, e] = mm_half(jnp.concatenate([p.T, sq_t], axis=0), do)
        pdo_out[j, n * heads + e] = by_do[n, e][:CH]

    fillers = [functools.partial(output, u) for u in units] + [functools.partial(value, e) for e in range(heads)]
    inv = inverse_blocks([u[2] for u in units], BASE, fillers)
    size = BASE.bit_length() - 1
    while (1 << size) < CH:
        near = ((row >> (size + 1)) == (col >> (size + 1))) & ((row >> size) != (col >> size))
        width = 1 << size
        half = [mm(odd_blocks(jnp.where(near, u[2], 0.0), width), t) for u, t in zip(units, inv)]
        odds = [odd_blocks(t, width) for t in inv]
        odds = [t - mm(t, with_odd(None, h, width)) for t, h in zip(odds, half)]
        inv = [with_odd(t, o, width) for t, o in zip(inv, odds)]
        size += 1
    solved = []
    for (n, e, low, p, beta, bsk, kw_t, sq_t, s_last), t in zip(units, inv):
        inv_out[j, n * heads + e] = t
        ub = mm(t, beta * values[e][n * CH : (n + 1) * CH])
        ws = mm(t, bsk)
        ub_out[j, n * heads + e] = ub
        ws_out[j, n * heads + e] = ws
        solved.append((ub, ws))
    result = {}
    for (n, e, low, p, beta, bsk, kw_t, sq_t, s_last), (ub, ws) in zip(units, solved):
        a = mm(kw_t, ub)
        m = s_last * eye - mm(kw_t, ws)
        g = by_do[n, e][CH:] - mm(ws.T, by_do[n, e][:CH])
        result[n, e] = (m, m.T, a, g)
    for e in range(heads):
        m0, m0_t, a0, g0 = result[0, e]
        m1, m1_t, a1, g1 = result[1, e]
        for i, x in enumerate((m0, m1, m1_t, m0_t)):
            maps[j, e, i] = x
        for i, x in enumerate((a0, a1, g1, g0)):
            affs[j, e, i] = x
        w_buf[j, e] = jnp.where(first, a1, g0) + mm(jnp.where(first, m1, m0_t), jnp.where(first, a0, g1))


def spill_rows(da, taps, mask):
    zeros = jnp.zeros_like(da)
    total = zeros
    for d in range(1, TAPS):
        ext = jnp.concatenate([da * mask[d - 1][:HALO], zeros], axis=0)
        total = total + taps[TAPS - 1 - d : TAPS - d, :] * pltpu.roll(ext, 2 * HALO - d, 0)[HALO:]
    return total


def backward_phase(
    send, j, first, other, q_taps, k_taps, v_taps, masks, rows,
    q_scale, k_scale, v_scale, v_all, qn, kn, seq_grad, inv, decays, ub_in, ws_in, pdo_in, kk_in, qk_in,
    maps, affs, y_buf, s_buf, z_got, out, q_body, k_body, v_body, q_tail, k_tail, v_tail, spill, row_grads,
):
    tokens = qn.shape[1]
    blocks = tokens // CH
    keys = qn.shape[2] // CH
    heads = v_all.shape[2] // CH
    rep = heads // keys
    row, col = iota(0), iota(1)
    states, leaving = [], []
    for e in range(heads):
        y, s1, z = y_buf[j, e], s_buf[j, e], z_got[j, e]
        t1 = affs[j, e, other] + mm(maps[j, e, other], z)
        states.append((jnp.where(first, y, z), jnp.where(first, s1, t1)))
        leaving.append((jnp.where(first, t1, s1), jnp.where(first, z, y)))
    info = []
    for n in range(blocks):
        flat = rows[j, n]
        info.append((flat, columns(flat)))
    order = [(n, e) for n in range(blocks) for e in range(heads)]
    work = {}

    def at(ref, n, h):
        return ref[j, n * CH : (n + 1) * CH, tile(h)]

    for n, e in order:
        flat, cols = info[n]
        (beta, c, s, w, bs), rs = head_scalars(cols, flat, e, heads)
        i = n * heads + e
        q, k = at(qn, n, e // rep), at(kn, n, e // rep)
        st, ds_out = states[e][n], leaving[e][n]
        by_st = mm(jnp.concatenate([ws_in[j, i], q], axis=0), st)
        u = ub_in[j, i] - by_st[:CH]
        du = pdo_in[j, i] + mm(k * w, ds_out)
        work[n, e] = (by_st[CH:], u, du)
    for n, e in order:
        flat, cols = info[n]
        (beta, c, s, w, bs), rs = head_scalars(cols, flat, e, heads)
        i = n * heads + e
        qs, u, du = work[n, e]
        o = s * qs + mm(decays[j, i] * qk_in[j, n * keys + e // rep], u)
        out[n * CH : (n + 1) * CH, tile(e)] = o.astype(bf16)
        work[n, e] = (qs, u, mm(inv[j, i].T, du))
    dqs, dks, dvs = {}, {}, {}
    none = jnp.zeros((CH, CH), bf16)
    mask = [masks[d] for d in range(TAPS - 1)]

    def slope(n, h, grads, y_ref, scale_ref, gain):
        da = grads[n, h]
        if y_ref is not None:
            y = at(y_ref, n, h)
            da = da - y * (rowsum(y * da) * float(gain))
        return da * at(scale_ref, n, h)

    kinds = (
        (dqs, keys, q_taps, q_body, q_tail, qn, q_scale, DK),
        (dks, keys, k_taps, k_body, k_tail, kn, k_scale, 1),
        (dvs, heads, v_taps, v_body, v_tail, None, v_scale, 1),
    )
    slopes = {}
    for n in range(blocks):
        flat, cols = info[n]
        packed = jnp.zeros((CH, CH), f32)
        minus = []
        for h in range(keys):
            q, k = at(qn, n, h), at(kn, n, h)
            kk, qk = kk_in[j, n * keys + h], qk_in[j, n * keys + h]
            dqk_sum = dkk_sum = dq = dk = 0.0
            for e in range(h * rep, (h + 1) * rep):
                (beta, c, s, w, bs), rs = head_scalars(cols, flat, e, heads)
                s_last = rs[2][:, CH - 1 :]
                i = n * heads + e
                qs, u, y = work[n, e]
                st, ds_out = states[e][n], leaving[e][n]
                do_half = at(seq_grad, n, e)
                do = do_half.astype(f32)
                y_high, y_low = split(y)
                do_y = jnp.concatenate(
                    [jnp.concatenate([do_half, y_high], axis=0), jnp.concatenate([none, y_low], axis=0)], axis=1
                )
                by_u = mm_nt_split(do_y, u)
                by_s = mm_nt_split(do_y, st)
                dos, zneg = by_s[:CH], by_s[CH:]
                dkw = mm_nt(u, ds_out)
                decay = decays[j, i]
                dpd = by_u[:CH] * decay
                dls = by_u[CH:] * jnp.where(row > col, decay, 0.0)
                dlb = dls * kk
                f = dpd * qk - beta * dlb
                zk = zneg * k
                wk = w * (dkw * k)
                dbeta = rowsum(y * at(v_all, n, e) - s * zk - dlb)
                extra = jnp.sum(rowsum(wk + s_last * (ds_out * st)), axis=0, keepdims=True)
                dc = rowsum(f + s * (do * qs) - bs * zk - wk)
                dc = dc + jnp.where(row[:, :1] == CH - 1, extra, 0.0)
                packed = jnp.where(col == e, dbeta, packed)
                packed = jnp.where(col == heads + e, dc, packed)
                minus.append(jnp.sum(f, axis=0, keepdims=True))
                dqk_sum = dqk_sum + dpd
                dkk_sum = dkk_sum + beta * dls
                dq = dq + s * dos
                dk = dk + w * dkw - bs * zneg
                dvs[n, e] = beta * y
            by_k = mm(jnp.concatenate([dqk_sum, dkk_sum + dkk_sum.T], axis=0), k)
            dqs[n, h] = dq + by_k[:CH]
            dks[n, h] = dk + mm(dqk_sum.T, q) - by_k[CH:]
        row_grads[j, n] = packed.T[: 2 * heads] - jnp.concatenate([jnp.zeros((heads, CH), f32)] + minus, axis=0)
        at_col = 0
        for kind, (grads, count, taps, body_out, tail_out, y_ref, scale_ref, gain) in enumerate(kinds):
            for h in range(count):
                slopes[kind, n, h] = slope(n, h, grads, y_ref, scale_ref, gain)
                if n == 0:
                    spill[j, :, at_col : at_col + CH] = spill_rows(slopes[kind, n, h][:HALO], taps[:, tile(h)], mask)
                at_col += CH
        if n == 0:
            send()
    for kind, (grads, count, taps, body_out, tail_out, y_ref, scale_ref, gain) in enumerate(kinds):
        for h in range(count):
            da = jnp.concatenate([slopes[kind, n, h] for n in range(blocks)], axis=0)
            full = conv_back(da, taps[:, tile(h)], mask)
            body_out[j, :, tile(h)] = full[:tokens].astype(bf16)
            tail_out[j, :, tile(h)] = full[tokens - 2 * HALO : tokens]


def fused_kernel(ctxs, steps, *refs):
    swap_ref, a_log, dt_bias, beta_logit, gate_logit, doc_ids = refs[:6]
    taps, sources, refs = refs[6:9], refs[9:16], refs[16:]
    results, beta_grad, gate_grad, refs = refs[:4], refs[4], refs[5], refs[6:]
    raws, tap_rows, out, refs = refs[:4], refs[4:7], refs[7], refs[8:]
    gots, halos, (beta_got, gate_got, ids_got), refs = refs[:4], refs[4:7], refs[7:10], refs[10:]
    (masks, docs, rows, betas, factors), refs = refs[:5], refs[5:]
    saved, refs = refs[:14], refs[14:]
    (maps, affs, w_buf, w_got, x_buf, y_buf, s_buf, z_buf, z_got), refs = refs[:9], refs[9:]
    bodies, tails, (spill, spill_got, row_grads), refs = refs[:3], refs[3:6], refs[6:9], refs[9:]
    load_s, store_s, refs = refs[0], refs[1], refs[2:]
    swap_s, swap_r, hop_s, hop_r, pair_s, pair_r, spill_s, spill_r, got_s, got_r, halo_s, halo_r, few_s, few_r = refs
    heads = w_buf.shape[1]
    tokens = raws[0].shape[1]
    core = lax.axis_index("pair")
    ctx = lax.axis_index("ctx")
    first = core == 0
    mine, other = 2 * core, 2 - 2 * core
    peer_ctx = jnp.where(first, ctx - 1, ctx + 1)
    has_peer = (peer_ctx >= 0) & (peer_ctx < ctxs)
    has_prev = jnp.logical_not(first) | has_peer
    has_next = first | has_peer
    partner = {"pair": 1 - core}
    peer = {"ctx": jnp.clip(peer_ctx, 0, ctxs - 1), "pair": 1 - core}
    following = {"ctx": jnp.clip(ctx + core, 0, ctxs - 1), "pair": 1 - core}
    previous = {"ctx": jnp.clip(ctx - 1 + core, 0, ctxs - 1), "pair": 1 - core}
    swap_flag = swap_ref[0]
    swaps = [jnp.where(first, 0, swap_flag), jnp.where(first, swap_flag, 0)]

    def remote(src, dst, send, recv, device):
        return pltpu.make_async_remote_copy(src, dst, send, recv, device_id=device, device_id_type=pl.DeviceIdType.MESH)

    def swap(j):
        return remote(w_buf.at[j], w_got.at[j], swap_s.at[j], swap_r.at[j], partner)

    def hop(j):
        return remote(x_buf.at[j], y_buf.at[j], hop_s.at[j], hop_r.at[j], peer)

    def pair(j):
        return remote(z_buf.at[j], z_got.at[j], pair_s.at[j], pair_r.at[j], partner)

    def spilled(j):
        return remote(spill.at[j], spill_got.at[j], spill_s.at[j], spill_r.at[j], previous)

    start = pl.multiple_of(jnp.where(first, SWAP, 0), SWAP)

    def exchanged(i, j):
        width = gots[i].shape[2]
        at = pl.multiple_of(j * width, CH)
        return remote(
            sources[i].at[pl.ds(start, SWAP), pl.ds(at, width)], gots[i].at[j], got_s.at[i, j], got_r.at[i, j], partner
        )

    def neighbour(i, j):
        width = halos[i].shape[2]
        at = pl.multiple_of(j * width, CH)
        return remote(
            sources[i].at[pl.ds(tokens - 2 * HALO, 2 * HALO), pl.ds(at, width)], halos[i].at[j], halo_s.at[i, j],
            halo_r.at[i, j], following,
        )

    def loaded(i, j):
        width = raws[i].shape[2]
        at = pl.multiple_of(j * width, CH)
        return pltpu.make_async_copy(sources[i].at[:, pl.ds(at, width)], raws[i].at[j], load_s.at[i, j])

    def stored(i, j):
        held = (out, *bodies)[i]
        width = held.shape[2]
        at = pl.multiple_of(j * width, CH)
        return pltpu.make_async_copy(held.at[j], results[i].at[:, pl.ds(at, width)], store_s.at[i, j])

    def logits(i):
        return remote(sources[4 + i].at[:, pl.ds(start, SWAP)], (beta_got, gate_got)[i], few_s.at[i], few_r.at[i], partner)

    ids_copy = remote(sources[6], ids_got, few_s.at[2], few_r.at[2], following)

    def fetch_rows(j):
        for i in range(4):
            exchanged(i, j).start()

        @pl.when(has_next)
        def _():
            for i in range(3):
                neighbour(i, j).start()

    def advance(j, at, got):
        mid = [affs[j, e, at] + mm(maps[j, e, at], got[j, e]) for e in range(heads)]
        return mid, [affs[j, e, at + 1] + mm(maps[j, e, at + 1], mid[e]) for e in range(heads)]

    def chains(step, over, back):
        if over:
            swap(step - 1).wait_recv()
            mid, end = advance(step - 1, other, w_got)
            for e in range(heads):
                x_buf[step - 1, e] = end[e]

            @pl.when(has_peer)
            def _():
                hop(step - 1).start()

        if back:
            @pl.when(has_peer)
            def _():
                hop(step - 2).wait_recv()

            @pl.when(jnp.logical_not(has_peer))
            def _():
                y_buf[step - 2] = jnp.zeros(y_buf.shape[1:], f32)

            mid, end = advance(step - 2, mine, y_buf)
            for e in range(heads):
                s_buf[step - 2, e] = mid[e]
                z_buf[step - 2, e] = end[e]
            pair(step - 2).start()

    for i in range(4):
        loaded(i, 0).start()
    barrier = pltpu.get_barrier_semaphore()
    pl.semaphore_signal(barrier, inc=1, device_id=partner, device_id_type=pl.DeviceIdType.MESH)

    @pl.when(has_peer)
    def _():
        pl.semaphore_signal(barrier, inc=1, device_id=peer, device_id_type=pl.DeviceIdType.MESH)

    pl.semaphore_wait(barrier, jnp.where(has_peer, 2, 1))

    @pl.when(has_next)
    def _():
        ids_copy.start()

    for i in range(2):
        logits(i).start()
    fetch_rows(0)

    for j in range(1, steps):
        for i in range(4):
            loaded(i, j).start()
    for i in range(3):
        width = tap_rows[i].shape[2]
        for j in range(steps):
            tap_rows[i][j] = taps[i][:, j * width : (j + 1) * width].astype(f32)

    @pl.when(has_prev)
    def _():
        ids_copy.wait_recv()

    @pl.when(jnp.logical_not(has_prev))
    def _():
        ids_got[...] = jnp.zeros(ids_got.shape, jnp.int32)
        for halo in halos:
            halo[...] = jnp.zeros(halo.shape, bf16)

    for i in range(2):
        logits(i).wait_recv()
    setup_phase(
        has_prev, swaps, a_log, dt_bias, beta_logit, gate_logit, doc_ids, beta_got, gate_got, ids_got,
        masks, docs, rows, betas, factors,
    )

    def ahead(step, carry):
        for i in range(4):
            loaded(i, step).wait()
            exchanged(i, step).wait_recv()

        @pl.when(has_prev)
        def _():
            for i in range(3):
                neighbour(i, step).wait_recv()

        @pl.when(step < steps - 1)
        def _():
            fetch_rows(step + 1)

        forward_phase(
            step, first, swaps, *[x.at[step] for x in raws], *[x.at[step] for x in tap_rows], *gots, *halos, masks, docs,
            rows, *saved, maps, affs, w_buf,
        )
        swap(step).start()

        @pl.when(step == 1)
        def _():
            chains(step, True, False)

        @pl.when(step >= 2)
        def _():
            chains(step, True, True)

        return carry

    def emit(j):
        @pl.when(has_next)
        def _():
            spilled(j).wait_recv()

        @pl.when(jnp.logical_not(has_next))
        def _():
            spill_got[j] = jnp.zeros(spill_got.shape[1:], f32)

        at = 0
        for i, (held, tail) in enumerate(zip(bodies, tails)):
            width = held.shape[2]
            last = tail[j]
            last = jnp.concatenate([last[:HALO], last[HALO:] + spill_got[j, :, at : at + width]], axis=0)
            held[j, tokens - 2 * HALO :] = last.astype(bf16)
            stored(i + 1, j).start()
            at += width

    def back(j, carry):
        pair(j).wait_recv()
        def send():
            @pl.when(has_prev)
            def _():
                spilled(j).start()

        backward_phase(
            send, j, first, other, *[x.at[j] for x in tap_rows], masks, rows, *saved, maps, affs, y_buf, s_buf, z_got, out.at[j],
            *bodies, *tails, spill, row_grads,
        )
        stored(0, j).start()

        @pl.when(j == 0)
        def _():
            chains(steps, True, True)

        @pl.when(j == 1)
        def _():
            chains(steps + 1, False, True)

        @pl.when(j >= 1)
        def _():
            emit(j - 1)

        return carry

    lax.fori_loop(0, steps, ahead, 0)
    lax.fori_loop(0, steps, back, 0)
    blocks = tokens // CH
    weights = (iota(0) >= iota(1)).astype(bf16)
    for n in range(blocks):
        dbeta = jnp.concatenate([row_grads[j, n, :heads] for j in range(steps)], axis=0)
        dc = jnp.concatenate([row_grads[j, n, heads:] for j in range(steps)], axis=0)
        beta = betas[n]
        beta_grad[:, tile(n)] = (dbeta * beta * (1.0 - beta)).astype(bf16)
        gate_grad[:, tile(n)] = (summed(dc, weights) * factors[n]).astype(bf16)
    emit(steps - 1)
    for i in range(2):
        logits(i).wait_send()

    @pl.when(has_next)
    def _():
        ids_copy.wait_send()

    for j in range(steps):
        swap(j).wait_send()
        pair(j).wait_send()
        for i in range(4):
            stored(i, j).wait()
            exchanged(i, j).wait_send()

        @pl.when(has_peer)
        def _():
            hop(j).wait_send()

        @pl.when(has_next)
        def _():
            for i in range(3):
                neighbour(i, j).wait_send()

        @pl.when(has_prev)
        def _():
            spilled(j).wait_send()


def join_kernel(m, a, g, a_in, g_in, a_out, g_out):
    for e in range(m.shape[0]):
        here = m[e]
        a_out[e] = a[e] + mm(here, a_in[e])
        g_out[e] = g[e] + mm(here.T, g_in[e])


def norm_back(dy, a, scale):
    sig = sigmoid(a)
    u = a * sig
    inverse = 1.0 / jnp.sqrt(rowsum(u * u) + GUARD)
    y = u * inverse
    dy = dy * scale
    du = (dy - y * rowsum(y * dy)) * inverse
    return du * (sig + u * (1.0 - sig))


def main_kernel(
    a_q, a_k, a_v, qn, kn, seq_grad, inv, kk_in, qk_in, pdo_in, q_taps, k_taps, v_taps, masks, docs, rows,
    s_in, d_in, out, q_grad, k_grad, v_grad, q_end, k_end, v_end, q_spill, k_spill, v_spill, row_grads,
):
    tokens = a_q.shape[0]
    blocks = tokens // CH
    heads = a_v.shape[1] // CH
    row, col = iota(0), iota(1)
    va = a_v[...]
    v_sig = sigmoid(va)
    v_all = va * v_sig
    info = []
    for n in range(blocks):
        q = qn[n * CH : (n + 1) * CH, :]
        k = kn[n * CH : (n + 1) * CH, :]
        info.append((q, k, q.T, k.T, rows[0, n], columns(rows[0, n])))
    fwd = {}
    carried = [s_in[e] for e in range(heads)]
    for n in range(blocks):
        q, k, q_t, k_t, flat, cols = info[n]
        kq = jnp.concatenate([k, q], axis=0)
        for e in range(heads):
            beta, c, s, w = [cols[:, 4 * e + i : 4 * e + i + 1] for i in range(4)]
            beta_r, c_r, s_r, w_r = [flat[4 * e + i : 4 * e + i + 1, :] for i in range(4)]
            s_last = s_r[:, CH - 1 :]
            v = v_all[n * CH : (n + 1) * CH, e * CH : (e + 1) * CH]
            decay = jnp.exp(jnp.minimum(c - c_r, 0.0)) * docs[n]
            p = decay * qk_in[0, n]
            st = carried[e]
            kqs = mm(kq, st)
            ks, qs = kqs[:CH], kqs[CH:]
            t = inv[0, e, n]
            u = mm(t, beta * (v - s * ks))
            o = s * qs + mm(p, u)
            out[n * CH : (n + 1) * CH, e * CH : (e + 1) * CH] = o.astype(bf16)
            if n + 1 < blocks:
                carried[e] = s_last * st + mm(k_t * w_r, u)
            fwd[n, e] = (st, u, qs, decay, p, v)
    grads = [d_in[e] for e in range(heads)]
    dqs, dks, dvs = [None] * blocks, [None] * blocks, {}
    for n in reversed(range(blocks)):
        q, k, q_t, k_t, flat, cols = info[n]
        packed = jnp.zeros((CH, CH), f32)
        dqk_sum = dkk_sum = dq = dk = 0.0
        for e in range(heads):
            beta, c, s, w = [cols[:, 4 * e + i : 4 * e + i + 1] for i in range(4)]
            beta_r, c_r, s_r, w_r = [flat[4 * e + i : 4 * e + i + 1, :] for i in range(4)]
            s_last = s_r[:, CH - 1 :]
            st, u, qs, decay, p, v = fwd[n, e]
            ds_out = grads[e]
            do_half = seq_grad[n * CH : (n + 1) * CH, e * CH : (e + 1) * CH]
            do = do_half.astype(f32)
            du = pdo_in[0, e, n] + mm(k * w, ds_out)
            y = mm(inv[0, e, n].T, du)
            do_y = jnp.concatenate([do, y], axis=0)
            by_u = mm_nt(do_y, u)
            by_s = mm_nt(do_y, st)
            dp, dl = by_u[:CH], -by_u[CH:]
            dos, z = by_s[:CH], -by_s[CH:]
            dkw = mm_nt(u, ds_out)
            strict = jnp.where(row > col, decay, 0.0)
            bk = strict * kk_in[0, n]
            dlb = dl * bk
            f = dp * p + beta * dlb
            zk = z * k
            wk = w * (dkw * k)
            bs = beta * s
            dbeta = rowsum(y * v + s * zk + dlb)
            extra = jnp.sum(rowsum(wk + s_last * (ds_out * st)), axis=0, keepdims=True)
            dc = rowsum((f - f.T) + s * (do * qs) + bs * zk - wk)
            dc = dc + jnp.where(row[:, :1] == CH - 1, extra, 0.0)
            packed = jnp.where(col == 2 * e, dbeta, packed)
            packed = jnp.where(col == 2 * e + 1, dc, packed)
            dqk_sum = dqk_sum + dp * decay
            dkk_sum = dkk_sum + dl * (beta * strict)
            dq = dq + s * dos
            dk = dk + w * dkw + bs * z
            dvs[n, e] = beta * y
            if n > 0:
                grads[e] = mm_half(q_t * s_r, do_half) + s_last * ds_out - mm(k_t * (beta_r * s_r), y)
        dqs[n] = dq + mm(dqk_sum, k)
        dks[n] = dk + mm(dqk_sum.T, q) + mm(dkk_sum + dkk_sum.T, k)
        row_grads[0, n] = packed.T[: row_grads.shape[2]]
    dq = jnp.concatenate(dqs, axis=0)
    dk = jnp.concatenate(dks, axis=0)
    dv = jnp.concatenate(
        [jnp.concatenate([dvs[n, e] for e in range(heads)], axis=1) for n in range(blocks)], axis=0
    )
    daq = norm_back(dq, a_q[...], SCALE)
    dak = norm_back(dk, a_k[...], 1.0)
    dav = dv * (v_sig + v_all * (1.0 - v_sig))
    for da, taps, grad, end, spill in (
        (daq, q_taps, q_grad, q_end, q_spill),
        (dak, k_taps, k_grad, k_end, k_spill),
        (dav, v_taps, v_grad, v_end, v_spill),
    ):
        full = conv_back(da, taps, masks)
        grad[...] = full[:tokens].astype(bf16)
        end[...] = full[tokens - HALO : tokens]
        spill[...] = full[tokens:]


def shifted(array, by):
    peers = lax.axis_size(SEQ)
    return lax.ppermute(array, SEQ, [(i, i + by) for i in range(peers) if 0 <= i + by < peers])


def tri(upper):
    i = jnp.arange(CH)
    return ((i[:, None] <= i[None, :]) if upper else (i[:, None] >= i[None, :])).astype(f32)


def sds(shape, dtype=f32):
    return jax.ShapeDtypeStruct(shape, dtype)


def staged_call(inputs, hk, hv, tokens, hops):
    blocks = tokens // CH
    rep = hv // hk
    qw = hk * DK
    vw = rep * DK
    col = lambda rows_, width, off=0: pl.BlockSpec((rows_, width), lambda i, off=off, width=width: (0, off // width + i))
    fixed = lambda shape: pl.BlockSpec(shape, lambda i: (0,) * len(shape))
    per = lambda shape: pl.BlockSpec(shape, lambda i: (i,) + (0,) * (len(shape) - 1))
    taps_specs = [col(TAPS, DK), col(TAPS, DK), col(TAPS, vw)]
    common_specs = taps_specs + [
        fixed((TAPS - 1, tokens, CH)),
        fixed((blocks, CH, CH)),
        per((1, blocks, rep * 4, CH)),
    ]
    params = pltpu.CompilerParams(dimension_semantics=("arbitrary",), vmem_limit_bytes=48 * 2**20)
    saved_specs = [
        col(tokens, DK), col(tokens, DK), col(tokens, vw), col(tokens, DK), col(tokens, DK), col(tokens, vw),
        per((1, rep, blocks, CH, CH)), per((1, blocks, CH, CH)), per((1, blocks, CH, CH)),
        per((1, rep, blocks, CH, CH)),
    ]
    saved_shapes = [
        sds((tokens, qw)), sds((tokens, qw)), sds((tokens, hv * DK)), sds((tokens, qw)), sds((tokens, qw)),
        sds((tokens, hv * DK), bf16), sds((hk, rep, blocks, CH, CH)), sds((hk, blocks, CH, CH)),
        sds((hk, blocks, CH, CH)), sds((hk, rep, blocks, CH, CH)),
    ]
    state_spec = per((rep, DK, DK))
    state_shape = sds((hv, DK, DK))
    units = hv * blocks * 2 * 4 * CH**3
    *taps, masks, docs, rows = inputs[12:]
    in_specs = [
        pl.BlockSpec(memory_space=pltpu.SMEM),
        col(tokens, DK), col(tokens, DK), col(tokens, vw), col(tokens, vw),
        col(SWAP, DK), col(SWAP, DK, qw), col(SWAP, vw, 2 * qw), col(SWAP, vw, 2 * qw + hv * DK),
        col(HALO, DK), col(HALO, DK, qw), col(HALO, vw, 2 * qw),
    ] + common_specs
    prepare_cost = pl.CostEstimate(flops=22 * units, bytes_accessed=24 * 2**20, transcendentals=2**20)
    prepared = pl.pallas_call(
        prepare_kernel,
        grid=(hk,),
        in_specs=in_specs,
        out_specs=saved_specs + [state_spec] * 3,
        out_shape=saved_shapes + [state_shape] * 3,
        compiler_params=params,
        cost_estimate=prepare_cost,
        name="prepare",
    )(*inputs)
    saved, (m, a, g) = prepared[:10], prepared[10:]
    join = pl.pallas_call(
        join_kernel,
        grid=(hk,),
        in_specs=[state_spec] * 5,
        out_specs=[state_spec] * 2,
        out_shape=[state_shape] * 2,
        compiler_params=params,
        cost_estimate=pl.CostEstimate(flops=hv * 16 * CH**3, bytes_accessed=7 * 2**20, transcendentals=0),
        name="join",
    )
    s_in, d_in = a, g
    for step in range(hops):
        s_in, d_in = shifted(s_in, 1), shifted(d_in, -1)
        if step < hops - 1:
            s_in, d_in = join(m, a, g, s_in, d_in)

    ends = [col(HALO, DK), col(HALO, DK), col(HALO, vw)]
    end_shapes = [sds((HALO, qw)), sds((HALO, qw)), sds((HALO, hv * DK))]
    return pl.pallas_call(
        main_kernel,
        grid=(hk,),
        in_specs=saved_specs + common_specs + [state_spec] * 2,
        out_specs=[col(tokens, vw), col(tokens, DK), col(tokens, DK), col(tokens, vw)] + ends + ends + [per((1, blocks, 8, CH))],
        out_shape=[
            sds((tokens, hv * DK), bf16), sds((tokens, qw), bf16), sds((tokens, qw), bf16), sds((tokens, hv * DK), bf16)
        ] + end_shapes + end_shapes + [sds((hk, blocks, 8, CH))],
        compiler_params=params,
        cost_estimate=pl.CostEstimate(flops=17 * units, bytes_accessed=24 * 2**20, transcendentals=2**20),
        name="main",
    )(*saved, *taps, masks, docs, rows, s_in, d_in)


def copy_kernel(*refs):
    count = (len(refs) - 2) // 3
    held = refs[2 * count : 3 * count]
    in_sems, out_sems = refs[3 * count :]
    pieces = []
    for src, dst, mid in zip(refs[:count], refs[count : 2 * count], held):
        size = max(16, min(src.shape[0], COPY_BYTES // (2 * src.shape[1])))
        for at in range(0, src.shape[0], size):
            rows, i = pl.ds(at, size), len(pieces)
            pieces.append((
                pltpu.make_async_copy(src.at[rows], mid.at[rows], in_sems.at[i]),
                pltpu.make_async_copy(mid.at[rows], dst.at[rows], out_sems.at[i]),
            ))
    for load, store in pieces:
        load.start()
    for load, store in pieces:
        load.wait()
        store.start()
    for load, store in pieces:
        store.wait()


def copied(arrays):
    hbm = pl.BlockSpec(memory_space=pl.ANY)
    return pl.pallas_call(
        copy_kernel,
        in_specs=[hbm] * len(arrays),
        out_specs=[hbm] * len(arrays),
        out_shape=[sds(x.shape, x.dtype) for x in arrays],
        scratch_shapes=[pltpu.VMEM(x.shape, x.dtype) for x in arrays] + [pltpu.SemaphoreType.DMA((32,))] * 2,
        name="copies",
    )(*arrays)


def fused_call(
    q_raw, k_raw, v_raw, beta_logit, gate_logit, out_grad, conv_q, conv_k, conv_v, a_log, dt_bias, doc_ids, swap_blocks
):
    tokens, qw = q_raw.shape
    blocks = tokens // CH
    hk = qw // DK
    hv = v_raw.shape[1] // DK
    steps = hk // GROUP
    heads = hv // steps
    gw, vw = GROUP * DK, heads * DK
    doc_ids = doc_ids.reshape(blocks, CH)
    fixed = lambda shape: pl.BlockSpec(memory_space=pltpu.VMEM)
    smem = pl.BlockSpec(memory_space=pltpu.SMEM)
    hbm = pl.BlockSpec(memory_space=pl.ANY)
    in_specs = [smem] * 3 + [fixed(x.shape) for x in (beta_logit, gate_logit, doc_ids, conv_q, conv_k, conv_v)] + [hbm] * 7
    vm = lambda *shape: pltpu.VMEM(shape, f32)
    half = lambda *shape: pltpu.VMEM(shape, bf16)
    square = lambda *lead: vm(steps, *lead, CH, CH)
    wide = lambda width: vm(steps, tokens, width)
    units = blocks * heads
    sems = lambda *shape: pltpu.SemaphoreType.DMA(shape)
    scratch = [half(steps, tokens, gw), half(steps, tokens, gw), half(steps, tokens, vw), half(steps, tokens, vw)]
    scratch += [vm(steps, TAPS, gw), vm(steps, TAPS, gw), vm(steps, TAPS, vw), half(steps, tokens, vw)]
    scratch += [half(steps, SWAP, gw), half(steps, SWAP, gw), half(steps, SWAP, vw), half(steps, SWAP, vw)]
    scratch += [half(steps, 2 * HALO, gw), half(steps, 2 * HALO, gw), half(steps, 2 * HALO, vw)]
    scratch += [half(hv, SWAP), half(hv, SWAP), pltpu.VMEM((blocks, CH), jnp.int32)]
    scratch += [vm(TAPS - 1, tokens, CH), vm(blocks, CH, CH), vm(steps, blocks, KINDS * heads, CH)]
    scratch += [vm(blocks, hv, CH), vm(blocks, hv, CH)]
    scratch += [wide(gw), wide(gw), wide(vw), wide(vw), wide(gw), wide(gw), half(steps, tokens, vw)]
    scratch += [square(units)] * 5 + [square(blocks * GROUP)] * 2 + [square(heads, 4)] * 2 + [square(heads)] * 7
    scratch += [half(steps, tokens, gw), half(steps, tokens, gw), half(steps, tokens, vw)]
    scratch += [vm(steps, 2 * HALO, gw), vm(steps, 2 * HALO, gw), vm(steps, 2 * HALO, vw)]
    scratch += [vm(steps, HALO, 2 * gw + vw)] * 2 + [vm(steps, blocks, 2 * heads, CH)]
    scratch += [sems(4, steps)] * 2 + [sems(steps)] * 8 + [sems(4, steps)] * 2 + [sems(3, steps)] * 2 + [sems(3)] * 2
    return pl.pallas_call(
        functools.partial(fused_kernel, lax.axis_size("ctx"), steps),
        in_specs=in_specs,
        out_specs=[hbm] * 4 + [fixed((hv, tokens))] * 2,
        out_shape=[
            sds((tokens, hv * DK), bf16), sds((tokens, qw), bf16), sds((tokens, qw), bf16), sds((tokens, hv * DK), bf16),
            sds((hv, tokens), bf16), sds((hv, tokens), bf16),
        ],
        scratch_shapes=scratch,
        compiler_params=pltpu.CompilerParams(
            vmem_limit_bytes=56 * 2**20, collective_id=0, has_side_effects=True
        ),
        cost_estimate=pl.CostEstimate(
            flops=30 * hv * blocks * 8 * CH**3, bytes_accessed=8 * 2**20, transcendentals=2**21
        ),
        name="fused",
    )(
        swap_blocks, a_log, dt_bias, beta_logit, gate_logit, doc_ids, conv_q, conv_k, conv_v,
        q_raw, k_raw, v_raw, out_grad, beta_logit, gate_logit, doc_ids,
    )


def body(
    q_raw, k_raw, v_raw, beta_logit, gate_logit, out_grad, conv_q, conv_k, conv_v, a_log, dt_bias, doc_ids, swap_blocks
):
    tokens = q_raw.shape[0]
    blocks = tokens // CH
    hk = q_raw.shape[1] // DK
    hv = v_raw.shape[1] // DK
    rep = hv // hk
    shards = lax.axis_size(SEQ)
    hops = max(1, shards // DOC_PARTS)
    if hops == lax.axis_size("pair") and blocks == 2 and hk % GROUP == 0:
        return copied(
            fused_call(
                q_raw, k_raw, v_raw, beta_logit, gate_logit, out_grad, conv_q, conv_k, conv_v, a_log, dt_bias, doc_ids,
                swap_blocks,
            )
        )
    core = lax.axis_index("pair")
    swap = swap_blocks[0]
    flags = jnp.stack([jnp.where(core == 1, swap, 0), jnp.where(core == 0, swap, 0)]).astype(jnp.int32)

    start = jnp.where(core == 0, SWAP, 0)
    logits = jnp.concatenate([beta_logit, gate_logit], axis=0)
    bg_send = lax.dynamic_slice_in_dim(logits, start, SWAP, 1)
    send = jnp.concatenate(
        [lax.dynamic_slice_in_dim(x, start, SWAP, 0) for x in (q_raw, k_raw, v_raw, out_grad)], axis=1
    )
    got = lax.ppermute(send, "pair", [(0, 1), (1, 0)])
    send, bg_send, tail_ids, tails = lax.optimization_barrier(
        (send, bg_send, doc_ids[tokens - HALO :], [x[tokens - HALO :] for x in (q_raw, k_raw, v_raw)])
    )
    bg_got = lax.ppermute(bg_send, "pair", [(0, 1), (1, 0)])
    ids_col = jnp.broadcast_to((tail_ids + 1).astype(bf16)[:, None], (HALO, CH))
    tail = jnp.concatenate(tails + [ids_col], axis=1)
    before = shifted(tail, 1)
    own = jnp.concatenate([x[SWAP - HALO : SWAP] for x in (q_raw, k_raw, v_raw)], axis=1)
    chans = own.shape[1]
    halo = jnp.where(flags[0] > 0, own, before[:, :chans]).astype(f32)
    qw = hk * DK

    first = jnp.where(flags[0] > 0, bg_got, logits[:, :SWAP])
    second = jnp.where(flags[1] > 0, bg_got, logits[:, SWAP:])
    logits = jnp.concatenate([first, second], axis=1).astype(f32)
    beta = jax.nn.sigmoid(logits[:hv])
    gate = logits[hv:] + dt_bias[:, None]
    rate = -jnp.exp(a_log)[:, None]
    decay_log = rate * jax.nn.softplus(gate)
    c = jnp.dot(decay_log.reshape(hv * blocks, CH), tri(True), precision=highest).reshape(hv, blocks, CH)
    ids = doc_ids.astype(f32) + 1.0
    ext_ids = jnp.concatenate([before[:, chans].astype(f32), ids])
    doc = ids.reshape(blocks, CH)
    doc_before = ext_ids[HALO - 1 : HALO - 1 + tokens : CH]
    s = jnp.where(doc == doc_before[:, None], jnp.exp(c), 0.0)
    w = jnp.where(doc == doc[:, CH - 1 :], jnp.exp(jnp.minimum(c[:, :, CH - 1 :] - c, 0.0)), 0.0)
    rows = jnp.stack([beta.reshape(hv, blocks, CH), c, s, w], axis=2)
    rows = rows.reshape(hk, rep, blocks, 4, CH).transpose(0, 2, 1, 3, 4).reshape(hk, blocks, rep * 4, CH)
    docs = ((doc[:, :, None] == doc[:, None, :]) & (tri(False) > 0)[None]).astype(f32)
    masks = jnp.stack(
        [
            jnp.broadcast_to((ext_ids[HALO - d : HALO - d + tokens] == ids).astype(f32)[:, None], (tokens, CH))
            for d in range(1, TAPS)
        ]
    )
    taps = [x.astype(f32) for x in (conv_q, conv_k, conv_v)]

    results = staged_call(
        (flags, q_raw, k_raw, v_raw, out_grad, got, got, got, got, halo, halo, halo, *taps, masks, docs, rows), hk, hv,
        tokens, hops,
    )
    layer_out, q_grad, k_grad, v_grad = results[:4]
    spilled = shifted(jnp.concatenate(results[7:10], axis=1), -1)
    ends_out = []
    at = 0
    for grad, end in zip((q_grad, k_grad, v_grad), results[4:7]):
        width = end.shape[1]
        last = (end + spilled[:, at : at + width]).astype(bf16)
        ends_out.append(lax.dynamic_update_slice(grad, last, (tokens - HALO, 0)))
        at += width
    rg = results[10][:, :, : 2 * rep].reshape(hk, blocks, rep, 2, CH).transpose(3, 0, 2, 1, 4)
    dbeta = rg[0].reshape(hv, tokens)
    dg = jnp.dot(rg[1].reshape(hv * blocks, CH), tri(False), precision=highest).reshape(hv, tokens)
    beta_grad = dbeta * beta * (1.0 - beta)
    gate_grad = dg * rate * jax.nn.sigmoid(gate)
    return (layer_out, ends_out[0], ends_out[1], ends_out[2], beta_grad.astype(bf16), gate_grad.astype(bf16))


def solution(mesh):
    rows = P(("groups", "ctx", "pair"), "head")
    rates = P("head", ("groups", "ctx", "pair"))
    taps = P(None, "head")
    return jax.shard_map(
        body,
        mesh=mesh,
        in_specs=(
            rows, rows, rows, rates, rates, rows, taps, taps, taps, P("head"), P("head"),
            P(("groups", "ctx", "pair")), P(("groups", "ctx")),
        ),
        out_specs=(rows, rows, rows, rows, rates, rates),
        check_vma=False,
    )
```

```python
import functools
import math

import jax
import jax.numpy as jnp
from jax import lax
from jax.experimental import pallas as pl
from jax.experimental.pallas import tpu as pltpu
from jax.sharding import PartitionSpec as P

DK = 128
TAPS = 4
CH = 128
SWAP = 128
HALO = 8
GUARD = 1e-06
SCALE = 1.0 / math.sqrt(DK)
DOC_PARTS = 4
GROUP = 2
BASE = 16
KINDS = 5
COPY_BYTES = 2**17

f32 = jnp.float32
bf16 = jnp.bfloat16
highest = lax.Precision.HIGHEST
SEQ = ("ctx", "pair")


def split(x):
    high = x.astype(bf16)
    return high, (x - high.astype(f32)).astype(bf16)


def mm(a, b):
    ah, al = split(a)
    bh, bl = split(b)
    lhs = jnp.concatenate([ah, al], axis=1)
    rhs = jnp.concatenate(
        [jnp.concatenate([bh, bl], axis=1), jnp.concatenate([bh, jnp.zeros_like(bh)], axis=1)], axis=0
    )
    r = lax.dot_general(lhs, rhs, (((1,), (0,)), ((), ())), preferred_element_type=f32)
    n = b.shape[1]
    return r[:, :n] + r[:, n:]


def mm_half(a, b):
    return lax.dot_general(
        jnp.concatenate(split(a), axis=1), jnp.concatenate([b, b], axis=0), (((1,), (0,)), ((), ())),
        preferred_element_type=f32,
    )


def odd_blocks(x, size):
    return jnp.concatenate([x[i : i + size] for i in range(size, CH, 2 * size)], axis=0)


def with_odd(even, odd, size):
    parts = []
    for i in range(0, CH // 2, size):
        parts.append(jnp.zeros((size, CH), odd.dtype) if even is None else even[2 * i : 2 * i + size])
        parts.append(odd[i : i + size])
    return jnp.concatenate(parts, axis=0)


def mm_nt(a, b):
    ah, al = split(a)
    bh, bl = split(b)
    lhs = jnp.concatenate([ah, al], axis=1)
    rhs = jnp.concatenate(
        [jnp.concatenate([bh, bh], axis=1), jnp.concatenate([bl, jnp.zeros_like(bl)], axis=1)], axis=0
    )
    r = lax.dot_general(lhs, rhs, (((1,), (1,)), ((), ())), preferred_element_type=f32)
    n = b.shape[0]
    return r[:, :n] + r[:, n:]


def mm_nt_split(lhs, b):
    bh, bl = split(b)
    rhs = jnp.concatenate(
        [jnp.concatenate([bh, bh], axis=1), jnp.concatenate([bl, jnp.zeros_like(bl)], axis=1)], axis=0
    )
    r = lax.dot_general(lhs, rhs, (((1,), (1,)), ((), ())), preferred_element_type=f32)
    n = b.shape[0]
    return r[:, :n] + r[:, n:]


def iota(axis):
    return lax.broadcasted_iota(jnp.int32, (CH, CH), axis)


def rowsum(x):
    return jnp.sum(x, axis=1, keepdims=True)


def columns(rows):
    return jnp.concatenate([rows, jnp.zeros((CH - rows.shape[0], CH), f32)], axis=0).T


def sigmoid(a):
    return 1.0 / (1.0 + jnp.exp(-a))


def fetch(raw, recv, flags):
    first = raw[:SWAP, :]
    second = raw[SWAP:, :]
    got = recv[...]
    first = jnp.where(flags[0] > 0, got, first)
    second = jnp.where(flags[1] > 0, got, second)
    return jnp.concatenate([first, second], axis=0)


def conv(x, halo, taps, masks):
    ext = jnp.concatenate([halo, x], axis=0)
    width = x.shape[1] // CH
    total = taps[TAPS - 1 : TAPS, :] * x
    for d in range(1, TAPS):
        moved = pltpu.roll(ext, d, 0)[HALO:, :]
        mask = masks[d - 1]
        if width > 1:
            mask = jnp.concatenate([mask] * width, axis=1)
        total = total + taps[TAPS - 1 - d : TAPS - d, :] * (moved * mask)
    return total


def conv_back(da, taps, masks):
    width = da.shape[1] // CH
    zeros = jnp.zeros((HALO, da.shape[1]), f32)
    total = taps[TAPS - 1 : TAPS, :] * jnp.concatenate([da, zeros], axis=0)
    size = total.shape[0]
    for d in range(1, TAPS):
        mask = masks[d - 1]
        if width > 1:
            mask = jnp.concatenate([mask] * width, axis=1)
        ext = jnp.concatenate([da * mask, zeros], axis=0)
        total = total + taps[TAPS - 1 - d : TAPS - d, :] * pltpu.roll(ext, size - d, 0)
    return total


def local_maps(
    flags, q_raw, k_raw, v_raw, g_raw, q_got, k_got, v_got, g_got, q_halo, k_halo, v_halo,
    q_taps, k_taps, v_taps, masks, docs, rows,
    a_q, a_k, a_v, qn_out, kn_out, seq_grad, inv_out, kk_out, qk_out, pdo_out,
):
    blocks = q_raw.shape[0] // CH
    qa = conv(fetch(q_raw, q_got, flags).astype(f32), q_halo[...], q_taps, masks)
    ka = conv(fetch(k_raw, k_got, flags).astype(f32), k_halo[...], k_taps, masks)
    va = conv(fetch(v_raw, v_got, flags).astype(f32), v_halo[...], v_taps, masks)
    a_q[...] = qa
    a_k[...] = ka
    a_v[...] = va
    gs = fetch(g_raw, g_got, flags)
    seq_grad[...] = gs
    do_all = gs
    qu = qa * sigmoid(qa)
    ku = ka * sigmoid(ka)
    v_all = va * sigmoid(va)
    qn = qu * (SCALE / jnp.sqrt(rowsum(qu * qu) + GUARD))
    kn = ku * (1.0 / jnp.sqrt(rowsum(ku * ku) + GUARD))
    qn_out[...] = qn
    kn_out[...] = kn
    row, col = iota(0), iota(1)
    eye = (row == col).astype(f32)
    heads = v_raw.shape[1] // CH
    state = []
    for n in range(blocks):
        q = qn[n * CH : (n + 1) * CH]
        k = kn[n * CH : (n + 1) * CH]
        both = mm_nt(jnp.concatenate([k, q], axis=0), k)
        kk, qk = both[:CH], both[CH:]
        kk_out[0, n] = kk
        qk_out[0, n] = qk
        q_t, k_t = q.T, k.T
        flat = rows[0, n]
        cols = columns(flat)
        for e in range(heads):
            beta, c, s, w = [cols[:, 4 * e + i : 4 * e + i + 1] for i in range(4)]
            beta_r, c_r, s_r, w_r = [flat[4 * e + i : 4 * e + i + 1, :] for i in range(4)]
            s_last = s_r[:, CH - 1 :]
            decay = jnp.exp(jnp.minimum(c - c_r, 0.0)) * docs[n]
            low = jnp.where(row > col, beta * decay * kk, 0.0)
            do = do_all[n * CH : (n + 1) * CH, e * CH : (e + 1) * CH]
            v = v_all[n * CH : (n + 1) * CH, e * CH : (e + 1) * CH]
            state.append((n, e, low, decay * qk, do, v, k * w, (beta_r * s_r) * k_t, beta * s * k, s_r * q_t, beta * v, s_last))
    inv = []
    for item in state:
        inv.append(eye - jnp.where((row >> 1) == (col >> 1), item[2], 0.0))
    size = 1
    while (2 << size) <= CH:
        near = ((row >> (size + 1)) == (col >> (size + 1))) & ((row >> size) != (col >> size))
        width = 1 << size
        if width < 8:
            half = [mm(jnp.where(near, item[2], 0.0), t) for item, t in zip(state, inv)]
            inv = [t - mm(t, h) for t, h in zip(inv, half)]
        else:
            half = [mm(odd_blocks(jnp.where(near, item[2], 0.0), width), t) for item, t in zip(state, inv)]
            odds = [odd_blocks(t, width) for t in inv]
            odds = [t - mm(t, with_odd(None, h, width)) for t, h in zip(odds, half)]
            inv = [with_odd(t, o, width) for t, o in zip(inv, odds)]
        size += 1
    maps = {}
    for item, t in zip(state, inv):
        n, e, low, p, do, v, kw, bsk_t, bsk, sq_t, bv, s_last = item
        inv_out[0, e, n] = t
        pdo = mm_half(p.T, do)
        pdo_out[0, e, n] = pdo
        t_t = t.T
        b = mm(t_t, kw)
        cc = mm(t_t, pdo)
        b_t = b.T
        m = s_last * eye - mm(b_t, bsk)
        a = mm(b_t, bv)
        g = mm_half(sq_t, do) - mm(bsk_t, cc)
        maps[n, e] = (m, a, g)
    results = []
    for e in range(heads):
        m, a, g = maps[0, e]
        for n in range(1, blocks):
            m2, a2, g2 = maps[n, e]
            g = g + mm(m.T, g2)
            a = mm(m2, a) + a2
            m = mm(m2, m)
        results.append((m, a, g))
    return results


def prepare_kernel(*refs):
    m_out, a_out, g_out = refs[-3:]
    for e, (m, a, g) in enumerate(local_maps(*refs[:-3])):
        m_out[e] = m
        a_out[e] = a
        g_out[e] = g


def inverse_blocks(lows, size, fillers):
    regs = size // 8
    lane = lax.broadcasted_iota(jnp.int32, (8, CH), 1)
    sub = lax.broadcasted_iota(jnp.int32, (8, CH), 0)
    base = lane - lax.rem(lane, size)
    packed, inv = [], []
    for low in lows:
        rows_, eyes = [], []
        for r in range(regs):
            acc = low[8 * r : 8 * r + 8]
            for at in range(size, CH, size):
                acc = jnp.where(lane >= at, low[at + 8 * r : at + 8 * r + 8], acc)
            rows_.append(acc)
            eyes.append((lane - base == sub + 8 * r).astype(f32))
        packed.append(rows_)
        inv.append(eyes)
    fillers = list(fillers)
    every = max(1, (size - 1) // max(1, len(fillers)))
    for j in range(size - 1):
        here = j // 8
        index = base + j
        for low, t in zip(packed, inv):
            line = jnp.broadcast_to(t[here][j % 8 : j % 8 + 1], (8, CH))
            for r in range(here if j % 8 < 7 else here + 1, regs):
                t[r] = t[r] - jnp.take_along_axis(low[r], index, axis=1, mode="promise_in_bounds") * line
        if fillers and j % every == 0:
            fillers.pop(0)()
    for filler in fillers:
        filler()
    return [
        jnp.concatenate([jnp.where(base == at, x, 0.0) for at in range(0, CH, size) for x in t], axis=0) for t in inv
    ]


def head_scalars(cols, flat, e, heads):
    return (
        [cols[:, i * heads + e : i * heads + e + 1] for i in range(KINDS)],
        [flat[i * heads + e : i * heads + e + 1, :] for i in range(KINDS)],
    )


def part(x, n, h):
    return x[n * CH : (n + 1) * CH, h * CH : (h + 1) * CH]


def tile(h):
    return slice(h * CH, (h + 1) * CH)


def summed(x, weights):
    high = x.astype(bf16)
    rest = x - high.astype(f32)
    middle = rest.astype(bf16)
    low = (rest - middle.astype(f32)).astype(bf16)
    n = x.shape[0]
    r = lax.dot_general(
        jnp.concatenate([high, middle, low], axis=0), weights, (((1,), (0,)), ((), ())), preferred_element_type=f32
    )
    return r[:n] + r[n : 2 * n] + r[2 * n :]


def per_head(ref, count):
    row = lax.broadcasted_iota(jnp.int32, (count, CH), 0)
    total = jnp.zeros((count, CH), f32)
    for h in range(count):
        total = jnp.where(row == h, ref[h], total)
    return total


def setup_phase(
    has_prev, swaps, a_log, dt_bias, beta_logit, gate_logit, doc_ids, beta_got, gate_got, ids_got,
    masks, docs, rows, betas, factors,
):
    blocks = doc_ids.shape[0]
    steps = rows.shape[0]
    hv = beta_logit.shape[0]
    heads = hv // steps
    row, col = iota(0), iota(1)
    before = jnp.where(has_prev, ids_got[blocks - 1 :].astype(f32) + 1.0, 0.0)
    ids = jnp.concatenate(
        [before, doc_ids[...].astype(f32) + 1.0, jnp.zeros((8 - 1 - blocks, CH), f32)], axis=0
    )
    lane = lax.broadcasted_iota(jnp.int32, (8, CH), 1)
    same = []
    for d in range(1, TAPS):
        moved = pltpu.roll(ids, d, 1)
        moved = jnp.where(lane < d, pltpu.roll(moved, 1, 0), moved)
        same.append((moved == ids).astype(f32))
    rate = -jnp.exp(per_head(a_log, hv))
    bias = per_head(dt_bias, hv)
    logs = []
    for n in range(blocks):
        cols = columns(jnp.concatenate([x[n + 1 : n + 2] for x in same] + [ids[n + 1 : n + 2]], axis=0))
        for d in range(TAPS - 1):
            masks[d, n * CH : (n + 1) * CH] = jnp.broadcast_to(cols[:, d : d + 1], (CH, CH))
        here = (cols[:, TAPS - 1 : TAPS] == ids[n + 1 : n + 2]) & (row >= col)
        docs[n] = jnp.where(here, 1.0, 0.0)
        beta = jnp.where(swaps[n] > 0, beta_got[...], beta_logit[:, tile(n)]).astype(f32)
        gate = jnp.where(swaps[n] > 0, gate_got[...], gate_logit[:, tile(n)]).astype(f32) + bias
        betas[n] = sigmoid(beta)
        factors[n] = rate * sigmoid(gate)
        logs.append(rate * (jnp.maximum(gate, 0.0) + jnp.log1p(jnp.exp(-jnp.abs(gate)))))
    sums = summed(jnp.concatenate(logs, axis=0), (row <= col).astype(bf16))
    for n in range(blocks):
        doc = ids[n + 1 : n + 2]
        c = sums[n * hv : (n + 1) * hv]
        s = jnp.where(doc == ids[n : n + 1, CH - 1 :], jnp.exp(c), 0.0)
        w = jnp.where(doc == doc[:, CH - 1 :], jnp.exp(jnp.minimum(c[:, CH - 1 :] - c, 0.0)), 0.0)
        beta = betas[n]
        for i, x in enumerate((beta, c, s, w, beta * s)):
            for j in range(steps):
                rows[j, n, i * heads : (i + 1) * heads] = x[j * heads : (j + 1) * heads]


def forward_phase(
    j, first, swaps, q_raw, k_raw, v_raw, g_raw, q_taps, k_taps, v_taps,
    q_got, k_got, v_got, g_got, q_halo, k_halo, v_halo, masks, docs, rows,
    q_scale, k_scale, v_scale, v_out, qn_out, kn_out, grad_out,
    inv_out, decay_out, ub_out, ws_out, pdo_out, kk_out, qk_out, maps, affs, w_buf,
):
    keys = q_raw.shape[1] // CH
    heads = v_raw.shape[1] // CH
    rep = heads // keys
    blocks = q_raw.shape[0] // CH
    mask = [masks[d] for d in range(TAPS - 1)]
    tail = 2 * HALO

    def fetched(raw, got, h):
        parts = [jnp.where(swaps[n] > 0, got[j, :, tile(h)], raw[n * CH : (n + 1) * CH, tile(h)]) for n in range(blocks)]
        return jnp.concatenate(parts, axis=0)

    def activate(raw, got, halo, taps, h):
        own = raw[SWAP - tail : SWAP, tile(h)]
        before = jnp.where(swaps[0] > 0, own, halo[j, :, tile(h)]).astype(f32)[HALO:]
        x = conv(fetched(raw, got, h).astype(f32), before, taps[:, tile(h)], mask)
        sig = sigmoid(x)
        u = x * sig
        return u, sig + u * (1.0 - sig)

    def unit(raw, got, halo, taps, h, scale, out, scale_out):
        u, slope = activate(raw, got, halo, taps, h)
        factor = scale / jnp.sqrt(rowsum(u * u) + GUARD)
        y = u * factor
        out[j, :, tile(h)] = y
        scale_out[j, :, tile(h)] = slope * factor
        return y

    kn = [unit(k_raw, k_got, k_halo, k_taps, h, 1.0, kn_out, k_scale) for h in range(keys)]
    qn = [unit(q_raw, q_got, q_halo, q_taps, h, SCALE, qn_out, q_scale) for h in range(keys)]
    row, col = iota(0), iota(1)
    eye = (row == col).astype(f32)
    units = []
    for n in range(blocks):
        flat = rows[j, n]
        cols = columns(flat)
        for h in range(keys):
            q, k = qn[h][n * CH : (n + 1) * CH], kn[h][n * CH : (n + 1) * CH]
            both = mm_nt(jnp.concatenate([k, q], axis=0), k)
            kk, qk = both[:CH], both[CH:]
            kk_out[j, n * keys + h] = kk
            qk_out[j, n * keys + h] = qk
            q_t, k_t = q.T, k.T
            for e in range(h * rep, (h + 1) * rep):
                (beta, c, s, w, bs), (beta_r, c_r, s_r, w_r, bs_r) = head_scalars(cols, flat, e, heads)
                decay = jnp.exp(jnp.minimum(c - c_r, 0.0)) * docs[n]
                decay_out[j, n * heads + e] = decay
                low = jnp.where(row > col, beta * decay * kk, 0.0)
                units.append((n, e, low, decay * qk, beta, bs * k, k_t * w_r, s_r * q_t, s_r[:, CH - 1 :]))
    values, by_do = {}, {}

    def value(e):
        u, slope = activate(v_raw, v_got, v_halo, v_taps, e)
        v_out[j, :, tile(e)] = u
        v_scale[j, :, tile(e)] = slope
        values[e] = u

    def output(u):
        n, e, p, sq_t = u[0], u[1], u[3], u[7]
        do = jnp.where(swaps[n] > 0, g_got[j, :, tile(e)], g_raw[n * CH : (n + 1) * CH, tile(e)])
        grad_out[j, n * CH : (n + 1) * CH, tile(e)] = do
        by_do[n, e] = mm_half(jnp.concatenate([p.T, sq_t], axis=0), do)
        pdo_out[j, n * heads + e] = by_do[n, e][:CH]

    fillers = [functools.partial(output, u) for u in units] + [functools.partial(value, e) for e in range(heads)]
    inv = inverse_blocks([u[2] for u in units], BASE, fillers)
    size = BASE.bit_length() - 1
    while (1 << size) < CH:
        near = ((row >> (size + 1)) == (col >> (size + 1))) & ((row >> size) != (col >> size))
        width = 1 << size
        half = [mm(odd_blocks(jnp.where(near, u[2], 0.0), width), t) for u, t in zip(units, inv)]
        odds = [odd_blocks(t, width) for t in inv]
        odds = [t - mm(t, with_odd(None, h, width)) for t, h in zip(odds, half)]
        inv = [with_odd(t, o, width) for t, o in zip(inv, odds)]
        size += 1
    solved = []
    for (n, e, low, p, beta, bsk, kw_t, sq_t, s_last), t in zip(units, inv):
        inv_out[j, n * heads + e] = t
        ub = mm(t, beta * values[e][n * CH : (n + 1) * CH])
        ws = mm(t, bsk)
        ub_out[j, n * heads + e] = ub
        ws_out[j, n * heads + e] = ws
        solved.append((ub, ws))
    result = {}
    for (n, e, low, p, beta, bsk, kw_t, sq_t, s_last), (ub, ws) in zip(units, solved):
        a = mm(kw_t, ub)
        m = s_last * eye - mm(kw_t, ws)
        g = by_do[n, e][CH:] - mm(ws.T, by_do[n, e][:CH])
        result[n, e] = (m, m.T, a, g)
    for e in range(heads):
        m0, m0_t, a0, g0 = result[0, e]
        m1, m1_t, a1, g1 = result[1, e]
        for i, x in enumerate((m0, m1, m1_t, m0_t)):
            maps[j, e, i] = x
        for i, x in enumerate((a0, a1, g1, g0)):
            affs[j, e, i] = x
        w_buf[j, e] = jnp.where(first, a1, g0) + mm(jnp.where(first, m1, m0_t), jnp.where(first, a0, g1))


def spill_rows(da, taps, mask):
    zeros = jnp.zeros_like(da)
    total = zeros
    for d in range(1, TAPS):
        ext = jnp.concatenate([da * mask[d - 1][:HALO], zeros], axis=0)
        total = total + taps[TAPS - 1 - d : TAPS - d, :] * pltpu.roll(ext, 2 * HALO - d, 0)[HALO:]
    return total


def backward_phase(
    send, j, first, other, q_taps, k_taps, v_taps, masks, rows,
    q_scale, k_scale, v_scale, v_all, qn, kn, seq_grad, inv, decays, ub_in, ws_in, pdo_in, kk_in, qk_in,
    maps, affs, y_buf, s_buf, z_got, out, q_body, k_body, v_body, q_tail, k_tail, v_tail, spill, row_grads,
):
    tokens = qn.shape[1]
    blocks = tokens // CH
    keys = qn.shape[2] // CH
    heads = v_all.shape[2] // CH
    rep = heads // keys
    row, col = iota(0), iota(1)
    states, leaving = [], []
    for e in range(heads):
        y, s1, z = y_buf[j, e], s_buf[j, e], z_got[j, e]
        t1 = affs[j, e, other] + mm(maps[j, e, other], z)
        states.append((jnp.where(first, y, z), jnp.where(first, s1, t1)))
        leaving.append((jnp.where(first, t1, s1), jnp.where(first, z, y)))
    info = []
    for n in range(blocks):
        flat = rows[j, n]
        info.append((flat, columns(flat)))
    order = [(n, e) for n in range(blocks) for e in range(heads)]
    work = {}

    def at(ref, n, h):
        return ref[j, n * CH : (n + 1) * CH, tile(h)]

    for n, e in order:
        flat, cols = info[n]
        (beta, c, s, w, bs), rs = head_scalars(cols, flat, e, heads)
        i = n * heads + e
        q, k = at(qn, n, e // rep), at(kn, n, e // rep)
        st, ds_out = states[e][n], leaving[e][n]
        by_st = mm(jnp.concatenate([ws_in[j, i], q], axis=0), st)
        u = ub_in[j, i] - by_st[:CH]
        du = pdo_in[j, i] + mm(k * w, ds_out)
        work[n, e] = (by_st[CH:], u, du)
    for n, e in order:
        flat, cols = info[n]
        (beta, c, s, w, bs), rs = head_scalars(cols, flat, e, heads)
        i = n * heads + e
        qs, u, du = work[n, e]
        o = s * qs + mm(decays[j, i] * qk_in[j, n * keys + e // rep], u)
        out[n * CH : (n + 1) * CH, tile(e)] = o.astype(bf16)
        work[n, e] = (qs, u, mm(inv[j, i].T, du))
    dqs, dks, dvs = {}, {}, {}
    none = jnp.zeros((CH, CH), bf16)
    mask = [masks[d] for d in range(TAPS - 1)]

    def slope(n, h, grads, y_ref, scale_ref, gain):
        da = grads[n, h]
        if y_ref is not None:
            y = at(y_ref, n, h)
            da = da - y * (rowsum(y * da) * float(gain))
        return da * at(scale_ref, n, h)

    kinds = (
        (dqs, keys, q_taps, q_body, q_tail, qn, q_scale, DK),
        (dks, keys, k_taps, k_body, k_tail, kn, k_scale, 1),
        (dvs, heads, v_taps, v_body, v_tail, None, v_scale, 1),
    )
    slopes = {}
    for n in range(blocks):
        flat, cols = info[n]
        packed = jnp.zeros((CH, CH), f32)
        minus = []
        for h in range(keys):
            q, k = at(qn, n, h), at(kn, n, h)
            kk, qk = kk_in[j, n * keys + h], qk_in[j, n * keys + h]
            dqk_sum = dkk_sum = dq = dk = 0.0
            for e in range(h * rep, (h + 1) * rep):
                (beta, c, s, w, bs), rs = head_scalars(cols, flat, e, heads)
                s_last = rs[2][:, CH - 1 :]
                i = n * heads + e
                qs, u, y = work[n, e]
                st, ds_out = states[e][n], leaving[e][n]
                do_half = at(seq_grad, n, e)
                do = do_half.astype(f32)
                y_high, y_low = split(y)
                do_y = jnp.concatenate(
                    [jnp.concatenate([do_half, y_high], axis=0), jnp.concatenate([none, y_low], axis=0)], axis=1
                )
                by_u = mm_nt_split(do_y, u)
                by_s = mm_nt_split(do_y, st)
                dos, zneg = by_s[:CH], by_s[CH:]
                dkw = mm_nt(u, ds_out)
                decay = decays[j, i]
                dpd = by_u[:CH] * decay
                dls = by_u[CH:] * jnp.where(row > col, decay, 0.0)
                dlb = dls * kk
                f = dpd * qk - beta * dlb
                zk = zneg * k
                wk = w * (dkw * k)
                dbeta = rowsum(y * at(v_all, n, e) - s * zk - dlb)
                extra = jnp.sum(rowsum(wk + s_last * (ds_out * st)), axis=0, keepdims=True)
                dc = rowsum(f + s * (do * qs) - bs * zk - wk)
                dc = dc + jnp.where(row[:, :1] == CH - 1, extra, 0.0)
                packed = jnp.where(col == e, dbeta, packed)
                packed = jnp.where(col == heads + e, dc, packed)
                minus.append(jnp.sum(f, axis=0, keepdims=True))
                dqk_sum = dqk_sum + dpd
                dkk_sum = dkk_sum + beta * dls
                dq = dq + s * dos
                dk = dk + w * dkw - bs * zneg
                dvs[n, e] = beta * y
            by_k = mm(jnp.concatenate([dqk_sum, dkk_sum + dkk_sum.T], axis=0), k)
            dqs[n, h] = dq + by_k[:CH]
            dks[n, h] = dk + mm(dqk_sum.T, q) - by_k[CH:]
        row_grads[j, n] = packed.T[: 2 * heads] - jnp.concatenate([jnp.zeros((heads, CH), f32)] + minus, axis=0)
        at_col = 0
        for kind, (grads, count, taps, body_out, tail_out, y_ref, scale_ref, gain) in enumerate(kinds):
            for h in range(count):
                slopes[kind, n, h] = slope(n, h, grads, y_ref, scale_ref, gain)
                if n == 0:
                    spill[j, :, at_col : at_col + CH] = spill_rows(slopes[kind, n, h][:HALO], taps[:, tile(h)], mask)
                at_col += CH
        if n == 0:
            send()
    for kind, (grads, count, taps, body_out, tail_out, y_ref, scale_ref, gain) in enumerate(kinds):
        for h in range(count):
            da = jnp.concatenate([slopes[kind, n, h] for n in range(blocks)], axis=0)
            full = conv_back(da, taps[:, tile(h)], mask)
            body_out[j, :, tile(h)] = full[:tokens].astype(bf16)
            tail_out[j, :, tile(h)] = full[tokens - 2 * HALO : tokens]


def fused_kernel(ctxs, steps, *refs):
    swap_ref, a_log, dt_bias, beta_logit, gate_logit, doc_ids = refs[:6]
    taps, sources, refs = refs[6:9], refs[9:16], refs[16:]
    results, refs = refs[:6], refs[6:]
    raws, tap_rows, out, refs = refs[:4], refs[4:7], refs[7], refs[8:]
    gots, halos, (beta_got, gate_got, ids_got), refs = refs[:4], refs[4:7], refs[7:10], refs[10:]
    (masks, docs, rows, betas, factors), refs = refs[:5], refs[5:]
    saved, refs = refs[:14], refs[14:]
    (maps, affs, w_buf, w_got, x_buf, y_buf, s_buf, z_buf, z_got), refs = refs[:9], refs[9:]
    bodies, tails, (spill, spill_got, row_grads), refs = refs[:3], refs[3:6], refs[6:9], refs[9:]
    (beta_grad, gate_grad, load_s, store_s, last_s, few_out), refs = refs[:6], refs[6:]
    swap_s, swap_r, hop_s, hop_r, pair_s, pair_r, spill_s, spill_r, got_s, got_r, halo_s, halo_r, few_s, few_r = refs
    heads = w_buf.shape[1]
    tokens = raws[0].shape[1]
    core = lax.axis_index("pair")
    ctx = lax.axis_index("ctx")
    first = core == 0
    mine, other = 2 * core, 2 - 2 * core
    peer_ctx = jnp.where(first, ctx - 1, ctx + 1)
    has_peer = (peer_ctx >= 0) & (peer_ctx < ctxs)
    has_prev = jnp.logical_not(first) | has_peer
    has_next = first | has_peer
    partner = {"pair": 1 - core}
    peer = {"ctx": jnp.clip(peer_ctx, 0, ctxs - 1), "pair": 1 - core}
    following = {"ctx": jnp.clip(ctx + core, 0, ctxs - 1), "pair": 1 - core}
    previous = {"ctx": jnp.clip(ctx - 1 + core, 0, ctxs - 1), "pair": 1 - core}
    swap_flag = swap_ref[0]
    swaps = [jnp.where(first, 0, swap_flag), jnp.where(first, swap_flag, 0)]

    def remote(src, dst, send, recv, device):
        return pltpu.make_async_remote_copy(src, dst, send, recv, device_id=device, device_id_type=pl.DeviceIdType.MESH)

    def swap(j):
        return remote(w_buf.at[j], w_got.at[j], swap_s.at[j], swap_r.at[j], partner)

    def hop(j):
        return remote(x_buf.at[j], y_buf.at[j], hop_s.at[j], hop_r.at[j], peer)

    def pair(j):
        return remote(z_buf.at[j], z_got.at[j], pair_s.at[j], pair_r.at[j], partner)

    def spilled(j):
        return remote(spill.at[j], spill_got.at[j], spill_s.at[j], spill_r.at[j], previous)

    start = pl.multiple_of(jnp.where(first, SWAP, 0), SWAP)

    def exchanged(i, j):
        width = gots[i].shape[2]
        at = pl.multiple_of(j * width, CH)
        return remote(
            sources[i].at[pl.ds(start, SWAP), pl.ds(at, width)], gots[i].at[j], got_s.at[i, j], got_r.at[i, j], partner
        )

    def neighbour(i, j):
        width = halos[i].shape[2]
        at = pl.multiple_of(j * width, CH)
        return remote(
            sources[i].at[pl.ds(tokens - 2 * HALO, 2 * HALO), pl.ds(at, width)], halos[i].at[j], halo_s.at[i, j],
            halo_r.at[i, j], following,
        )

    def loaded(i, j):
        width = raws[i].shape[2]
        at = pl.multiple_of(j * width, CH)
        return pltpu.make_async_copy(sources[i].at[:, pl.ds(at, width)], raws[i].at[j], load_s.at[i, j])

    def stored(i, j, first_row, count, sems):
        held = (out, *bodies)[i]
        width = held.shape[2]
        at = pl.multiple_of(j * width, CH)
        lines = pl.ds(first_row, count)
        return pltpu.make_async_copy(held.at[j, lines], results[i].at[lines, pl.ds(at, width)], sems.at[i, j])

    edge = tokens - 2 * HALO

    def stored_body(i, j):
        return stored(i, j, 0, tokens if i == 0 else edge, store_s)

    def stored_edge(i, j):
        return stored(i, j, edge, 2 * HALO, last_s)

    def stored_few(i):
        return pltpu.make_async_copy((beta_grad, gate_grad)[i], results[4 + i], few_out.at[i])

    def logits(i):
        return remote(sources[4 + i].at[:, pl.ds(start, SWAP)], (beta_got, gate_got)[i], few_s.at[i], few_r.at[i], partner)

    ids_copy = remote(sources[6], ids_got, few_s.at[2], few_r.at[2], following)

    def fetch_rows(j):
        for i in range(4):
            exchanged(i, j).start()

        @pl.when(has_next)
        def _():
            for i in range(3):
                neighbour(i, j).start()

    def advance(j, at, got):
        mid = [affs[j, e, at] + mm(maps[j, e, at], got[j, e]) for e in range(heads)]
        return mid, [affs[j, e, at + 1] + mm(maps[j, e, at + 1], mid[e]) for e in range(heads)]

    def chains(step, over, back):
        if over:
            swap(step - 1).wait_recv()
            mid, end = advance(step - 1, other, w_got)
            for e in range(heads):
                x_buf[step - 1, e] = end[e]

            @pl.when(has_peer)
            def _():
                hop(step - 1).start()

        if back:
            @pl.when(has_peer)
            def _():
                hop(step - 2).wait_recv()

            @pl.when(jnp.logical_not(has_peer))
            def _():
                y_buf[step - 2] = jnp.zeros(y_buf.shape[1:], f32)

            mid, end = advance(step - 2, mine, y_buf)
            for e in range(heads):
                s_buf[step - 2, e] = mid[e]
                z_buf[step - 2, e] = end[e]
            pair(step - 2).start()

    for i in range(4):
        loaded(i, 0).start()
    barrier = pltpu.get_barrier_semaphore()
    pl.semaphore_signal(barrier, inc=1, device_id=partner, device_id_type=pl.DeviceIdType.MESH)

    @pl.when(has_peer)
    def _():
        pl.semaphore_signal(barrier, inc=1, device_id=peer, device_id_type=pl.DeviceIdType.MESH)

    pl.semaphore_wait(barrier, jnp.where(has_peer, 2, 1))

    @pl.when(has_next)
    def _():
        ids_copy.start()

    for i in range(2):
        logits(i).start()
    fetch_rows(0)

    for j in range(1, steps):
        for i in range(4):
            loaded(i, j).start()
    for i in range(3):
        width = tap_rows[i].shape[2]
        for j in range(steps):
            tap_rows[i][j] = taps[i][:, j * width : (j + 1) * width].astype(f32)

    @pl.when(has_prev)
    def _():
        ids_copy.wait_recv()

    @pl.when(jnp.logical_not(has_prev))
    def _():
        ids_got[...] = jnp.zeros(ids_got.shape, jnp.int32)
        for halo in halos:
            halo[...] = jnp.zeros(halo.shape, bf16)

    for i in range(2):
        logits(i).wait_recv()
    setup_phase(
        has_prev, swaps, a_log, dt_bias, beta_logit, gate_logit, doc_ids, beta_got, gate_got, ids_got,
        masks, docs, rows, betas, factors,
    )

    def ahead(step, carry):
        for i in range(4):
            loaded(i, step).wait()
            exchanged(i, step).wait_recv()

        @pl.when(has_prev)
        def _():
            for i in range(3):
                neighbour(i, step).wait_recv()

        @pl.when(step < steps - 1)
        def _():
            fetch_rows(step + 1)

        forward_phase(
            step, first, swaps, *[x.at[step] for x in raws], *[x.at[step] for x in tap_rows], *gots, *halos, masks, docs,
            rows, *saved, maps, affs, w_buf,
        )
        swap(step).start()

        @pl.when(step == 1)
        def _():
            chains(step, True, False)

        @pl.when(step >= 2)
        def _():
            chains(step, True, True)

        return carry

    def emit(j):
        @pl.when(has_next)
        def _():
            spilled(j).wait_recv()

        @pl.when(jnp.logical_not(has_next))
        def _():
            spill_got[j] = jnp.zeros(spill_got.shape[1:], f32)

        at = 0
        for i, (held, tail) in enumerate(zip(bodies, tails)):
            width = held.shape[2]
            last = tail[j]
            last = jnp.concatenate([last[:HALO], last[HALO:] + spill_got[j, :, at : at + width]], axis=0)
            held[j, tokens - 2 * HALO :] = last.astype(bf16)
            stored_edge(i + 1, j).start()
            at += width

    def back(j, carry):
        pair(j).wait_recv()
        def send():
            @pl.when(has_prev)
            def _():
                spilled(j).start()

        backward_phase(
            send, j, first, other, *[x.at[j] for x in tap_rows], masks, rows, *saved, maps, affs, y_buf, s_buf, z_got, out.at[j],
            *bodies, *tails, spill, row_grads,
        )
        for i in range(4):
            stored_body(i, j).start()

        @pl.when(j == 0)
        def _():
            chains(steps, True, True)

        @pl.when(j == 1)
        def _():
            chains(steps + 1, False, True)

        @pl.when(j >= 1)
        def _():
            emit(j - 1)

        return carry

    lax.fori_loop(0, steps, ahead, 0)
    lax.fori_loop(0, steps, back, 0)
    blocks = tokens // CH
    weights = (iota(0) >= iota(1)).astype(bf16)
    for n in range(blocks):
        dbeta = jnp.concatenate([row_grads[j, n, :heads] for j in range(steps)], axis=0)
        dc = jnp.concatenate([row_grads[j, n, heads:] for j in range(steps)], axis=0)
        beta = betas[n]
        beta_grad[:, tile(n)] = (dbeta * beta * (1.0 - beta)).astype(bf16)
        gate_grad[:, tile(n)] = (summed(dc, weights) * factors[n]).astype(bf16)
    for i in range(2):
        stored_few(i).start()
    emit(steps - 1)
    for i in range(2):
        stored_few(i).wait()
    for i in range(2):
        logits(i).wait_send()

    @pl.when(has_next)
    def _():
        ids_copy.wait_send()

    for j in range(steps):
        swap(j).wait_send()
        pair(j).wait_send()
        for i in range(4):
            stored_body(i, j).wait()
            if i > 0:
                stored_edge(i, j).wait()
            exchanged(i, j).wait_send()

        @pl.when(has_peer)
        def _():
            hop(j).wait_send()

        @pl.when(has_next)
        def _():
            for i in range(3):
                neighbour(i, j).wait_send()

        @pl.when(has_prev)
        def _():
            spilled(j).wait_send()


def join_kernel(m, a, g, a_in, g_in, a_out, g_out):
    for e in range(m.shape[0]):
        here = m[e]
        a_out[e] = a[e] + mm(here, a_in[e])
        g_out[e] = g[e] + mm(here.T, g_in[e])


def norm_back(dy, a, scale):
    sig = sigmoid(a)
    u = a * sig
    inverse = 1.0 / jnp.sqrt(rowsum(u * u) + GUARD)
    y = u * inverse
    dy = dy * scale
    du = (dy - y * rowsum(y * dy)) * inverse
    return du * (sig + u * (1.0 - sig))


def main_kernel(
    a_q, a_k, a_v, qn, kn, seq_grad, inv, kk_in, qk_in, pdo_in, q_taps, k_taps, v_taps, masks, docs, rows,
    s_in, d_in, out, q_grad, k_grad, v_grad, q_end, k_end, v_end, q_spill, k_spill, v_spill, row_grads,
):
    tokens = a_q.shape[0]
    blocks = tokens // CH
    heads = a_v.shape[1] // CH
    row, col = iota(0), iota(1)
    va = a_v[...]
    v_sig = sigmoid(va)
    v_all = va * v_sig
    info = []
    for n in range(blocks):
        q = qn[n * CH : (n + 1) * CH, :]
        k = kn[n * CH : (n + 1) * CH, :]
        info.append((q, k, q.T, k.T, rows[0, n], columns(rows[0, n])))
    fwd = {}
    carried = [s_in[e] for e in range(heads)]
    for n in range(blocks):
        q, k, q_t, k_t, flat, cols = info[n]
        kq = jnp.concatenate([k, q], axis=0)
        for e in range(heads):
            beta, c, s, w = [cols[:, 4 * e + i : 4 * e + i + 1] for i in range(4)]
            beta_r, c_r, s_r, w_r = [flat[4 * e + i : 4 * e + i + 1, :] for i in range(4)]
            s_last = s_r[:, CH - 1 :]
            v = v_all[n * CH : (n + 1) * CH, e * CH : (e + 1) * CH]
            decay = jnp.exp(jnp.minimum(c - c_r, 0.0)) * docs[n]
            p = decay * qk_in[0, n]
            st = carried[e]
            kqs = mm(kq, st)
            ks, qs = kqs[:CH], kqs[CH:]
            t = inv[0, e, n]
            u = mm(t, beta * (v - s * ks))
            o = s * qs + mm(p, u)
            out[n * CH : (n + 1) * CH, e * CH : (e + 1) * CH] = o.astype(bf16)
            if n + 1 < blocks:
                carried[e] = s_last * st + mm(k_t * w_r, u)
            fwd[n, e] = (st, u, qs, decay, p, v)
    grads = [d_in[e] for e in range(heads)]
    dqs, dks, dvs = [None] * blocks, [None] * blocks, {}
    for n in reversed(range(blocks)):
        q, k, q_t, k_t, flat, cols = info[n]
        packed = jnp.zeros((CH, CH), f32)
        dqk_sum = dkk_sum = dq = dk = 0.0
        for e in range(heads):
            beta, c, s, w = [cols[:, 4 * e + i : 4 * e + i + 1] for i in range(4)]
            beta_r, c_r, s_r, w_r = [flat[4 * e + i : 4 * e + i + 1, :] for i in range(4)]
            s_last = s_r[:, CH - 1 :]
            st, u, qs, decay, p, v = fwd[n, e]
            ds_out = grads[e]
            do_half = seq_grad[n * CH : (n + 1) * CH, e * CH : (e + 1) * CH]
            do = do_half.astype(f32)
            du = pdo_in[0, e, n] + mm(k * w, ds_out)
            y = mm(inv[0, e, n].T, du)
            do_y = jnp.concatenate([do, y], axis=0)
            by_u = mm_nt(do_y, u)
            by_s = mm_nt(do_y, st)
            dp, dl = by_u[:CH], -by_u[CH:]
            dos, z = by_s[:CH], -by_s[CH:]
            dkw = mm_nt(u, ds_out)
            strict = jnp.where(row > col, decay, 0.0)
            bk = strict * kk_in[0, n]
            dlb = dl * bk
            f = dp * p + beta * dlb
            zk = z * k
            wk = w * (dkw * k)
            bs = beta * s
            dbeta = rowsum(y * v + s * zk + dlb)
            extra = jnp.sum(rowsum(wk + s_last * (ds_out * st)), axis=0, keepdims=True)
            dc = rowsum((f - f.T) + s * (do * qs) + bs * zk - wk)
            dc = dc + jnp.where(row[:, :1] == CH - 1, extra, 0.0)
            packed = jnp.where(col == 2 * e, dbeta, packed)
            packed = jnp.where(col == 2 * e + 1, dc, packed)
            dqk_sum = dqk_sum + dp * decay
            dkk_sum = dkk_sum + dl * (beta * strict)
            dq = dq + s * dos
            dk = dk + w * dkw + bs * z
            dvs[n, e] = beta * y
            if n > 0:
                grads[e] = mm_half(q_t * s_r, do_half) + s_last * ds_out - mm(k_t * (beta_r * s_r), y)
        dqs[n] = dq + mm(dqk_sum, k)
        dks[n] = dk + mm(dqk_sum.T, q) + mm(dkk_sum + dkk_sum.T, k)
        row_grads[0, n] = packed.T[: row_grads.shape[2]]
    dq = jnp.concatenate(dqs, axis=0)
    dk = jnp.concatenate(dks, axis=0)
    dv = jnp.concatenate(
        [jnp.concatenate([dvs[n, e] for e in range(heads)], axis=1) for n in range(blocks)], axis=0
    )
    daq = norm_back(dq, a_q[...], SCALE)
    dak = norm_back(dk, a_k[...], 1.0)
    dav = dv * (v_sig + v_all * (1.0 - v_sig))
    for da, taps, grad, end, spill in (
        (daq, q_taps, q_grad, q_end, q_spill),
        (dak, k_taps, k_grad, k_end, k_spill),
        (dav, v_taps, v_grad, v_end, v_spill),
    ):
        full = conv_back(da, taps, masks)
        grad[...] = full[:tokens].astype(bf16)
        end[...] = full[tokens - HALO : tokens]
        spill[...] = full[tokens:]


def shifted(array, by):
    peers = lax.axis_size(SEQ)
    return lax.ppermute(array, SEQ, [(i, i + by) for i in range(peers) if 0 <= i + by < peers])


def tri(upper):
    i = jnp.arange(CH)
    return ((i[:, None] <= i[None, :]) if upper else (i[:, None] >= i[None, :])).astype(f32)


def sds(shape, dtype=f32):
    return jax.ShapeDtypeStruct(shape, dtype)


def staged_call(inputs, hk, hv, tokens, hops):
    blocks = tokens // CH
    rep = hv // hk
    qw = hk * DK
    vw = rep * DK
    col = lambda rows_, width, off=0: pl.BlockSpec((rows_, width), lambda i, off=off, width=width: (0, off // width + i))
    fixed = lambda shape: pl.BlockSpec(shape, lambda i: (0,) * len(shape))
    per = lambda shape: pl.BlockSpec(shape, lambda i: (i,) + (0,) * (len(shape) - 1))
    taps_specs = [col(TAPS, DK), col(TAPS, DK), col(TAPS, vw)]
    common_specs = taps_specs + [
        fixed((TAPS - 1, tokens, CH)),
        fixed((blocks, CH, CH)),
        per((1, blocks, rep * 4, CH)),
    ]
    params = pltpu.CompilerParams(dimension_semantics=("arbitrary",), vmem_limit_bytes=48 * 2**20)
    saved_specs = [
        col(tokens, DK), col(tokens, DK), col(tokens, vw), col(tokens, DK), col(tokens, DK), col(tokens, vw),
        per((1, rep, blocks, CH, CH)), per((1, blocks, CH, CH)), per((1, blocks, CH, CH)),
        per((1, rep, blocks, CH, CH)),
    ]
    saved_shapes = [
        sds((tokens, qw)), sds((tokens, qw)), sds((tokens, hv * DK)), sds((tokens, qw)), sds((tokens, qw)),
        sds((tokens, hv * DK), bf16), sds((hk, rep, blocks, CH, CH)), sds((hk, blocks, CH, CH)),
        sds((hk, blocks, CH, CH)), sds((hk, rep, blocks, CH, CH)),
    ]
    state_spec = per((rep, DK, DK))
    state_shape = sds((hv, DK, DK))
    units = hv * blocks * 2 * 4 * CH**3
    *taps, masks, docs, rows = inputs[12:]
    in_specs = [
        pl.BlockSpec(memory_space=pltpu.SMEM),
        col(tokens, DK), col(tokens, DK), col(tokens, vw), col(tokens, vw),
        col(SWAP, DK), col(SWAP, DK, qw), col(SWAP, vw, 2 * qw), col(SWAP, vw, 2 * qw + hv * DK),
        col(HALO, DK), col(HALO, DK, qw), col(HALO, vw, 2 * qw),
    ] + common_specs
    prepare_cost = pl.CostEstimate(flops=22 * units, bytes_accessed=24 * 2**20, transcendentals=2**20)
    prepared = pl.pallas_call(
        prepare_kernel,
        grid=(hk,),
        in_specs=in_specs,
        out_specs=saved_specs + [state_spec] * 3,
        out_shape=saved_shapes + [state_shape] * 3,
        compiler_params=params,
        cost_estimate=prepare_cost,
        name="prepare",
    )(*inputs)
    saved, (m, a, g) = prepared[:10], prepared[10:]
    join = pl.pallas_call(
        join_kernel,
        grid=(hk,),
        in_specs=[state_spec] * 5,
        out_specs=[state_spec] * 2,
        out_shape=[state_shape] * 2,
        compiler_params=params,
        cost_estimate=pl.CostEstimate(flops=hv * 16 * CH**3, bytes_accessed=7 * 2**20, transcendentals=0),
        name="join",
    )
    s_in, d_in = a, g
    for step in range(hops):
        s_in, d_in = shifted(s_in, 1), shifted(d_in, -1)
        if step < hops - 1:
            s_in, d_in = join(m, a, g, s_in, d_in)

    ends = [col(HALO, DK), col(HALO, DK), col(HALO, vw)]
    end_shapes = [sds((HALO, qw)), sds((HALO, qw)), sds((HALO, hv * DK))]
    return pl.pallas_call(
        main_kernel,
        grid=(hk,),
        in_specs=saved_specs + common_specs + [state_spec] * 2,
        out_specs=[col(tokens, vw), col(tokens, DK), col(tokens, DK), col(tokens, vw)] + ends + ends + [per((1, blocks, 8, CH))],
        out_shape=[
            sds((tokens, hv * DK), bf16), sds((tokens, qw), bf16), sds((tokens, qw), bf16), sds((tokens, hv * DK), bf16)
        ] + end_shapes + end_shapes + [sds((hk, blocks, 8, CH))],
        compiler_params=params,
        cost_estimate=pl.CostEstimate(flops=17 * units, bytes_accessed=24 * 2**20, transcendentals=2**20),
        name="main",
    )(*saved, *taps, masks, docs, rows, s_in, d_in)


def copy_kernel(*refs):
    count = (len(refs) - 2) // 3
    held = refs[2 * count : 3 * count]
    in_sems, out_sems = refs[3 * count :]
    pieces = []
    for src, dst, mid in zip(refs[:count], refs[count : 2 * count], held):
        size = max(16, min(src.shape[0], COPY_BYTES // (2 * src.shape[1])))
        for at in range(0, src.shape[0], size):
            rows, i = pl.ds(at, size), len(pieces)
            pieces.append((
                pltpu.make_async_copy(src.at[rows], mid.at[rows], in_sems.at[i]),
                pltpu.make_async_copy(mid.at[rows], dst.at[rows], out_sems.at[i]),
            ))
    for load, store in pieces:
        load.start()
    for load, store in pieces:
        load.wait()
        store.start()
    for load, store in pieces:
        store.wait()


def copied(arrays):
    hbm = pl.BlockSpec(memory_space=pl.ANY)
    return pl.pallas_call(
        copy_kernel,
        in_specs=[hbm] * len(arrays),
        out_specs=[hbm] * len(arrays),
        out_shape=[sds(x.shape, x.dtype) for x in arrays],
        scratch_shapes=[pltpu.VMEM(x.shape, x.dtype) for x in arrays] + [pltpu.SemaphoreType.DMA((64,))] * 2,
        name="copies",
    )(*arrays)


def fused_call(
    q_raw, k_raw, v_raw, beta_logit, gate_logit, out_grad, conv_q, conv_k, conv_v, a_log, dt_bias, doc_ids, swap_blocks
):
    tokens, qw = q_raw.shape
    blocks = tokens // CH
    hk = qw // DK
    hv = v_raw.shape[1] // DK
    steps = hk // GROUP
    heads = hv // steps
    gw, vw = GROUP * DK, heads * DK
    doc_ids = doc_ids.reshape(blocks, CH)
    fixed = lambda shape: pl.BlockSpec(memory_space=pltpu.VMEM)
    smem = pl.BlockSpec(memory_space=pltpu.SMEM)
    hbm = pl.BlockSpec(memory_space=pl.ANY)
    in_specs = [smem] * 3 + [fixed(x.shape) for x in (beta_logit, gate_logit, doc_ids, conv_q, conv_k, conv_v)] + [hbm] * 7
    vm = lambda *shape: pltpu.VMEM(shape, f32)
    half = lambda *shape: pltpu.VMEM(shape, bf16)
    square = lambda *lead: vm(steps, *lead, CH, CH)
    wide = lambda width: vm(steps, tokens, width)
    units = blocks * heads
    sems = lambda *shape: pltpu.SemaphoreType.DMA(shape)
    scratch = [half(steps, tokens, gw), half(steps, tokens, gw), half(steps, tokens, vw), half(steps, tokens, vw)]
    scratch += [vm(steps, TAPS, gw), vm(steps, TAPS, gw), vm(steps, TAPS, vw), half(steps, tokens, vw)]
    scratch += [half(steps, SWAP, gw), half(steps, SWAP, gw), half(steps, SWAP, vw), half(steps, SWAP, vw)]
    scratch += [half(steps, 2 * HALO, gw), half(steps, 2 * HALO, gw), half(steps, 2 * HALO, vw)]
    scratch += [half(hv, SWAP), half(hv, SWAP), pltpu.VMEM((blocks, CH), jnp.int32)]
    scratch += [vm(TAPS - 1, tokens, CH), vm(blocks, CH, CH), vm(steps, blocks, KINDS * heads, CH)]
    scratch += [vm(blocks, hv, CH), vm(blocks, hv, CH)]
    scratch += [wide(gw), wide(gw), wide(vw), wide(vw), wide(gw), wide(gw), half(steps, tokens, vw)]
    scratch += [square(units)] * 5 + [square(blocks * GROUP)] * 2 + [square(heads, 4)] * 2 + [square(heads)] * 7
    scratch += [half(steps, tokens, gw), half(steps, tokens, gw), half(steps, tokens, vw)]
    scratch += [vm(steps, 2 * HALO, gw), vm(steps, 2 * HALO, gw), vm(steps, 2 * HALO, vw)]
    scratch += [vm(steps, HALO, 2 * gw + vw)] * 2 + [vm(steps, blocks, 2 * heads, CH)]
    scratch += [half(hv, tokens), half(hv, tokens)] + [sems(4, steps)] * 3 + [sems(2)] + [sems(steps)] * 8 + [sems(4, steps)] * 2 + [sems(3, steps)] * 2 + [sems(3)] * 2
    return pl.pallas_call(
        functools.partial(fused_kernel, lax.axis_size("ctx"), steps),
        in_specs=in_specs,
        out_specs=[hbm] * 6,
        out_shape=[
            sds((tokens, hv * DK), bf16), sds((tokens, qw), bf16), sds((tokens, qw), bf16), sds((tokens, hv * DK), bf16),
            sds((hv, tokens), bf16), sds((hv, tokens), bf16),
        ],
        scratch_shapes=scratch,
        compiler_params=pltpu.CompilerParams(
            vmem_limit_bytes=56 * 2**20, collective_id=0, has_side_effects=True
        ),
        cost_estimate=pl.CostEstimate(
            flops=30 * hv * blocks * 8 * CH**3, bytes_accessed=8 * 2**20, transcendentals=2**21
        ),
        name="fused",
    )(
        swap_blocks, a_log, dt_bias, beta_logit, gate_logit, doc_ids, conv_q, conv_k, conv_v,
        q_raw, k_raw, v_raw, out_grad, beta_logit, gate_logit, doc_ids,
    )


def body(
    q_raw, k_raw, v_raw, beta_logit, gate_logit, out_grad, conv_q, conv_k, conv_v, a_log, dt_bias, doc_ids, swap_blocks
):
    tokens = q_raw.shape[0]
    blocks = tokens // CH
    hk = q_raw.shape[1] // DK
    hv = v_raw.shape[1] // DK
    rep = hv // hk
    shards = lax.axis_size(SEQ)
    hops = max(1, shards // DOC_PARTS)
    if hops == lax.axis_size("pair") and blocks == 2 and hk % GROUP == 0:
        return copied(
            fused_call(
                q_raw, k_raw, v_raw, beta_logit, gate_logit, out_grad, conv_q, conv_k, conv_v, a_log, dt_bias, doc_ids,
                swap_blocks,
            )
        )
    core = lax.axis_index("pair")
    swap = swap_blocks[0]
    flags = jnp.stack([jnp.where(core == 1, swap, 0), jnp.where(core == 0, swap, 0)]).astype(jnp.int32)

    start = jnp.where(core == 0, SWAP, 0)
    logits = jnp.concatenate([beta_logit, gate_logit], axis=0)
    bg_send = lax.dynamic_slice_in_dim(logits, start, SWAP, 1)
    send = jnp.concatenate(
        [lax.dynamic_slice_in_dim(x, start, SWAP, 0) for x in (q_raw, k_raw, v_raw, out_grad)], axis=1
    )
    got = lax.ppermute(send, "pair", [(0, 1), (1, 0)])
    send, bg_send, tail_ids, tails = lax.optimization_barrier(
        (send, bg_send, doc_ids[tokens - HALO :], [x[tokens - HALO :] for x in (q_raw, k_raw, v_raw)])
    )
    bg_got = lax.ppermute(bg_send, "pair", [(0, 1), (1, 0)])
    ids_col = jnp.broadcast_to((tail_ids + 1).astype(bf16)[:, None], (HALO, CH))
    tail = jnp.concatenate(tails + [ids_col], axis=1)
    before = shifted(tail, 1)
    own = jnp.concatenate([x[SWAP - HALO : SWAP] for x in (q_raw, k_raw, v_raw)], axis=1)
    chans = own.shape[1]
    halo = jnp.where(flags[0] > 0, own, before[:, :chans]).astype(f32)
    qw = hk * DK

    first = jnp.where(flags[0] > 0, bg_got, logits[:, :SWAP])
    second = jnp.where(flags[1] > 0, bg_got, logits[:, SWAP:])
    logits = jnp.concatenate([first, second], axis=1).astype(f32)
    beta = jax.nn.sigmoid(logits[:hv])
    gate = logits[hv:] + dt_bias[:, None]
    rate = -jnp.exp(a_log)[:, None]
    decay_log = rate * jax.nn.softplus(gate)
    c = jnp.dot(decay_log.reshape(hv * blocks, CH), tri(True), precision=highest).reshape(hv, blocks, CH)
    ids = doc_ids.astype(f32) + 1.0
    ext_ids = jnp.concatenate([before[:, chans].astype(f32), ids])
    doc = ids.reshape(blocks, CH)
    doc_before = ext_ids[HALO - 1 : HALO - 1 + tokens : CH]
    s = jnp.where(doc == doc_before[:, None], jnp.exp(c), 0.0)
    w = jnp.where(doc == doc[:, CH - 1 :], jnp.exp(jnp.minimum(c[:, :, CH - 1 :] - c, 0.0)), 0.0)
    rows = jnp.stack([beta.reshape(hv, blocks, CH), c, s, w], axis=2)
    rows = rows.reshape(hk, rep, blocks, 4, CH).transpose(0, 2, 1, 3, 4).reshape(hk, blocks, rep * 4, CH)
    docs = ((doc[:, :, None] == doc[:, None, :]) & (tri(False) > 0)[None]).astype(f32)
    masks = jnp.stack(
        [
            jnp.broadcast_to((ext_ids[HALO - d : HALO - d + tokens] == ids).astype(f32)[:, None], (tokens, CH))
            for d in range(1, TAPS)
        ]
    )
    taps = [x.astype(f32) for x in (conv_q, conv_k, conv_v)]

    results = staged_call(
        (flags, q_raw, k_raw, v_raw, out_grad, got, got, got, got, halo, halo, halo, *taps, masks, docs, rows), hk, hv,
        tokens, hops,
    )
    layer_out, q_grad, k_grad, v_grad = results[:4]
    spilled = shifted(jnp.concatenate(results[7:10], axis=1), -1)
    ends_out = []
    at = 0
    for grad, end in zip((q_grad, k_grad, v_grad), results[4:7]):
        width = end.shape[1]
        last = (end + spilled[:, at : at + width]).astype(bf16)
        ends_out.append(lax.dynamic_update_slice(grad, last, (tokens - HALO, 0)))
        at += width
    rg = results[10][:, :, : 2 * rep].reshape(hk, blocks, rep, 2, CH).transpose(3, 0, 2, 1, 4)
    dbeta = rg[0].reshape(hv, tokens)
    dg = jnp.dot(rg[1].reshape(hv * blocks, CH), tri(False), precision=highest).reshape(hv, tokens)
    beta_grad = dbeta * beta * (1.0 - beta)
    gate_grad = dg * rate * jax.nn.sigmoid(gate)
    return (layer_out, ends_out[0], ends_out[1], ends_out[2], beta_grad.astype(bf16), gate_grad.astype(bf16))


def solution(mesh):
    rows = P(("groups", "ctx", "pair"), "head")
    rates = P("head", ("groups", "ctx", "pair"))
    taps = P(None, "head")
    return jax.shard_map(
        body,
        mesh=mesh,
        in_specs=(
            rows, rows, rows, rates, rates, rows, taps, taps, taps, P("head"), P("head"),
            P(("groups", "ctx", "pair")), P(("groups", "ctx")),
        ),
        out_specs=(rows, rows, rows, rows, rates, rates),
        check_vma=False,
    )
```
